512 devices in a mesh: cls: 8 (over z_lo, core), ptcl: 64 (over y, z_hi, x).
Axes of the slice: x: 4, y: 4, z: 16 (z_hi: 4, z_lo: 4; z = z_hi * 4 + z_lo), core: 2. Of those that a mesh axis runs over, the one named last changes fastest.
Arguments:
- particles: bfloat16 [65536, 2048], P('ptcl')
- panels: bfloat16 [8, 128, 2048], P('cls', 'ptcl')
- sigma2: float32 [32], replicated, may hold values from 0.5 to 2
- defocus_bins: int32 [65536], P('ptcl'), may hold values from 0 to 15
- half_sets: int32 [65536], P('ptcl'), may hold values 0 or 1
- prior_mask: int32 [65536, 8], P('ptcl', 'cls'), may hold values from 0 to 1, as said below
- orient_ids: int32 [128], replicated, may hold values from 0 to 127, each once
Outputs:
- half_maps: float32 [8, 256, 2048], P('cls', 'ptcl')
- log_evidence: float32 [65536], P('ptcl')
The draws below stay inside these ranges and needn't reach their ends.
Inputs may be any that keep to these rules, and one draw needn't show every extreme that they name: `prior_mask`: every particle allows at least one class. `orient_ids`: each direction 0 to 127 appears once.
All inputs are finite; a program needn't handle non-finite values. No bound on the sum of `half_sets` on one device may be relied on, other than what follows from the above.
Results may differ from the reference program's by a relative error of at most 0.0015.
The reference program's roundings to bfloat16 on the way (of `weighted`, `power`, `panel_power`, `by_direction` and `centred`) count: a program that leaves them out, or rounds other values in their place, can miss the bound.
Values may be sent and summed in bfloat16 or wider, within the bound.
No kernel may reach another device: no remote copies, remote signals or barrier semaphores. Data moves between devices by JAX's collectives and lax.ppermute only.
A program may use at most 64 MiB of HBM per device.

```python
import math
import jax
import jax.numpy as jnp
from jax import lax

PIXC = 1024
ORIENT = 128
NSHELL = 32
NBIN = 16
PTCLS = 65536
CLASSES = 8


def ctf_values(bins):
    defocus = (bins.astype(jnp.float32) + 1.0) / NBIN
    radius = (jnp.arange(PIXC, dtype=jnp.float32) + 0.5) / PIXC
    phase = 0.3 + 2.5 * defocus[:, None] * radius[None, :]
    return jnp.sin(phase) + 0.1 * jnp.cos(phase)


def source_labels(key):
    classes = jax.random.randint(jax.random.fold_in(key, 101), (PTCLS,), 0, CLASSES)
    orients = jax.random.randint(jax.random.fold_in(key, 102), (PTCLS,), 0, ORIENT)
    bins = jax.random.randint(jax.random.fold_in(key, 103), (PTCLS,), 0, NBIN)
    return (classes, orients, bins)


def panel_values(key):
    shape = (CLASSES, ORIENT, 2 * PIXC)
    spread = 3.0 / PIXC ** 0.5
    values = spread * jax.random.normal(jax.random.fold_in(key, 201), shape, jnp.float32)
    near = values[:, 0] + 0.03 * spread * jax.random.normal(jax.random.fold_in(key, 202), (CLASSES, 2 * PIXC), jnp.float32)
    values = values.at[:, 1].set(near)
    return values


def draw_panels(key, part):
    return panel_values(key).astype(jnp.bfloat16)


def draw_defocus_bins(key, part):
    return source_labels(key)[2].astype(jnp.int32)


def draw_prior_mask(key, part):
    classes = source_labels(key)[0]
    coin = jax.random.randint(jax.random.fold_in(key, 301), (PTCLS, CLASSES), 0, 2)
    own = (classes[:, None] == jnp.arange(CLASSES)[None, :]).astype(jnp.int32)
    return jnp.maximum(coin, own).astype(jnp.int32)


def draw_particles(key, part):
    classes, orients, bins = source_labels(key)
    rows = jnp.arange(PTCLS)
    strong = rows % 97 == 0
    amplitude = jnp.where(strong, 16.0 + 8.0 * (rows // 97 % 3).astype(jnp.float32), 1.0)
    orients = jnp.where(strong, 0, orients)
    signal = panel_values(key)[classes, orients]
    contrast = ctf_values(bins)
    doubled = jnp.concatenate([contrast, contrast], axis=1)
    noise = jax.random.normal(jax.random.fold_in(key, 401), (PTCLS, 2 * PIXC), jnp.float32)
    return (amplitude[:, None] * doubled * signal + noise).astype(jnp.bfloat16)


def plant(result, own_key, least, high):
    index_at = [jax.random.randint(jax.random.fold_in(own_key, axis), (), 0, length) for axis, length in enumerate(result.shape)]
    widest = result.shape.index(max(result.shape))
    beside = index_at[:widest] + [(index_at[widest] + 1) % result.shape[widest]] + index_at[widest + 1:]
    return result.at[tuple(index_at)].set(least).at[tuple(beside)].set(high)


def setup_inputs(seed: int = 0) -> dict:
    key_list = jax.random.split(jax.random.key(seed), 8)
    return {
        "particles": draw_particles(jax.random.fold_in(key_list[7], 71), 0),
        "panels": draw_panels(jax.random.fold_in(key_list[7], 71), 0),
        "sigma2": jnp.clip(jnp.exp(jax.random.uniform(key_list[2], (NSHELL,), jnp.float32, math.log(0.5), math.log(2.0))), 0.5, 2.0),
        "defocus_bins": draw_defocus_bins(jax.random.fold_in(key_list[7], 71), 0),
        "half_sets": plant((jax.random.randint(key_list[4], (PTCLS,), 0, 2) < 1).astype(jnp.int32), jax.random.fold_in(key_list[4], 1), 0, 1),
        "prior_mask": draw_prior_mask(jax.random.fold_in(key_list[7], 71), 0),
        "orient_ids": jax.random.permutation(key_list[6], ORIENT).astype(jnp.int32),
    }


def ctf_table():
    bins = jnp.arange(NBIN, dtype=jnp.float32)
    defocus = (bins + 1.0) / NBIN
    radius = (jnp.arange(PIXC, dtype=jnp.float32) + 0.5) / PIXC
    phase = 0.3 + 2.5 * defocus[:, None] * radius[None, :]
    return jnp.sin(phase) + 0.1 * jnp.cos(phase)

def reference(particles, panels, sigma2, defocus_bins, half_sets, prior_mask, orient_ids):
    shells = jnp.arange(PIXC, dtype=jnp.int32) * NSHELL // PIXC
    inverse_noise = 1.0 / sigma2[shells]
    contrast = ctf_table()[defocus_bins]
    doubled = jnp.concatenate([contrast, contrast], axis=1)
    noise_pair = jnp.concatenate([inverse_noise, inverse_noise])
    images = particles.astype(jnp.float32)
    weighted = (images * doubled * noise_pair[None, :]).astype(jnp.bfloat16)
    power = (contrast * contrast * inverse_noise[None, :]).astype(jnp.bfloat16)
    panel_f = panels.astype(jnp.float32)
    panel_power = (panel_f[..., :PIXC] ** 2 + panel_f[..., PIXC:] ** 2).astype(jnp.bfloat16)
    flat_panels = panels.reshape(CLASSES * ORIENT, 2 * PIXC)
    flat_power = panel_power.reshape(CLASSES * ORIENT, PIXC)
    scores = jnp.dot(weighted, flat_panels.T, preferred_element_type=jnp.float32)
    scores = scores - 0.5 * jnp.dot(power, flat_power.T, preferred_element_type=jnp.float32)
    scores = scores.reshape(PTCLS, CLASSES, ORIENT)
    allowed = (prior_mask > 0)[:, :, None]
    masked = jnp.where(allowed, scores, -1e+30)
    peak = lax.optimization_barrier(jnp.max(masked, axis=(1, 2)))
    weights_exp = jnp.where(allowed, jnp.exp(masked - peak[:, None, None]), 0.0)
    total = lax.optimization_barrier(jnp.sum(weights_exp, axis=(1, 2)))
    log_evidence = peak + jnp.log(total)
    posterior = (weights_exp / total[:, None, None]).astype(jnp.bfloat16)
    inverse = jnp.zeros((ORIENT,), jnp.int32).at[orient_ids].set(jnp.arange(ORIENT, dtype=jnp.int32))
    by_direction = posterior[:, :, inverse]
    half_col = half_sets.astype(jnp.bfloat16)[:, None, None]
    split_post = jnp.stack([by_direction * (1 - half_col), by_direction * half_col], axis=2)
    flat_post = split_post.reshape(PTCLS, CLASSES * 2 * ORIENT)
    centred = (images * doubled).astype(jnp.bfloat16)
    squares_ctf = (contrast * contrast).astype(jnp.bfloat16)
    data = jnp.dot(flat_post.T, centred, preferred_element_type=jnp.float32).reshape(CLASSES, 2, ORIENT, 2 * PIXC)
    weight = jnp.dot(flat_post.T, squares_ctf, preferred_element_type=jnp.float32).reshape(CLASSES, 2, ORIENT, PIXC)

    def per_shell(values):
        summed = lax.optimization_barrier(jnp.sum(values, axis=1))
        folded = summed[:, :PIXC] + summed[:, PIXC:]
        return lax.optimization_barrier(jnp.sum(folded.reshape(CLASSES, NSHELL, PIXC // NSHELL), axis=2))
    cross = per_shell(data[:, 0] * data[:, 1])
    power_zero = per_shell(data[:, 0] * data[:, 0])
    power_one = per_shell(data[:, 1] * data[:, 1])
    fsc = cross / jnp.sqrt(power_zero * power_one + 1e-06)
    factor = (1.0 + fsc[:, shells]) / 2.0
    factor_pair = jnp.concatenate([factor, factor], axis=1)
    weight_pair = jnp.concatenate([weight, weight], axis=3)
    half_maps = data * factor_pair[:, None, None, :] / (weight_pair + 1.0)
    return (half_maps.reshape(CLASSES, 2 * ORIENT, 2 * PIXC), log_evidence)
```

```python
import jax
import jax.numpy as jnp
from jax import lax
from jax.sharding import Mesh
from jax.sharding import PartitionSpec as P

PIXC = 1024
ORIENT = 128
NSHELL = 32
NBIN = 16
AXES = ("zl", "co", "y", "zh", "x")
CLS = ("zl", "co")
PTCL = ("y", "zh", "x")
EXTRA = 128


def ctf_table():
    bins = jnp.arange(NBIN, dtype=jnp.float32)
    defocus = (bins + 1.0) / NBIN
    radius = (jnp.arange(PIXC, dtype=jnp.float32) + 0.5) / PIXC
    phase = 0.3 + 2.5 * defocus[:, None] * radius[None, :]
    return jnp.sin(phase) + 0.1 * jnp.cos(phase)


def lookup_small(indices, values):
    count = values.shape[0]
    match = indices[:, None] == jnp.arange(count, dtype=jnp.int32)[None, :]
    return jnp.sum(jnp.where(match, values[None, :], 0.0), axis=1)


def exchange(blocks, axes):
    return lax.all_to_all(blocks, axes, split_axis=0, concat_axis=0, tiled=True)


def from_all(shard, axes, count):
    return exchange(jnp.broadcast_to(shard[None], (count,) + shard.shape), axes)


def row_maps():
    r = jnp.arange(2 * ORIENT, dtype=jnp.int32)
    j, half, zh, x, y = r % 2, (r // 2) % 2, (r // 4) % 4, (r // 16) % 4, r // 64
    return 4 * (((y % 2) * 4 + zh) * 4 + x) + 2 * (y // 2) + j, half


def gathered_orients():
    r = jnp.arange(ORIENT, dtype=jnp.int32)
    j, zh, x, y = r % 2, (r // 2) % 4, (r // 8) % 4, r // 32
    return ((y * 4 + zh) * 4 + x) * 2 + j


def three_parts(table):
    high = table.astype(jnp.bfloat16)
    rest = table - high.astype(jnp.float32)
    mid = rest.astype(jnp.bfloat16)
    low = (rest - mid.astype(jnp.float32)).astype(jnp.bfloat16)
    return high, mid, low


def on_device(particles, panels, sigma2, defocus_bins, half_sets, prior_mask, orient_ids):
    by_zh = from_all(panels[0], "zh", 4).reshape(8, 2 * PIXC)
    piece = from_all(by_zh, ("y", "x"), 16).reshape(ORIENT, 2 * PIXC)

    shells = jnp.arange(PIXC, dtype=jnp.int32) * NSHELL // PIXC
    inverse_noise = lookup_small(shells, 1.0 / sigma2)
    table = ctf_table()
    match = defocus_bins[:, None] == jnp.arange(NBIN, dtype=jnp.int32)[None, :]
    onehot = match.astype(jnp.float32)
    contrast = jnp.dot(onehot, table, precision=lax.Precision.HIGHEST)
    doubled = jnp.concatenate([contrast, contrast], axis=1)
    noise_pair = jnp.concatenate([inverse_noise, inverse_noise])
    images = particles.astype(jnp.float32)
    weighted = (images * doubled * noise_pair[None, :]).astype(jnp.bfloat16)
    centred = (images * doubled).astype(jnp.bfloat16)
    power = (table * table * inverse_noise[None, :]).astype(jnp.bfloat16)
    squares = (table * table).astype(jnp.bfloat16).astype(jnp.float32)

    piece_f = piece.astype(jnp.float32)
    piece_power = (piece_f[:, :PIXC] ** 2 + piece_f[:, PIXC:] ** 2).astype(jnp.bfloat16)
    direct = lax.dot_general(
        piece, weighted, (((1,), (1,)), ((), ())), preferred_element_type=jnp.float32
    )
    norm_table = lax.dot_general(
        piece_power, power, (((1,), (1,)), ((), ())), preferred_element_type=jnp.float32
    )
    norm_part = lax.dot_general(
        norm_table, onehot, (((1,), (1,)), ((), ())), precision=lax.Precision.HIGHEST
    )
    scores = direct - 0.5 * norm_part
    allowed = (prior_mask.reshape(-1) > 0)[None, :]
    masked = jnp.where(allowed, scores, -1e30)
    own_peak = jnp.max(masked, axis=0)
    own_exp = jnp.where(allowed, jnp.exp(masked - own_peak[None, :]), 0.0)
    own_total = jnp.sum(own_exp, axis=0)

    both = from_all(jnp.stack([own_peak, own_total]), CLS, 8)
    peak = jnp.max(both[:, 0], axis=0)
    total = jnp.sum(both[:, 1] * jnp.exp(both[:, 0] - peak[None, :]), axis=0)
    log_evidence = peak + jnp.log(total)
    posterior = (own_exp * (jnp.exp(own_peak - peak) / total)[None, :]).astype(jnp.bfloat16)

    direction, half = row_maps()
    select = jnp.sum(
        jnp.where(
            gathered_orients()[:, None] == jnp.arange(ORIENT, dtype=jnp.int32)[None, :],
            orient_ids[None, :],
            0,
        ),
        axis=1,
    )
    permuter = (direction[:, None] == select[None, :]).astype(jnp.bfloat16)
    by_direction = jnp.dot(permuter, posterior, preferred_element_type=jnp.float32)
    split_post = jnp.where(half[:, None] == half_sets[None, :], by_direction, 0.0).astype(
        jnp.bfloat16
    )
    data_part = jnp.dot(split_post, centred, preferred_element_type=jnp.float32)
    bin_part = jnp.dot(split_post, match.astype(jnp.bfloat16), preferred_element_type=jnp.float32)

    top = jnp.max(jnp.abs(data_part), axis=1, keepdims=True)
    expo = jnp.clip(jnp.floor(jnp.log2(jnp.maximum(top, 1e-30))), -100.0, 126.0) - 13.0
    small = (data_part * jnp.exp2(-expo)).astype(jnp.float16)
    bin_high = bin_part.astype(jnp.float16)
    bin_low = (bin_part - bin_high.astype(jnp.float32)).astype(jnp.float16)
    side = jnp.concatenate(
        [bin_high, bin_low, jnp.broadcast_to(expo, (2 * ORIENT, EXTRA - 2 * NBIN)).astype(jnp.float16)],
        axis=1,
    )
    packed = jnp.concatenate([small, side], axis=1).reshape(16, 16, 2 * PIXC + EXTRA)
    came = exchange(packed, ("y", "x")).astype(jnp.float32)
    unscale = jnp.exp2(came[:, :, -1:])
    data_16 = jnp.sum(came[:, :, : 2 * PIXC] * unscale, axis=0)
    bins_16 = jnp.sum(came[:, :, 2 * PIXC :], axis=0)
    second = jnp.concatenate([data_16, bins_16], axis=1).reshape(4, 4, 2 * PIXC + EXTRA)
    summed = jnp.sum(exchange(second, "zh"), axis=0)
    data = summed[:, : 2 * PIXC]
    bins = summed[:, 2 * PIXC : 2 * PIXC + NBIN] + summed[:, 2 * PIXC + NBIN : 2 * PIXC + 2 * NBIN]
    weight = jnp.dot(bins, squares, precision=lax.Precision.HIGHEST)
    weight_pair = jnp.concatenate([weight, weight], axis=1)
    scaled = data / (weight_pair + 1.0)

    upper = lax.axis_index("y") // 2
    keep = jnp.where(upper == 0, scaled[:2], scaled[2:])
    give = jnp.where(upper == 0, scaled[2:], scaled[:2])
    got = lax.ppermute(give, "y", [(i, i ^ 2) for i in range(4)])

    def per_shell(values):
        summed_rows = jnp.sum(values, axis=0)
        folded = summed_rows[:PIXC] + summed_rows[PIXC:]
        return jnp.sum(folded.reshape(NSHELL, PIXC // NSHELL), axis=1)

    stats = jnp.concatenate(
        [
            per_shell(data[:2] * data[2:]),
            per_shell(data[:2] * data[:2]),
            per_shell(data[2:] * data[2:]),
            jnp.zeros((32,), jnp.float32),
        ]
    )
    stats = jnp.sum(from_all(stats[None], ("y", "x"), 16), axis=0)
    totals = jnp.sum(from_all(stats, "zh", 4), axis=0).reshape(4, NSHELL)
    fsc = totals[0] / jnp.sqrt(totals[1] * totals[2] + 1e-06)
    factor = (1.0 + lookup_small(shells, fsc)) / 2.0
    factor_pair = jnp.concatenate([factor, factor])
    first = jnp.where(upper == 0, keep, got)
    last = jnp.where(upper == 0, got, keep)
    half_maps = jnp.concatenate([first, last], axis=0) * factor_pair[None, :]
    return (half_maps[None], log_evidence)


def solution(mesh):
    split = Mesh(mesh.devices.reshape(4, 2, 4, 4, 4), AXES)
    placed = (
        P(PTCL, None),
        P(CLS, PTCL, None),
        P(),
        P(PTCL),
        P(PTCL),
        P(PTCL, CLS),
        P(),
    )
    return jax.shard_map(
        on_device,
        mesh=split,
        in_specs=placed,
        out_specs=(P(CLS, PTCL, None), P(PTCL)),
        check_vma=False,
    )
```

```python
import jax
import jax.numpy as jnp
from jax import lax
from jax.experimental import pallas as pl
from jax.experimental.pallas import tpu as pltpu
from jax.sharding import Mesh
from jax.sharding import PartitionSpec as P

PIXC = 1024
COLS = 2 * PIXC
ORIENT = 128
ROWS = 2 * ORIENT
NSHELL = 32
NBIN = 16
AXES = ("zl", "co", "y", "zh", "x")
CLS = ("zl", "co")
PTCL = ("y", "zh", "x")
PLANE = ("y", "x")
SIDE = 128
WIDE = COLS + SIDE
CODE = 32767.0
F32 = jnp.float32
BF16 = jnp.bfloat16
HIGHEST = lax.Precision.HIGHEST
PARAMS = pltpu.CompilerParams(vmem_limit_bytes=48 * 1024 * 1024)


def ctf_table():
    bins = jnp.arange(NBIN, dtype=F32)
    defocus = (bins + 1.0) / NBIN
    radius = (jnp.arange(PIXC, dtype=F32) + 0.5) / PIXC
    phase = 0.3 + 2.5 * defocus[:, None] * radius[None, :]
    return jnp.sin(phase) + 0.1 * jnp.cos(phase)


def lookup_small(indices, values):
    count = values.shape[0]
    match = indices[:, None] == jnp.arange(count, dtype=jnp.int32)[None, :]
    return jnp.sum(jnp.where(match, values[None, :], 0.0), axis=1)


def exchange(blocks, axes):
    return lax.all_to_all(blocks, axes, split_axis=0, concat_axis=0, tiled=True)


def from_all(shard, axes, count):
    return exchange(jnp.broadcast_to(shard[None], (count,) + shard.shape), axes)


def row_maps():
    r = jnp.arange(ROWS, dtype=jnp.int32)
    j, swap, zh, x, y = r % 2, (r // 2) % 2, (r // 4) % 4, (r // 16) % 4, r // 64
    direction = 4 * (((y % 2) * 4 + zh) * 4 + x) + 2 * (y // 2) + j
    return direction, (swap + y // 2) % 2


def gathered_orients():
    r = jnp.arange(ORIENT, dtype=jnp.int32)
    j, zh, x, y = r % 2, (r // 2) % 4, (r // 8) % 4, r // 32
    return ((y * 4 + zh) * 4 + x) * 2 + j


def three_parts(table, axis):
    high = table.astype(BF16)
    rest = table - high.astype(F32)
    mid = rest.astype(BF16)
    low = (rest - mid.astype(F32)).astype(BF16)
    return jnp.concatenate([high, mid, low], axis=axis)


def table_parts(table):
    high = lax.reduce_precision(table, 8, 7)
    mid = lax.reduce_precision(table - high, 8, 7)
    low = table - high - mid
    return jnp.concatenate([high, mid, low], axis=0).astype(BF16)


def bin_match(bins, copies):
    row = lax.broadcasted_iota(jnp.int32, (copies * NBIN, bins.shape[1]), 0)
    return jnp.where(row % NBIN == bins, 1.0, 0.0).astype(BF16)


def contract(left, right, dims):
    return lax.dot_general(left, right, (dims, ((), ())), preferred_element_type=F32)


def encode(values):
    top = jnp.max(jnp.abs(values), axis=1, keepdims=True)
    expo = jnp.floor(jnp.log2(jnp.maximum(top, 1e-30))) + 1.0
    root = jnp.sqrt(jnp.sqrt(jnp.minimum(jnp.abs(values) * jnp.exp2(-expo), 1.0)))
    size = jnp.floor(root * CODE + 0.5)
    codes = jnp.where(values < 0.0, -size, size).astype(jnp.int32).astype(jnp.int16)
    return codes, expo


def side_block(sums, expo, unit):
    fixed = jnp.floor(sums * unit + 0.5).astype(jnp.int32)
    high = lax.shift_right_arithmetic(fixed, 16)
    low = (fixed & 65535) - 32768
    tail = jnp.broadcast_to(expo.astype(jnp.int32), (sums.shape[0], SIDE - 2 * NBIN))
    return jnp.concatenate([high, low, tail], axis=1).astype(jnp.int16)


def decode_sum(ref, count, unit):
    data = jnp.zeros((ref.shape[1], COLS), F32)
    sums = jnp.zeros((ref.shape[1], NBIN), F32)
    for source in range(count):
        side = ref[source, :, COLS:].astype(jnp.int32)
        scale = jnp.exp2(side[:, SIDE - 1 :].astype(F32))
        root = ref[source, :, :COLS].astype(jnp.int32).astype(F32) * (1.0 / CODE)
        data = data + root * jnp.abs(root) * (root * root) * scale
        fixed = side[:, :NBIN] * 65536 + (side[:, NBIN : 2 * NBIN] + 32768)
        sums = sums + fixed.astype(F32) * (1.0 / unit)
    return data, sums


def image_kernel(x_ref, bins_ref, table_ref, noise_ref, centred_ref, weighted_ref):
    match = bin_match(bins_ref[...], 3)
    contrast = contract(match, table_ref[...], ((0,), (0,)))
    noise = noise_ref[...]
    for part in range(2):
        cols = slice(part * PIXC, (part + 1) * PIXC)
        product = x_ref[:, cols].astype(F32) * contrast
        centred_ref[:, cols] = product.astype(BF16)
        weighted_ref[:, cols] = (product * noise).astype(BF16)


def score_kernel(panel_ref, weighted_ref, power_ref, bins_ref, mask_ref, exp_ref, pair_ref, norm_ref):
    @pl.when(pl.program_id(0) == 0)
    def _():
        real = panel_ref[:, :PIXC].astype(F32)
        imag = panel_ref[:, PIXC:].astype(F32)
        panel_power = (real * real + imag * imag).astype(BF16)
        norm = contract(panel_power, power_ref[...], ((1,), (1,)))
        norm_ref[...] = three_parts(norm, 1)

    direct = contract(panel_ref[...], weighted_ref[...], ((1,), (1,)))
    norm_part = contract(norm_ref[...], bin_match(bins_ref[...], 3), ((1,), (0,)))
    scores = direct - 0.5 * norm_part
    allowed = mask_ref[...] > 0
    masked = jnp.where(allowed, scores, -1e30)
    peak = jnp.max(masked, axis=0, keepdims=True)
    weights = jnp.where(allowed, jnp.exp(masked - peak), 0.0)
    exp_ref[...] = weights
    total = jnp.sum(weights, axis=0, keepdims=True)
    pair = jnp.concatenate([peak, total], axis=0)
    pair_ref[...] = jnp.broadcast_to(pair[None], pair_ref.shape)


def project_kernel(
    exp_ref, own_ref, both_ref, permuter_ref, row_half_ref, half_ref, bins_ref, centred_ref,
    packed_ref, evidence_ref, post_ref, data_ref
):
    step = pl.program_id(0)
    width = centred_ref.shape[1]

    @pl.when(step == 0)
    def _():
        own_peak = own_ref[0, 0:1, :]
        peak = both_ref[0, 0:1, :]
        for c in range(1, both_ref.shape[0]):
            peak = jnp.maximum(peak, both_ref[c, 0:1, :])
        total = jnp.zeros_like(peak)
        for c in range(both_ref.shape[0]):
            total = total + both_ref[c, 1:2, :] * jnp.exp(both_ref[c, 0:1, :] - peak)
        evidence_ref[...] = peak + jnp.log(total)
        posterior = (exp_ref[...] * (jnp.exp(own_peak - peak) / total)).astype(BF16)
        by_direction = contract(permuter_ref[...], posterior, ((1,), (0,)))
        kept = row_half_ref[...] == half_ref[...]
        post_ref[...] = jnp.where(kept, by_direction, 0.0).astype(BF16)

    data_ref[step] = contract(post_ref[...], centred_ref[...], ((1,), (0,)))

    @pl.when(step == pl.num_programs(0) - 1)
    def _():
        sums = contract(post_ref[...], bin_match(bins_ref[...], 1), ((1,), (1,)))
        for block in range(16):
            rows = slice(block * 16, block * 16 + 16)
            values = jnp.concatenate(
                [data_ref[s, rows, :] for s in range(data_ref.shape[0])], axis=1
            )
            codes, expo = encode(values)
            packed_ref[block, :, :COLS] = codes
            packed_ref[block, :, COLS:] = side_block(sums[rows], expo, 2.0**20)


def plane_kernel(came_ref, packed_ref):
    data, sums = decode_sum(came_ref, 16, 2.0**20)
    codes, expo = encode(data)
    side = side_block(sums, expo, 2.0**16)
    for other in range(4):
        packed_ref[other, :, :COLS] = codes
        packed_ref[other, :, COLS:] = side


def shell_kernel(where_ref, came_ref, squares_ref, shells_ref, keep_ref, give_ref, stats_ref):
    upper = where_ref[0]
    zh = where_ref[1]
    data, sums = decode_sum(came_ref, 4, 2.0**16)
    cross = jnp.zeros((1, COLS), F32)
    first = jnp.zeros((1, COLS), F32)
    second = jnp.zeros((1, COLS), F32)
    own_data = jnp.zeros((4, COLS), F32)
    own_sums = jnp.zeros((4, NBIN), F32)
    for z in range(4):
        rows = data[4 * z : 4 * z + 4]
        own_data = jnp.where(zh == z, rows, own_data)
        own_sums = jnp.where(zh == z, sums[4 * z : 4 * z + 4], own_sums)
        cross = cross + jnp.sum(rows[:2] * rows[2:], axis=0, keepdims=True)
        first = first + jnp.sum(rows[:2] * rows[:2], axis=0, keepdims=True)
        second = second + jnp.sum(rows[2:] * rows[2:], axis=0, keepdims=True)
    power0 = jnp.where(upper == 0, first, second)
    power1 = jnp.where(upper == 0, second, first)
    three = jnp.concatenate([cross, power0, power1, jnp.zeros((5, COLS), F32)], axis=0)
    folded = three[:, :PIXC] + three[:, PIXC:]
    by_shell = jnp.dot(folded, shells_ref[...], precision=HIGHEST, preferred_element_type=F32)
    stats_ref[...] = jnp.broadcast_to(by_shell[None], stats_ref.shape)
    weight = jnp.dot(own_sums, squares_ref[...], precision=HIGHEST, preferred_element_type=F32)
    for part in range(2):
        cols = slice(part * PIXC, (part + 1) * PIXC)
        scaled = own_data[:, cols] / (weight + 1.0)
        keep_ref[:, cols] = scaled[:2]
        give_ref[:, cols] = scaled[2:]


def finish_kernel(where_ref, came_ref, keep_ref, got_ref, shells_ref, out_ref):
    totals = came_ref[0]
    for source in range(1, 16):
        totals = totals + came_ref[source]
    fsc = totals[0:1] / jnp.sqrt(totals[1:2] * totals[2:3] + 1e-06)
    half = jnp.broadcast_to((1.0 + fsc) / 2.0, (8, ORIENT))
    factor = lax.dot_general(
        half, shells_ref[...], (((1,), (1,)), ((), ())), precision=HIGHEST,
        preferred_element_type=F32,
    )[0:1]
    low = where_ref[0] == 0
    for part in range(2):
        cols = slice(part * PIXC, (part + 1) * PIXC)
        keep = keep_ref[:, cols] * factor
        got = got_ref[:, cols] * factor
        out_ref[0, 0:2, cols] = jnp.where(low, keep, got)
        out_ref[0, 2:4, cols] = jnp.where(low, got, keep)


def full(shape):
    return pl.BlockSpec(shape, lambda i: (0,) * len(shape))


def on_device(particles, panels, sigma2, defocus_bins, half_sets, prior_mask, orient_ids):
    count = particles.shape[0]
    block = count // 4
    by_zh = from_all(panels[0], "zh", 4).reshape(8, COLS)
    piece = from_all(by_zh, PLANE, 16).reshape(ORIENT, COLS)

    shells = jnp.arange(PIXC, dtype=jnp.int32) * NSHELL // PIXC
    inverse_noise = lookup_small(shells, 1.0 / sigma2)
    table = ctf_table()
    power = (table * table * inverse_noise[None, :]).astype(BF16)
    squares = (table * table).astype(BF16).astype(F32)
    shell_match = (shells[:, None] == jnp.arange(ORIENT, dtype=jnp.int32)[None, :]).astype(F32)
    bins_row = defocus_bins[None, :]
    where = jnp.stack([lax.axis_index("y") // 2, lax.axis_index("zh")]).astype(jnp.int32)

    direction, row_half = row_maps()
    match = gathered_orients()[:, None] == jnp.arange(ORIENT, dtype=jnp.int32)[None, :]
    select = jnp.sum(jnp.where(match, orient_ids[None, :], 0), axis=1)
    permuter = (direction[:, None] == select[None, :]).astype(BF16)

    centred, weighted = pl.pallas_call(
        image_kernel,
        grid=(4,),
        in_specs=[
            pl.BlockSpec((block, COLS), lambda i: (i, 0)),
            pl.BlockSpec((1, block), lambda i: (0, i)),
            full((3 * NBIN, PIXC)),
            full((1, PIXC)),
        ],
        out_specs=[pl.BlockSpec((block, COLS), lambda i: (i, 0))] * 2,
        out_shape=[jax.ShapeDtypeStruct((count, COLS), BF16)] * 2,
        compiler_params=PARAMS,
        name="images",
    )(particles, bins_row, table_parts(table), inverse_noise[None, :])

    own_exp, pair = pl.pallas_call(
        score_kernel,
        grid=(4,),
        in_specs=[
            full((ORIENT, COLS)),
            pl.BlockSpec((block, COLS), lambda i: (i, 0)),
            full((NBIN, PIXC)),
            pl.BlockSpec((1, block), lambda i: (0, i)),
            pl.BlockSpec((1, block), lambda i: (0, i)),
        ],
        out_specs=[
            pl.BlockSpec((ORIENT, block), lambda i: (0, i)),
            pl.BlockSpec((8, 2, block), lambda i: (0, 0, i)),
        ],
        out_shape=[
            jax.ShapeDtypeStruct((ORIENT, count), F32),
            jax.ShapeDtypeStruct((8, 2, count), F32),
        ],
        scratch_shapes=[pltpu.VMEM((ORIENT, 3 * NBIN), BF16)],
        compiler_params=PARAMS,
        name="scores",
    )(piece, weighted, power, bins_row, prior_mask.reshape(1, count))

    both = exchange(pair, CLS)
    packed, evidence = pl.pallas_call(
        project_kernel,
        grid=(4,),
        in_specs=[
            full((ORIENT, count)),
            full((8, 2, count)),
            full((8, 2, count)),
            full((ROWS, ORIENT)),
            full((ROWS, 1)),
            full((1, count)),
            full((1, count)),
            pl.BlockSpec((count, COLS // 4), lambda i: (0, i)),
        ],
        out_specs=[full((16, 16, WIDE)), full((1, count))],
        out_shape=[
            jax.ShapeDtypeStruct((16, 16, WIDE), jnp.int16),
            jax.ShapeDtypeStruct((1, count), F32),
        ],
        scratch_shapes=[
            pltpu.VMEM((ROWS, count), BF16),
            pltpu.VMEM((4, ROWS, COLS // 4), F32),
        ],
        compiler_params=PARAMS,
        name="project",
    )(own_exp, pair, both, permuter, row_half[:, None], half_sets[None, :], bins_row, centred)

    second = pl.pallas_call(
        plane_kernel,
        out_shape=jax.ShapeDtypeStruct((4, 16, WIDE), jnp.int16),
        compiler_params=PARAMS,
        name="plane",
    )(exchange(packed, PLANE))

    smem = pl.BlockSpec(memory_space=pltpu.SMEM)
    vmem = pl.BlockSpec(memory_space=pltpu.VMEM)
    keep, give, stats = pl.pallas_call(
        shell_kernel,
        in_specs=[smem, vmem, vmem, vmem],
        out_shape=[
            jax.ShapeDtypeStruct((2, COLS), F32),
            jax.ShapeDtypeStruct((2, COLS), F32),
            jax.ShapeDtypeStruct((16, 8, ORIENT), F32),
        ],
        compiler_params=PARAMS,
        name="shells",
    )(where, exchange(second, "zh"), squares, shell_match)

    got = lax.ppermute(give, "y", [(i, i ^ 2) for i in range(4)])
    half_maps = pl.pallas_call(
        finish_kernel,
        in_specs=[smem, vmem, vmem, vmem, vmem],
        out_shape=jax.ShapeDtypeStruct((1, 4, COLS), F32),
        compiler_params=PARAMS,
        name="finish",
    )(where, exchange(stats, PLANE), keep, got, shell_match)
    return (half_maps, evidence.reshape(count))


def solution(mesh):
    split = Mesh(mesh.devices.reshape(4, 2, 4, 4, 4), AXES)
    placed = (
        P(PTCL, None),
        P(CLS, PTCL, None),
        P(),
        P(PTCL),
        P(PTCL),
        P(PTCL, CLS),
        P(),
    )
    return jax.shard_map(
        on_device,
        mesh=split,
        in_specs=placed,
        out_specs=(P(CLS, PTCL, None), P(PTCL)),
        check_vma=False,
    )
```

```python
import jax
import jax.numpy as jnp
from jax import lax
from jax.experimental import pallas as pl
from jax.experimental.pallas import tpu as pltpu
from jax.sharding import Mesh
from jax.sharding import PartitionSpec as P

PIXC = 1024
COLS = 2 * PIXC
ORIENT = 128
ROWS = 2 * ORIENT
NSHELL = 32
NBIN = 16
AXES = ("zl", "co", "y", "zh", "x")
CLS = ("zl", "co")
PTCL = ("y", "zh", "x")
PLANE = ("y", "x")
SIDE = 128
WIDE = COLS + SIDE
CODE = 32767.0
PARTS = 4
PART = COLS // PARTS
F32 = jnp.float32
BF16 = jnp.bfloat16
HIGHEST = lax.Precision.HIGHEST


def ctf_table():
    bins = jnp.arange(NBIN, dtype=F32)
    defocus = (bins + 1.0) / NBIN
    radius = (jnp.arange(PIXC, dtype=F32) + 0.5) / PIXC
    phase = 0.3 + 2.5 * defocus[:, None] * radius[None, :]
    return jnp.sin(phase) + 0.1 * jnp.cos(phase)


def lookup_small(indices, values):
    count = values.shape[0]
    match = indices[:, None] == jnp.arange(count, dtype=jnp.int32)[None, :]
    return jnp.sum(jnp.where(match, values[None, :], 0.0), axis=1)


def exchange(blocks, axes):
    return lax.all_to_all(blocks, axes, split_axis=0, concat_axis=0, tiled=True)


def from_all(shard, axes, count):
    return exchange(jnp.broadcast_to(shard[None], (count,) + shard.shape), axes)


def row_maps():
    r = jnp.arange(ROWS, dtype=jnp.int32)
    j, swap, zh, x, y = r % 2, (r // 2) % 2, (r // 4) % 4, (r // 16) % 4, r // 64
    direction = 4 * (((y % 2) * 4 + zh) * 4 + x) + 2 * (y // 2) + j
    return direction, (swap + y // 2) % 2


def gathered_orients():
    r = jnp.arange(ORIENT, dtype=jnp.int32)
    j, zh, x, y = r % 2, (r // 2) % 4, (r // 8) % 4, r // 32
    return ((y * 4 + zh) * 4 + x) * 2 + j


def three_parts(table, axis):
    high = table.astype(BF16)
    rest = table - high.astype(F32)
    mid = rest.astype(BF16)
    low = (rest - mid.astype(F32)).astype(BF16)
    return jnp.concatenate([high, mid, low], axis=axis)


def table_parts(table):
    high = lax.reduce_precision(table, 8, 7)
    mid = lax.reduce_precision(table - high, 8, 7)
    low = table - high - mid
    return jnp.concatenate([high, mid, low], axis=0).astype(BF16)


def bin_match(bins, copies):
    row = lax.broadcasted_iota(jnp.int32, (copies * NBIN, bins.shape[1]), 0)
    return jnp.where(row % NBIN == bins, 1.0, 0.0).astype(BF16)


def contract(left, right, dims):
    return lax.dot_general(left, right, (dims, ((), ())), preferred_element_type=F32)


def encode(values):
    size = jnp.abs(values)
    top = jnp.max(size, axis=1, keepdims=True)
    expo = jnp.floor(jnp.log2(jnp.maximum(top, 1e-30))) + 1.0
    root = lax.rsqrt(lax.rsqrt(jnp.maximum(size * jnp.exp2(-expo), 1e-36)))
    code = root * CODE + 0.5
    codes = jnp.where(values < 0.0, -code, code).astype(jnp.int32).astype(jnp.int16)
    return codes, expo


def side_block(sums, expos, unit):
    fixed = jnp.floor(sums * unit + 0.5).astype(jnp.int32)
    high = lax.shift_right_arithmetic(fixed, 16)
    low = (fixed & 65535) - 32768
    shape = (sums.shape[0], SIDE - 2 * NBIN)
    lane = lax.broadcasted_iota(jnp.int32, shape, 1)
    tail = jnp.zeros(shape, F32)
    for part, expo in enumerate(expos):
        tail = jnp.where(lane == part, expo, tail)
    return jnp.concatenate([high, low, tail.astype(jnp.int32)], axis=1).astype(jnp.int16)


def decode_part(ref, count, part):
    cols = slice(part * PART, (part + 1) * PART)
    at = COLS + 2 * NBIN + part
    data = jnp.zeros((ref.shape[1], PART), F32)
    for source in range(count):
        expo = ref[source, :, COLS:].astype(jnp.int32)[:, at - COLS : at - COLS + 1]
        scale = jnp.exp2(expo.astype(F32)) * (1.0 / CODE**4)
        root = ref[source, :, cols].astype(jnp.int32).astype(F32)
        data = data + root * jnp.abs(root) * (root * root) * scale
    return data


def decode_bins(ref, count, unit):
    sums = jnp.zeros((ref.shape[1], NBIN), F32)
    for source in range(count):
        side = ref[source, :, COLS:].astype(jnp.int32)
        fixed = side[:, :NBIN] * 65536 + (side[:, NBIN : 2 * NBIN] + 32768)
        sums = sums + fixed.astype(F32) * (1.0 / unit)
    return sums


def image_kernel(
    x_ref, bins_ref, table_ref, noise_ref, centred_ref, weighted_ref, x_buf, centred_buf,
    weighted_buf, sems
):
    noise = noise_ref[...]
    step = x_buf.shape[0] // PARTS
    spans = [slice(i * step, (i + 1) * step) for i in range(PARTS)]
    reads, writes = [], []
    for i, rows in enumerate(spans):
        reads.append(pltpu.make_async_copy(x_ref.at[rows], x_buf.at[rows], sems.at[0, i]))
        reads[i].start()
    for i, rows in enumerate(spans):
        match = bin_match(bins_ref[:, rows], 3)
        contrast = contract(match, table_ref[...], ((0,), (0,)))
        reads[i].wait()
        for part in range(2):
            cols = slice(part * PIXC, (part + 1) * PIXC)
            product = x_buf[rows, cols].astype(F32) * contrast
            centred_buf[rows, cols] = product.astype(BF16)
            weighted_buf[rows, cols] = (product * noise).astype(BF16)
        for k, buf, out in ((1, centred_buf, centred_ref), (2, weighted_buf, weighted_ref)):
            writes.append(pltpu.make_async_copy(buf.at[rows], out.at[rows], sems.at[k, i]))
            writes[-1].start()
    for write in writes:
        write.wait()


def score_kernel(
    panel_ref, power_ref, bins_ref, mask_ref, weighted_ref, exp_ref, pair_ref, weighted_buf, sems
):
    step = weighted_buf.shape[0] // PARTS
    reads = []
    for i in range(PARTS):
        rows = slice(i * step, (i + 1) * step)
        reads.append(
            pltpu.make_async_copy(weighted_ref.at[rows], weighted_buf.at[rows], sems.at[i])
        )
        reads[i].start()
    real = panel_ref[:, :PIXC].astype(F32)
    imag = panel_ref[:, PIXC:].astype(F32)
    panel_power = (real * real + imag * imag).astype(BF16)
    norm = three_parts(contract(panel_power, power_ref[...], ((1,), (1,))), 1)
    for i in range(PARTS):
        rows = slice(i * step, (i + 1) * step)
        norm_part = contract(norm, bin_match(bins_ref[:, rows], 3), ((1,), (0,)))
        reads[i].wait()
        direct = contract(panel_ref[...], weighted_buf[rows, :], ((1,), (1,)))
        scores = direct - 0.5 * norm_part
        allowed = mask_ref[:, rows] > 0
        masked = jnp.where(allowed, scores, -1e30)
        peak = jnp.max(masked, axis=0, keepdims=True)
        weights = jnp.where(allowed, jnp.exp(masked - peak), 0.0)
        exp_ref[:, rows] = weights
        total = jnp.sum(weights, axis=0, keepdims=True)
        pair = jnp.concatenate([peak, total], axis=0)
        for other in range(8):
            pair_ref[other, :, rows] = pair


def project_kernel(
    exp_ref, own_ref, both_ref, permuter_ref, row_half_ref, half_ref, bins_ref, centred_ref,
    packed_ref, evidence_ref, centred_buf, sems
):
    spans = [slice(part * PART, (part + 1) * PART) for part in range(PARTS)]
    reads = []
    for part, cols in enumerate(spans):
        reads.append(
            pltpu.make_async_copy(centred_ref.at[:, cols], centred_buf.at[:, cols], sems.at[part])
        )
        reads[part].start()
    own_peak = own_ref[0, 0:1, :]
    peak = both_ref[0, 0:1, :]
    for c in range(1, both_ref.shape[0]):
        peak = jnp.maximum(peak, both_ref[c, 0:1, :])
    total = jnp.zeros_like(peak)
    for c in range(both_ref.shape[0]):
        total = total + both_ref[c, 1:2, :] * jnp.exp(both_ref[c, 0:1, :] - peak)
    evidence_ref[...] = peak + jnp.log(total)
    posterior = (exp_ref[...] * (jnp.exp(own_peak - peak) / total)).astype(BF16)
    by_direction = contract(permuter_ref[...], posterior, ((1,), (0,)))
    kept = row_half_ref[...] == half_ref[...]
    post = jnp.where(kept, by_direction, 0.0).astype(BF16)
    sums = contract(post, bin_match(bins_ref[...], 1), ((1,), (1,)))
    expos = []
    for part, cols in enumerate(spans):
        reads[part].wait()
        codes, expo = encode(contract(post, centred_buf[:, cols], ((1,), (0,))))
        expos.append(expo)
        packed_ref[:, cols] = codes
    packed_ref[:, COLS:] = side_block(sums, expos, 2.0**20)


def plane_kernel(came_ref, packed_ref):
    expos = []
    for part in range(PARTS):
        codes, expo = encode(decode_part(came_ref, 16, part))
        expos.append(expo)
        for other in range(4):
            packed_ref[other, :, part * PART : (part + 1) * PART] = codes
    side = side_block(decode_bins(came_ref, 16, 2.0**20), expos, 2.0**16)
    for other in range(4):
        packed_ref[other, :, COLS:] = side


def shell_kernel(where_ref, came_ref, squares_ref, shells_ref, keep_ref, stats_ref):
    upper = where_ref[0]
    zh = where_ref[1]
    data = jnp.concatenate([decode_part(came_ref, 4, part) for part in range(PARTS)], axis=1)
    sums = decode_bins(came_ref, 4, 2.0**16)
    cross = jnp.zeros((1, COLS), F32)
    first = jnp.zeros((1, COLS), F32)
    second = jnp.zeros((1, COLS), F32)
    own_data = jnp.zeros((4, COLS), F32)
    own_sums = jnp.zeros((4, NBIN), F32)
    for z in range(4):
        rows = data[4 * z : 4 * z + 4]
        own_data = jnp.where(zh == z, rows, own_data)
        own_sums = jnp.where(zh == z, sums[4 * z : 4 * z + 4], own_sums)
        cross = cross + jnp.sum(rows[:2] * rows[2:], axis=0, keepdims=True)
        first = first + jnp.sum(rows[:2] * rows[:2], axis=0, keepdims=True)
        second = second + jnp.sum(rows[2:] * rows[2:], axis=0, keepdims=True)
    power0 = jnp.where(upper == 0, first, second)
    power1 = jnp.where(upper == 0, second, first)
    three = jnp.concatenate([cross, power0, power1, jnp.zeros((5, COLS), F32)], axis=0)
    folded = three[:, :PIXC] + three[:, PIXC:]
    by_shell = jnp.dot(folded, shells_ref[...], precision=HIGHEST, preferred_element_type=F32)
    weight = jnp.dot(own_sums, squares_ref[...], precision=HIGHEST, preferred_element_type=F32)
    whole = own_data / (jnp.concatenate([weight, weight], axis=1) + 1.0)
    keep_ref[...] = whole[:2]
    for other in range(16):
        stats_ref[other, :, PART:] = by_shell
    for part in range(PARTS):
        piece = whole[2:, part * PART : (part + 1) * PART]
        for other in range(16):
            stats_ref[other, 2 * part : 2 * part + 2, :PART] = piece


def finish_kernel(where_ref, came_ref, keep_ref, shells_ref, out_ref):
    totals = came_ref[0, :, PART:]
    for source in range(1, 16):
        totals = totals + came_ref[source, :, PART:]
    fsc = totals[0:1] / jnp.sqrt(totals[1:2] * totals[2:3] + 1e-06)
    half = jnp.broadcast_to((1.0 + fsc) / 2.0, (8, ORIENT))
    factor = lax.dot_general(
        half, shells_ref[...], (((1,), (1,)), ((), ())), precision=HIGHEST,
        preferred_element_type=F32,
    )[0:1]
    low = where_ref[0] == 0
    partner = came_ref[where_ref[2]]
    for part in range(PARTS):
        cols = slice(part * PART, (part + 1) * PART)
        start = (part * PART) % PIXC
        scale = factor[:, start : start + PART]
        keep = keep_ref[:, cols] * scale
        got = partner[2 * part : 2 * part + 2, :PART] * scale
        out_ref[0, 0:2, cols] = jnp.where(low, keep, got)
        out_ref[0, 2:4, cols] = jnp.where(low, got, keep)


def call(kernel, name, out_shape, mega, *args, scalars=0, far=(), far_out=(), scratch=()):
    def space(i, hbm):
        if i < 0:
            return pl.BlockSpec(memory_space=pltpu.MemorySpace.SMEM)
        return pl.BlockSpec(
            memory_space=pltpu.MemorySpace.HBM if i in hbm else pltpu.MemorySpace.VMEM
        )

    args = [
        pltpu.with_memory_space_constraint(arg, pltpu.MemorySpace.HBM) if i in far else arg
        for i, arg in enumerate(args)
    ]
    return pl.pallas_call(
        kernel,
        in_specs=[space(i if i >= scalars else -1, far) for i in range(len(args))],
        out_specs=[space(i, far_out) for i in range(len(out_shape))],
        out_shape=out_shape,
        scratch_shapes=scratch,
        compiler_params=pltpu.CompilerParams(vmem_limit_bytes=mega * 1024 * 1024),
        name=name,
    )(*args)


def on_device(particles, panels, sigma2, defocus_bins, half_sets, prior_mask, orient_ids):
    count = particles.shape[0]
    of = jax.ShapeDtypeStruct

    shells = jnp.arange(PIXC, dtype=jnp.int32) * NSHELL // PIXC
    inverse_noise = lookup_small(shells, 1.0 / sigma2)
    table = ctf_table()
    power = (table * table * inverse_noise[None, :]).astype(BF16)
    squares = (table * table).astype(BF16).astype(F32)
    shell_match = (shells[:, None] == jnp.arange(ORIENT, dtype=jnp.int32)[None, :]).astype(F32)
    bins_row = defocus_bins[None, :]
    y, zh, x = lax.axis_index("y"), lax.axis_index("zh"), lax.axis_index("x")
    where = jnp.stack([y // 2, zh, (y ^ 2) * 4 + x]).astype(jnp.int32)

    direction, row_half = row_maps()
    match = gathered_orients()[:, None] == jnp.arange(ORIENT, dtype=jnp.int32)[None, :]
    select = jnp.sum(jnp.where(match, orient_ids[None, :], 0), axis=1)
    permuter = (direction[:, None] == select[None, :]).astype(BF16)

    images = pltpu.VMEM((count, COLS), BF16)
    centred, weighted = call(
        image_kernel, "images", [pltpu.MemorySpace.HBM((count, COLS), BF16)] * 2, 24,
        particles, bins_row, table_parts(table), inverse_noise[None, :],
        far=(0,), far_out=(0, 1),
        scratch=[images] * 3 + [pltpu.SemaphoreType.DMA((3, PARTS))],
    )
    by_zh = from_all(panels[0], "zh", 4)
    by_zh, centred, weighted = lax.optimization_barrier((by_zh, centred, weighted))
    piece = from_all(by_zh.reshape(8, COLS), PLANE, 16).reshape(ORIENT, COLS)

    own_exp, pair = call(
        score_kernel, "scores", [of((ORIENT, count), F32), of((8, 2, count), F32)], 14,
        piece, power, bins_row, prior_mask.reshape(1, count), weighted,
        far=(4,), scratch=[images, pltpu.SemaphoreType.DMA((PARTS,))],
    )
    packed, evidence = call(
        project_kernel, "project", [of((ROWS, WIDE), jnp.int16), of((1, count), F32)], 20,
        own_exp, pair, exchange(pair, CLS), permuter, row_half[:, None], half_sets[None, :],
        bins_row, centred, far=(7,), scratch=[images, pltpu.SemaphoreType.DMA((PARTS,))],
    )
    (second,) = call(
        plane_kernel, "plane", [of((4, 16, WIDE), jnp.int16)], 8,
        exchange(packed.reshape(16, 16, WIDE), PLANE),
    )
    keep, stats = call(
        shell_kernel, "shells", [of((2, COLS), F32), of((16, 8, PART + ORIENT), F32)], 8,
        where, exchange(second, "zh"), squares, shell_match, scalars=1,
    )
    (half_maps,) = call(
        finish_kernel, "finish", [of((1, 4, COLS), F32)], 8,
        where, exchange(stats, PLANE), keep, shell_match, scalars=1,
    )
    return (half_maps, evidence.reshape(count))


def solution(mesh):
    split = Mesh(mesh.devices.reshape(4, 2, 4, 4, 4), AXES)
    placed = (
        P(PTCL, None),
        P(CLS, PTCL, None),
        P(),
        P(PTCL),
        P(PTCL),
        P(PTCL, CLS),
        P(),
    )
    return jax.shard_map(
        on_device,
        mesh=split,
        in_specs=placed,
        out_specs=(P(CLS, PTCL, None), P(PTCL)),
        check_vma=False,
    )
```

```python
import jax
import jax.numpy as jnp
from jax import lax
from jax.experimental import pallas as pl
from jax.experimental.pallas import tpu as pltpu
from jax.sharding import Mesh
from jax.sharding import PartitionSpec as P

PIXC = 1024
COLS = 2 * PIXC
ORIENT = 128
ROWS = 2 * ORIENT
NSHELL = 32
NBIN = 16
AXES = ("zl", "co", "y", "zh", "x")
CLS = ("zl", "co")
PTCL = ("y", "zh", "x")
PLANE = ("y", "x")
SIDE = 128
WIDE = COLS + SIDE
CODE = 32767.0
PARTS = 4
PART = COLS // PARTS
F32 = jnp.float32
BF16 = jnp.bfloat16


def ctf_table():
    bins = jnp.arange(NBIN, dtype=F32)
    defocus = (bins + 1.0) / NBIN
    radius = (jnp.arange(PIXC, dtype=F32) + 0.5) / PIXC
    phase = 0.3 + 2.5 * defocus[:, None] * radius[None, :]
    return jnp.sin(phase) + 0.1 * jnp.cos(phase)


def lookup_small(indices, values):
    count = values.shape[0]
    match = indices[:, None] == jnp.arange(count, dtype=jnp.int32)[None, :]
    return jnp.sum(jnp.where(match, values[None, :], 0.0), axis=1)


def exchange(blocks, axes):
    return lax.all_to_all(blocks, axes, split_axis=0, concat_axis=0, tiled=True)


def from_all(shard, axes, count):
    return exchange(jnp.broadcast_to(shard[None], (count,) + shard.shape), axes)


def row_maps():
    r = jnp.arange(ROWS, dtype=jnp.int32)
    j, swap, zh, x, y = r % 2, (r // 2) % 2, (r // 4) % 4, (r // 16) % 4, r // 64
    direction = 4 * (((y % 2) * 4 + zh) * 4 + x) + 2 * (y // 2) + j
    return direction, (swap + y // 2) % 2


def gathered_orients():
    r = jnp.arange(ORIENT, dtype=jnp.int32)
    j, zh, x, y = r % 2, (r // 2) % 4, (r // 8) % 4, r // 32
    return ((y * 4 + zh) * 4 + x) * 2 + j


def three_parts(table, axis):
    high = table.astype(BF16)
    rest = table - high.astype(F32)
    mid = rest.astype(BF16)
    low = (rest - mid.astype(F32)).astype(BF16)
    return jnp.concatenate([high, mid, low], axis=axis)


def table_parts(table):
    high = lax.reduce_precision(table, 8, 7)
    mid = lax.reduce_precision(table - high, 8, 7)
    low = table - high - mid
    return jnp.concatenate([high, mid, low], axis=0).astype(BF16)


def bin_match(bins, copies):
    row = lax.broadcasted_iota(jnp.int32, (copies * NBIN, bins.shape[1]), 0)
    return jnp.where(row % NBIN == bins, 1.0, 0.0).astype(BF16)


def contract(left, right, dims):
    return lax.dot_general(left, right, (dims, ((), ())), preferred_element_type=F32)


def encode(values):
    size = jnp.abs(values)
    top = jnp.max(size, axis=1, keepdims=True)
    expo = jnp.floor(jnp.log2(jnp.maximum(top, 1e-30))) + 1.0
    root = lax.rsqrt(lax.rsqrt(jnp.maximum(size * jnp.exp2(-expo), 1e-36)))
    code = root * CODE + 0.5
    codes = jnp.where(values < 0.0, -code, code).astype(jnp.int32).astype(jnp.int16)
    return codes, expo


def side_block(sums, expos, unit):
    fixed = jnp.floor(sums * unit + 0.5).astype(jnp.int32)
    high = lax.shift_right_arithmetic(fixed, 16)
    low = (fixed & 65535) - 32768
    shape = (sums.shape[0], SIDE - 2 * NBIN)
    lane = lax.broadcasted_iota(jnp.int32, shape, 1)
    tail = jnp.zeros(shape, F32)
    for part, expo in enumerate(expos):
        tail = jnp.where(lane == part, expo, tail)
    return jnp.concatenate([high, low, tail.astype(jnp.int32)], axis=1).astype(jnp.int16)


def decode_part(ref, count, part):
    cols = slice(part * PART, (part + 1) * PART)
    at = COLS + 2 * NBIN + part
    data = jnp.zeros((ref.shape[1], PART), F32)
    for source in range(count):
        expo = ref[source, :, COLS:].astype(jnp.int32)[:, at - COLS : at - COLS + 1]
        scale = jnp.exp2(expo.astype(F32)) * (1.0 / CODE**4)
        root = ref[source, :, cols].astype(jnp.int32).astype(F32)
        data = data + root * jnp.abs(root) * (root * root) * scale
    return data


def decode_bins(ref, count, unit):
    sums = jnp.zeros((ref.shape[1], NBIN), F32)
    for source in range(count):
        side = ref[source, :, COLS:].astype(jnp.int32)
        fixed = side[:, :NBIN] * 65536 + (side[:, NBIN : 2 * NBIN] + 32768)
        sums = sums + fixed.astype(F32) * (1.0 / unit)
    return sums


def image_kernel(
    x_ref, bins_ref, table_ref, noise_ref, centred_near, centred_far, weighted_near, weighted_far,
    x_buf, centred_buf, weighted_buf, sems
):
    noise = noise_ref[...]
    steps = PARTS
    step = x_buf.shape[0] // steps
    edge = weighted_near.shape[0] // step

    def read(i):
        rows = pl.ds(i * step, step)
        return pltpu.make_async_copy(x_ref.at[rows], x_buf.at[rows], sems.at[0, i])

    def write(i, k):
        if k == 1:
            rows, buf, out = pl.ds(i * step, step), centred_buf, centred_far
        else:
            rows, buf, out = pl.ds((i - edge) * step, step), weighted_buf, weighted_far
        return pltpu.make_async_copy(buf.at[rows], out.at[rows], sems.at[k, i])

    def chunk(i, keep):
        rows = pl.ds(pl.multiple_of(i * step, step), step)
        match = bin_match(bins_ref[:, rows], 3)
        contrast = contract(match, table_ref[...], ((0,), (0,)))
        read(i).wait()
        for part in range(2):
            cols = slice(part * PIXC, (part + 1) * PIXC)
            product = x_buf[rows, cols].astype(F32) * contrast
            rounded = product.astype(BF16)
            if part == 0:
                centred_near[rows, :] = rounded[:, :PART]
                centred_buf[rows, : PIXC - PART] = rounded[:, PART:]
            else:
                centred_buf[rows, PIXC - PART :] = rounded
            scaled = (product * noise).astype(BF16)
            if keep:
                weighted_near[rows, cols] = scaled
            else:
                weighted_buf[pl.ds(pl.multiple_of((i - edge) * step, step), step), cols] = scaled
        write(i, 1).start()
        if not keep:
            write(i, 2).start()

    for i in range(steps):
        read(i).start()
    lax.fori_loop(0, edge, lambda i, c: (chunk(i, True), c)[1], 0)
    lax.fori_loop(edge, steps, lambda i, c: (chunk(i, False), c)[1], 0)
    for i in range(steps):
        write(i, 1).wait()
        if i >= edge:
            write(i, 2).wait()


def score_kernel(
    panel_ref, power_ref, bins_ref, mask_ref, near_ref, far_ref, exp_ref, pair_ref, far_buf, sems
):
    step = near_ref.shape[0]

    def read(i):
        rows = pl.ds(i * step, step)
        return pltpu.make_async_copy(far_ref.at[rows], far_buf.at[rows], sems.at[i])

    for i in range(PARTS - 1):
        read(i).start()
    real = panel_ref[:, :PIXC].astype(F32)
    imag = panel_ref[:, PIXC:].astype(F32)
    panel_power = (real * real + imag * imag).astype(BF16)
    norm = three_parts(contract(panel_power, power_ref[...], ((1,), (1,))), 1)

    def chunk(at, weighted):
        rows = pl.ds(at, step)
        norm_part = contract(norm, bin_match(bins_ref[:, rows], 3), ((1,), (0,)))
        direct = contract(panel_ref[...], weighted, ((1,), (1,)))
        scores = direct - 0.5 * norm_part
        allowed = mask_ref[:, rows] > 0
        masked = jnp.where(allowed, scores, -1e30)
        peak = jnp.max(masked, axis=0, keepdims=True)
        weights = jnp.where(allowed, jnp.exp(masked - peak), 0.0)
        exp_ref[:, rows] = weights
        total = jnp.sum(weights, axis=0, keepdims=True)
        pair = jnp.concatenate([peak, total], axis=0)
        for other in range(8):
            pair_ref[other, :, rows] = pair

    def far_chunk(i, carry):
        read(i).wait()
        start = pl.multiple_of(i * step, step)
        chunk(pl.multiple_of(start + step, step), far_buf[pl.ds(start, step), :])
        return carry

    chunk(0, near_ref[...])
    lax.fori_loop(0, PARTS - 1, far_chunk, 0)


def split_kernel(exp_ref, permuter_ref, row_half_ref, half_ref, split_ref):
    parts = three_parts(exp_ref[...], 0)
    permuter = permuter_ref[...]
    rows = contract(jnp.concatenate([permuter] * 3, axis=1), parts, ((1,), (0,)))
    split_ref[...] = jnp.where(row_half_ref[...] == half_ref[...], rows, 0.0)


def project_kernel(
    split_ref, own_ref, both_ref, bins_ref, near_ref, far_ref, packed_ref, evidence_ref, far_buf,
    sems
):
    spans = [slice(part * PART, (part + 1) * PART) for part in range(PARTS)]
    reads = [
        pltpu.make_async_copy(far_ref.at[:, cols], far_buf.at[:, cols], sems.at[part])
        for part, cols in enumerate(spans[:-1])
    ]
    for read in reads:
        read.start()
    own_peak = own_ref[0, 0:1, :]
    peak = both_ref[0, 0:1, :]
    for c in range(1, both_ref.shape[0]):
        peak = jnp.maximum(peak, both_ref[c, 0:1, :])
    total = jnp.zeros_like(peak)
    for c in range(both_ref.shape[0]):
        total = total + both_ref[c, 1:2, :] * jnp.exp(both_ref[c, 0:1, :] - peak)
    evidence_ref[...] = peak + jnp.log(total)
    post = (split_ref[...] * (jnp.exp(own_peak - peak) / total)).astype(BF16)
    sums = contract(post, bin_match(bins_ref[...], 1), ((1,), (1,)))
    expos = []
    for part, cols in enumerate(spans):
        if part == 0:
            centred = near_ref[...]
        else:
            reads[part - 1].wait()
            centred = far_buf[:, spans[part - 1]]
        codes, expo = encode(contract(post, centred, ((1,), (0,))))
        expos.append(expo)
        packed_ref[:, cols] = codes
    packed_ref[:, COLS:] = side_block(sums, expos, 2.0**20)


def plane_kernel(came_ref, packed_ref):
    expos = []
    for part in range(PARTS):
        codes, expo = encode(decode_part(came_ref, 16, part))
        expos.append(expo)
        for other in range(4):
            packed_ref[other, :, part * PART : (part + 1) * PART] = codes
    side = side_block(decode_bins(came_ref, 16, 2.0**20), expos, 2.0**16)
    for other in range(4):
        packed_ref[other, :, COLS:] = side


def shell_kernel(where_ref, came_ref, squares_ref, shells_ref, keep_ref, stats_ref):
    upper = where_ref[0]
    zh = where_ref[1]
    data = jnp.concatenate([decode_part(came_ref, 4, part) for part in range(PARTS)], axis=1)
    sums = decode_bins(came_ref, 4, 2.0**16)
    cross = jnp.zeros((1, COLS), F32)
    first = jnp.zeros((1, COLS), F32)
    second = jnp.zeros((1, COLS), F32)
    own_data = jnp.zeros((4, COLS), F32)
    own_sums = jnp.zeros((4, NBIN), F32)
    for z in range(4):
        rows = data[4 * z : 4 * z + 4]
        own_data = jnp.where(zh == z, rows, own_data)
        own_sums = jnp.where(zh == z, sums[4 * z : 4 * z + 4], own_sums)
        cross = cross + jnp.sum(rows[:2] * rows[2:], axis=0, keepdims=True)
        first = first + jnp.sum(rows[:2] * rows[:2], axis=0, keepdims=True)
        second = second + jnp.sum(rows[2:] * rows[2:], axis=0, keepdims=True)
    power0 = jnp.where(upper == 0, first, second)
    power1 = jnp.where(upper == 0, second, first)
    three = jnp.concatenate([cross, power0, power1, jnp.zeros((5, COLS), F32)], axis=0)
    folded = three[:, :PIXC] + three[:, PIXC:]
    by_shell = contract(three_parts(folded, 0), shells_ref[...], ((1,), (0,)))
    by_shell = by_shell[0:8] + by_shell[8:16] + by_shell[16:24]
    squares = squares_ref[...]
    weight = contract(
        three_parts(own_sums, 1), jnp.concatenate([squares] * 3, axis=0), ((1,), (0,))
    )
    whole = own_data / (jnp.concatenate([weight, weight], axis=1) + 1.0)
    keep_ref[...] = whole[:2]
    for other in range(16):
        stats_ref[other, :, PART:] = by_shell
    for part in range(PARTS):
        piece = whole[2:, part * PART : (part + 1) * PART]
        for other in range(16):
            stats_ref[other, 2 * part : 2 * part + 2, :PART] = piece


def finish_kernel(where_ref, came_ref, keep_ref, spread_ref, out_ref):
    totals = came_ref[0, :, PART:]
    for source in range(1, 16):
        totals = totals + came_ref[source, :, PART:]
    fsc = totals[0:1] / jnp.sqrt(totals[1:2] * totals[2:3] + 1e-06)
    half = jnp.broadcast_to((1.0 + fsc) / 2.0, (8, ORIENT))
    factor = contract(three_parts(half, 0), spread_ref[...], ((1,), (0,)))
    factor = factor[0:1] + factor[8:9] + factor[16:17]
    low = where_ref[0] == 0
    partner = came_ref[where_ref[2]]
    for part in range(PARTS):
        cols = slice(part * PART, (part + 1) * PART)
        start = (part * PART) % PIXC
        scale = factor[:, start : start + PART]
        keep = keep_ref[:, cols] * scale
        got = partner[2 * part : 2 * part + 2, :PART] * scale
        out_ref[0, 0:2, cols] = jnp.where(low, keep, got)
        out_ref[0, 2:4, cols] = jnp.where(low, got, keep)


def call(kernel, name, out_shape, mega, *args, scalars=0, far=(), far_out=(), scratch=()):
    def space(i, hbm):
        if i < 0:
            return pl.BlockSpec(memory_space=pltpu.MemorySpace.SMEM)
        return pl.BlockSpec(
            memory_space=pltpu.MemorySpace.HBM if i in hbm else pltpu.MemorySpace.VMEM
        )

    args = [
        pltpu.with_memory_space_constraint(arg, pltpu.MemorySpace.HBM) if i in far else arg
        for i, arg in enumerate(args)
    ]
    return pl.pallas_call(
        kernel,
        in_specs=[space(i if i >= scalars else -1, far) for i in range(len(args))],
        out_specs=[space(i, far_out) for i in range(len(out_shape))],
        out_shape=out_shape,
        scratch_shapes=scratch,
        compiler_params=pltpu.CompilerParams(vmem_limit_bytes=mega * 1024 * 1024),
        name=name,
    )(*args)


def on_device(particles, panels, sigma2, defocus_bins, half_sets, prior_mask, orient_ids):
    count = particles.shape[0]
    of = jax.ShapeDtypeStruct

    shells = jnp.arange(PIXC, dtype=jnp.int32) * NSHELL // PIXC
    inverse_noise = lookup_small(shells, 1.0 / sigma2)
    table = ctf_table()
    power = (table * table * inverse_noise[None, :]).astype(BF16)
    squares = (table * table).astype(BF16)
    lanes = jnp.arange(ORIENT, dtype=jnp.int32)
    shell_match = (shells[:, None] == lanes[None, :]).astype(BF16)
    shell_spread = (lanes[:, None] == shells[None, :]).astype(BF16)
    y, zh, x = lax.axis_index("y"), lax.axis_index("zh"), lax.axis_index("x")
    where = jnp.stack([y // 2, zh, (y ^ 2) * 4 + x]).astype(jnp.int32)

    direction, row_half = row_maps()
    match = gathered_orients()[:, None] == jnp.arange(ORIENT, dtype=jnp.int32)[None, :]
    select = jnp.sum(jnp.where(match, orient_ids[None, :], 0), axis=1)

    near, far = pltpu.MemorySpace.VMEM, pltpu.MemorySpace.HBM
    first, rest = count // PARTS, count - count // PARTS
    by_zh, bins_row, parts, noise_row, power, squares, select = lax.optimization_barrier(
        (
            from_all(panels[0], "zh", 4), defocus_bins[None, :], table_parts(table),
            inverse_noise[None, :], power, squares, select,
        )
    )
    permuter = (direction[:, None] == select[None, :]).astype(BF16)
    centred_near, centred_far, weighted_near, weighted_far = call(
        image_kernel, "images",
        [
            near((count, PART), BF16), far((count, COLS - PART), BF16),
            near((first, COLS), BF16), far((rest, COLS), BF16),
        ],
        24, particles, bins_row, parts, noise_row,
        far=(0,), far_out=(1, 3),
        scratch=[
            near((count, COLS), BF16), near((count, COLS - PART), BF16), near((rest, COLS), BF16),
            pltpu.SemaphoreType.DMA((3, PARTS)),
        ],
    )
    piece = from_all(by_zh.reshape(8, COLS), PLANE, 16).reshape(ORIENT, COLS)

    own_exp, pair = call(
        score_kernel, "scores", [of((ORIENT, count), F32), of((8, 2, count), F32)], 14,
        piece, power, bins_row, prior_mask.reshape(1, count), weighted_near, weighted_far,
        far=(5,), scratch=[near((rest, COLS), BF16), pltpu.SemaphoreType.DMA((PARTS,))],
    )
    (split,) = call(
        split_kernel, "split", [of((ROWS, count), F32)], 8,
        own_exp, permuter, row_half[:, None], half_sets[None, :],
    )
    packed, evidence = call(
        project_kernel, "project", [of((ROWS, WIDE), jnp.int16), of((1, count), F32)], 20,
        split, pair, exchange(pair, CLS), bins_row, centred_near, centred_far, far=(5,),
        scratch=[near((count, COLS - PART), BF16), pltpu.SemaphoreType.DMA((PARTS,))],
    )
    (second,) = call(
        plane_kernel, "plane", [of((4, 16, WIDE), jnp.int16)], 8,
        exchange(packed.reshape(16, 16, WIDE), PLANE),
    )
    keep, stats = call(
        shell_kernel, "shells", [of((2, COLS), F32), of((16, 8, PART + ORIENT), F32)], 8,
        where, exchange(second, "zh"), squares, shell_match, scalars=1,
    )
    (half_maps,) = call(
        finish_kernel, "finish", [of((1, 4, COLS), F32)], 8,
        where, exchange(stats, PLANE), keep, shell_spread, scalars=1,
    )
    return (half_maps, evidence.reshape(count))


def solution(mesh):
    split = Mesh(mesh.devices.reshape(4, 2, 4, 4, 4), AXES)
    placed = (
        P(PTCL, None),
        P(CLS, PTCL, None),
        P(),
        P(PTCL),
        P(PTCL),
        P(PTCL, CLS),
        P(),
    )
    return jax.shard_map(
        on_device,
        mesh=split,
        in_specs=placed,
        out_specs=(P(CLS, PTCL, None), P(PTCL)),
        check_vma=False,
    )
```

```python
import jax
import jax.numpy as jnp
from jax import lax
from jax.experimental import pallas as pl
from jax.experimental.pallas import tpu as pltpu
from jax.sharding import Mesh
from jax.sharding import PartitionSpec as P

PIXC = 1024
COLS = 2 * PIXC
ORIENT = 128
ROWS = 2 * ORIENT
NSHELL = 32
NBIN = 16
AXES = ("zl", "co", "y", "zh", "x")
CLS = ("zl", "co")
PTCL = ("y", "zh", "x")
PLANE = ("y", "x")
SIDE = 128
WIDE = COLS + SIDE
CODE = 32767.0
PARTS = 4
PART = COLS // PARTS
F32 = jnp.float32
BF16 = jnp.bfloat16


def ctf_table():
    bins = jnp.arange(NBIN, dtype=F32)
    defocus = (bins + 1.0) / NBIN
    radius = (jnp.arange(PIXC, dtype=F32) + 0.5) / PIXC
    phase = 0.3 + 2.5 * defocus[:, None] * radius[None, :]
    return jnp.sin(phase) + 0.1 * jnp.cos(phase)


def lookup_small(indices, values):
    count = values.shape[0]
    match = indices[:, None] == jnp.arange(count, dtype=jnp.int32)[None, :]
    return jnp.sum(jnp.where(match, values[None, :], 0.0), axis=1)


def exchange(blocks, axes):
    return lax.all_to_all(blocks, axes, split_axis=0, concat_axis=0, tiled=True)


def from_all(shard, axes, count):
    return exchange(jnp.broadcast_to(shard[None], (count,) + shard.shape), axes)


def row_maps():
    r = jnp.arange(ROWS, dtype=jnp.int32)
    j, swap, zh, x, y = r % 2, (r // 2) % 2, (r // 4) % 4, (r // 16) % 4, r // 64
    direction = 4 * (((y % 2) * 4 + zh) * 4 + x) + 2 * (y // 2) + j
    return direction, (swap + y // 2) % 2


def gathered_orients():
    r = jnp.arange(ORIENT, dtype=jnp.int32)
    j, zh, x, y = r % 2, (r // 2) % 4, (r // 8) % 4, r // 32
    return ((y * 4 + zh) * 4 + x) * 2 + j


def three_parts(table, axis):
    high = table.astype(BF16)
    rest = table - high.astype(F32)
    mid = rest.astype(BF16)
    low = (rest - mid.astype(F32)).astype(BF16)
    return jnp.concatenate([high, mid, low], axis=axis)


def table_parts(table):
    high = lax.reduce_precision(table, 8, 7)
    mid = lax.reduce_precision(table - high, 8, 7)
    low = table - high - mid
    return jnp.concatenate([high, mid, low], axis=0).astype(BF16)


def bin_match(bins, copies):
    row = lax.broadcasted_iota(jnp.int32, (copies * NBIN, bins.shape[1]), 0)
    return jnp.where(row % NBIN == bins, 1.0, 0.0).astype(BF16)


def contract(left, right, dims):
    return lax.dot_general(left, right, (dims, ((), ())), preferred_element_type=F32)


def encode(values):
    size = jnp.abs(values)
    top = jnp.max(size, axis=1, keepdims=True)
    expo = jnp.floor(jnp.log2(jnp.maximum(top, 1e-30))) + 1.0
    root = lax.rsqrt(lax.rsqrt(jnp.maximum(size * jnp.exp2(-expo), 1e-36)))
    code = root * CODE + 0.5
    codes = jnp.where(values < 0.0, -code, code).astype(jnp.int32).astype(jnp.int16)
    return codes, expo


def side_block(sums, expos, unit):
    fixed = jnp.floor(sums * unit + 0.5).astype(jnp.int32)
    high = lax.shift_right_arithmetic(fixed, 16)
    low = (fixed & 65535) - 32768
    shape = (sums.shape[0], SIDE - 2 * NBIN)
    lane = lax.broadcasted_iota(jnp.int32, shape, 1)
    tail = jnp.zeros(shape, F32)
    for part, expo in enumerate(expos):
        tail = jnp.where(lane == part, expo, tail)
    return jnp.concatenate([high, low, tail.astype(jnp.int32)], axis=1).astype(jnp.int16)


def decode_part(ref, count, part):
    cols = slice(part * PART, (part + 1) * PART)
    at = COLS + 2 * NBIN + part
    data = jnp.zeros((ref.shape[1], PART), F32)
    for source in range(count):
        expo = ref[source, :, COLS:].astype(jnp.int32)[:, at - COLS : at - COLS + 1]
        scale = jnp.exp2(expo.astype(F32)) * (1.0 / CODE**4)
        root = ref[source, :, cols].astype(jnp.int32).astype(F32)
        data = data + root * jnp.abs(root) * (root * root) * scale
    return data


def decode_bins(ref, count, unit):
    sums = jnp.zeros((ref.shape[1], NBIN), F32)
    for source in range(count):
        side = ref[source, :, COLS:].astype(jnp.int32)
        fixed = side[:, :NBIN] * 65536 + (side[:, NBIN : 2 * NBIN] + 32768)
        sums = sums + fixed.astype(F32) * (1.0 / unit)
    return sums


def image_kernel(
    x_ref, bins_ref, table_ref, noise_ref, centred_near, centred_far, weighted_near, weighted_far,
    x_buf, centred_buf, weighted_buf, sems
):
    noise = noise_ref[...]
    steps = PARTS
    step = x_buf.shape[0] // steps
    edge = weighted_near.shape[0] // step

    def read(i):
        rows = pl.ds(i * step, step)
        return pltpu.make_async_copy(x_ref.at[rows], x_buf.at[rows], sems.at[0, i])

    def write(i, k):
        if k == 1:
            rows, buf, out = pl.ds(i * step, step), centred_buf, centred_far
        else:
            rows, buf, out = pl.ds((i - edge) * step, step), weighted_buf, weighted_far
        return pltpu.make_async_copy(buf.at[rows], out.at[rows], sems.at[k, i])

    def chunk(i, keep):
        rows = pl.ds(pl.multiple_of(i * step, step), step)
        match = bin_match(bins_ref[:, rows], 3)
        contrast = contract(match, table_ref[...], ((0,), (0,)))
        read(i).wait()
        for part in range(2):
            cols = slice(part * PIXC, (part + 1) * PIXC)
            product = x_buf[rows, cols].astype(F32) * contrast
            rounded = product.astype(BF16)
            if part == 0:
                centred_near[rows, :] = rounded[:, :PART]
                centred_buf[rows, : PIXC - PART] = rounded[:, PART:]
            else:
                centred_buf[rows, PIXC - PART :] = rounded
            scaled = (product * noise).astype(BF16)
            if keep:
                weighted_near[rows, cols] = scaled
            else:
                weighted_buf[pl.ds(pl.multiple_of((i - edge) * step, step), step), cols] = scaled
        write(i, 1).start()
        if not keep:
            write(i, 2).start()

    for i in range(steps):
        read(i).start()
    lax.fori_loop(0, edge, lambda i, c: (chunk(i, True), c)[1], 0)
    lax.fori_loop(edge, steps, lambda i, c: (chunk(i, False), c)[1], 0)
    for i in range(steps):
        write(i, 1).wait()
        if i >= edge:
            write(i, 2).wait()


def score_kernel(
    panel_ref, power_ref, bins_ref, mask_ref, near_ref, far_ref, exp_ref, pair_ref, far_buf, sems
):
    step = near_ref.shape[0]

    def read(i):
        rows = pl.ds(i * step, step)
        return pltpu.make_async_copy(far_ref.at[rows], far_buf.at[rows], sems.at[i])

    for i in range(PARTS - 1):
        read(i).start()
    real = panel_ref[:, :PIXC].astype(F32)
    imag = panel_ref[:, PIXC:].astype(F32)
    panel_power = (real * real + imag * imag).astype(BF16)
    norm = three_parts(contract(panel_power, power_ref[...], ((1,), (1,))), 1)

    def chunk(at, weighted):
        rows = pl.ds(at, step)
        norm_part = contract(norm, bin_match(bins_ref[:, rows], 3), ((1,), (0,)))
        direct = contract(panel_ref[...], weighted, ((1,), (1,)))
        scores = direct - 0.5 * norm_part
        allowed = mask_ref[:, rows] > 0
        masked = jnp.where(allowed, scores, -1e30)
        peak = jnp.max(masked, axis=0, keepdims=True)
        weights = jnp.where(allowed, jnp.exp(masked - peak), 0.0)
        exp_ref[:, rows] = weights
        total = jnp.sum(weights, axis=0, keepdims=True)
        pair = jnp.concatenate([peak, total], axis=0)
        for other in range(8):
            pair_ref[other, :, rows] = pair

    def far_chunk(i, carry):
        read(i).wait()
        start = pl.multiple_of(i * step, step)
        chunk(pl.multiple_of(start + step, step), far_buf[pl.ds(start, step), :])
        return carry

    chunk(0, near_ref[...])
    lax.fori_loop(0, PARTS - 1, far_chunk, 0)


def project_kernel(
    exp_ref, own_ref, both_ref, permuter_ref, row_half_ref, half_ref, bins_ref, near_ref, far_ref,
    packed_ref, evidence_ref, far_buf, evidence_buf, sems
):
    spans = [slice(part * PART, (part + 1) * PART) for part in range(PARTS)]
    reads = [
        pltpu.make_async_copy(far_ref.at[:, cols], far_buf.at[:, cols], sems.at[part])
        for part, cols in enumerate(spans[:-1])
    ]
    for read in reads:
        read.start()
    own_peak = own_ref[0, 0:1, :]
    peaks = both_ref[:, 0, :]
    peak = jnp.max(peaks, axis=0, keepdims=True)
    total = jnp.sum(both_ref[:, 1, :] * jnp.exp(peaks - peak), axis=0, keepdims=True)
    evidence_buf[...] = peak + jnp.log(total)
    evidence = pltpu.make_async_copy(evidence_buf, evidence_ref, sems.at[PARTS - 1])
    evidence.start()
    posterior = (exp_ref[...] * (jnp.exp(own_peak - peak) / total)).astype(BF16)
    by_direction = contract(permuter_ref[...], posterior, ((1,), (0,)))
    kept = row_half_ref[...] == half_ref[...]
    post = jnp.where(kept, by_direction, 0.0).astype(BF16)
    sums = contract(post, bin_match(bins_ref[...], 1), ((1,), (1,)))
    expos = []
    for part, cols in enumerate(spans):
        if part == 0:
            centred = near_ref[...]
        else:
            reads[part - 1].wait()
            centred = far_buf[:, spans[part - 1]]
        codes, expo = encode(contract(post, centred, ((1,), (0,))))
        expos.append(expo)
        packed_ref[:, cols] = codes
    packed_ref[:, COLS:] = side_block(sums, expos, 2.0**20)
    evidence.wait()


def plane_kernel(came_ref, packed_ref):
    expos = []
    for part in range(PARTS):
        codes, expo = encode(decode_part(came_ref, 16, part))
        expos.append(expo)
        for other in range(4):
            packed_ref[other, :, part * PART : (part + 1) * PART] = codes
    side = side_block(decode_bins(came_ref, 16, 2.0**20), expos, 2.0**16)
    for other in range(4):
        packed_ref[other, :, COLS:] = side


def shell_kernel(where_ref, came_ref, squares_ref, shells_ref, keep_ref, stats_ref):
    upper = where_ref[0]
    zh = where_ref[1]
    data = jnp.concatenate([decode_part(came_ref, 4, part) for part in range(PARTS)], axis=1)
    sums = decode_bins(came_ref, 4, 2.0**16)
    cross = jnp.zeros((1, COLS), F32)
    first = jnp.zeros((1, COLS), F32)
    second = jnp.zeros((1, COLS), F32)
    own_data = jnp.zeros((4, COLS), F32)
    own_sums = jnp.zeros((4, NBIN), F32)
    for z in range(4):
        rows = data[4 * z : 4 * z + 4]
        own_data = jnp.where(zh == z, rows, own_data)
        own_sums = jnp.where(zh == z, sums[4 * z : 4 * z + 4], own_sums)
        cross = cross + jnp.sum(rows[:2] * rows[2:], axis=0, keepdims=True)
        first = first + jnp.sum(rows[:2] * rows[:2], axis=0, keepdims=True)
        second = second + jnp.sum(rows[2:] * rows[2:], axis=0, keepdims=True)
    power0 = jnp.where(upper == 0, first, second)
    power1 = jnp.where(upper == 0, second, first)
    three = jnp.concatenate([cross, power0, power1, jnp.zeros((5, COLS), F32)], axis=0)
    folded = three[:, :PIXC] + three[:, PIXC:]
    by_shell = contract(three_parts(folded, 0), shells_ref[...], ((1,), (0,)))
    by_shell = by_shell[0:8] + by_shell[8:16] + by_shell[16:24]
    squares = squares_ref[...]
    weight = contract(
        three_parts(own_sums, 1), jnp.concatenate([squares] * 3, axis=0), ((1,), (0,))
    )
    whole = own_data / (jnp.concatenate([weight, weight], axis=1) + 1.0)
    keep_ref[...] = whole[:2]
    for other in range(16):
        stats_ref[other, :, PART:] = by_shell
    for part in range(PARTS):
        piece = whole[2:, part * PART : (part + 1) * PART]
        for other in range(16):
            stats_ref[other, 2 * part : 2 * part + 2, :PART] = piece


def finish_kernel(where_ref, came_ref, keep_ref, spread_ref, out_ref):
    totals = came_ref[0, :, PART:]
    for source in range(1, 16):
        totals = totals + came_ref[source, :, PART:]
    fsc = totals[0:1] / jnp.sqrt(totals[1:2] * totals[2:3] + 1e-06)
    half = jnp.broadcast_to((1.0 + fsc) / 2.0, (8, ORIENT))
    factor = contract(three_parts(half, 0), spread_ref[...], ((1,), (0,)))
    factor = factor[0:1] + factor[8:9] + factor[16:17]
    low = where_ref[0] == 0
    partner = came_ref[where_ref[2]]
    for part in range(PARTS):
        cols = slice(part * PART, (part + 1) * PART)
        start = (part * PART) % PIXC
        scale = factor[:, start : start + PART]
        keep = keep_ref[:, cols] * scale
        got = partner[2 * part : 2 * part + 2, :PART] * scale
        out_ref[0, 0:2, cols] = jnp.where(low, keep, got)
        out_ref[0, 2:4, cols] = jnp.where(low, got, keep)


def call(kernel, name, out_shape, mega, *args, scalars=0, far=(), far_out=(), scratch=()):
    def space(i, hbm):
        if i < 0:
            return pl.BlockSpec(memory_space=pltpu.MemorySpace.SMEM)
        return pl.BlockSpec(
            memory_space=pltpu.MemorySpace.HBM if i in hbm else pltpu.MemorySpace.VMEM
        )

    args = [
        pltpu.with_memory_space_constraint(arg, pltpu.MemorySpace.HBM) if i in far else arg
        for i, arg in enumerate(args)
    ]
    return pl.pallas_call(
        kernel,
        in_specs=[space(i if i >= scalars else -1, far) for i in range(len(args))],
        out_specs=[space(i, far_out) for i in range(len(out_shape))],
        out_shape=out_shape,
        scratch_shapes=scratch,
        compiler_params=pltpu.CompilerParams(vmem_limit_bytes=mega * 1024 * 1024),
        name=name,
    )(*args)


def on_device(particles, panels, sigma2, defocus_bins, half_sets, prior_mask, orient_ids):
    count = particles.shape[0]
    of = jax.ShapeDtypeStruct

    shells = jnp.arange(PIXC, dtype=jnp.int32) * NSHELL // PIXC
    inverse_noise = lookup_small(shells, 1.0 / sigma2)
    table = ctf_table()
    power = (table * table * inverse_noise[None, :]).astype(BF16)
    squares = (table * table).astype(BF16)
    lanes = jnp.arange(ORIENT, dtype=jnp.int32)
    shell_match = (shells[:, None] == lanes[None, :]).astype(BF16)
    shell_spread = (lanes[:, None] == shells[None, :]).astype(BF16)
    y, zh, x = lax.axis_index("y"), lax.axis_index("zh"), lax.axis_index("x")
    where = jnp.stack([y // 2, zh, (y ^ 2) * 4 + x]).astype(jnp.int32)

    direction, row_half = row_maps()
    match = gathered_orients()[:, None] == jnp.arange(ORIENT, dtype=jnp.int32)[None, :]
    select = jnp.sum(jnp.where(match, orient_ids[None, :], 0), axis=1)

    near, far = pltpu.MemorySpace.VMEM, pltpu.MemorySpace.HBM
    first, rest = count // PARTS, count - count // PARTS
    permuter = (direction[:, None] == select[None, :]).astype(BF16)
    (
        by_zh, bins_row, parts, noise_row, power, squares, permuter, row_half, where, shell_match,
        shell_spread, half_row, mask_row,
    ) = lax.optimization_barrier(
        (
            from_all(panels[0], "zh", 4), defocus_bins[None, :], table_parts(table),
            inverse_noise[None, :], power, squares, permuter, row_half[:, None], where,
            shell_match, shell_spread, half_sets[None, :], prior_mask.reshape(1, count),
        )
    )
    centred_near, centred_far, weighted_near, weighted_far = call(
        image_kernel, "images",
        [
            near((count, PART), BF16), far((count, COLS - PART), BF16),
            near((first, COLS), BF16), far((rest, COLS), BF16),
        ],
        24, particles, bins_row, parts, noise_row,
        far=(0,), far_out=(1, 3),
        scratch=[
            near((count, COLS), BF16), near((count, COLS - PART), BF16), near((rest, COLS), BF16),
            pltpu.SemaphoreType.DMA((3, PARTS)),
        ],
    )
    piece = from_all(by_zh.reshape(8, COLS), PLANE, 16).reshape(ORIENT, COLS)

    own_exp, pair = call(
        score_kernel, "scores", [of((ORIENT, count), F32), of((8, 2, count), F32)], 14,
        piece, power, bins_row, mask_row, weighted_near, weighted_far,
        far=(5,), scratch=[near((rest, COLS), BF16), pltpu.SemaphoreType.DMA((PARTS,))],
    )
    packed, evidence = call(
        project_kernel, "project", [of((ROWS, WIDE), jnp.int16), of((1, count), F32)], 20,
        own_exp, pair, exchange(pair, CLS), permuter, row_half, half_row, bins_row,
        centred_near, centred_far, far=(8,), far_out=(1,),
        scratch=[
            near((count, COLS - PART), BF16), near((1, count), F32),
            pltpu.SemaphoreType.DMA((PARTS,)),
        ],
    )
    (second,) = call(
        plane_kernel, "plane", [of((4, 16, WIDE), jnp.int16)], 8,
        exchange(packed.reshape(16, 16, WIDE), PLANE),
    )
    keep, stats = call(
        shell_kernel, "shells", [of((2, COLS), F32), of((16, 8, PART + ORIENT), F32)], 8,
        where, exchange(second, "zh"), squares, shell_match, scalars=1,
    )
    (half_maps,) = call(
        finish_kernel, "finish", [of((1, 4, COLS), F32)], 8,
        where, exchange(stats, PLANE), keep, shell_spread, scalars=1,
    )
    return (half_maps, evidence.reshape(count))


def solution(mesh):
    split = Mesh(mesh.devices.reshape(4, 2, 4, 4, 4), AXES)
    placed = (
        P(PTCL, None),
        P(CLS, PTCL, None),
        P(),
        P(PTCL),
        P(PTCL),
        P(PTCL, CLS),
        P(),
    )
    return jax.shard_map(
        on_device,
        mesh=split,
        in_specs=placed,
        out_specs=(P(CLS, PTCL, None), P(PTCL)),
        check_vma=False,
    )
```

```python
import jax
import jax.numpy as jnp
from jax import lax
from jax.experimental import pallas as pl
from jax.experimental.pallas import tpu as pltpu
from jax.sharding import Mesh
from jax.sharding import PartitionSpec as P

PIXC = 1024
COLS = 2 * PIXC
ORIENT = 128
ROWS = 2 * ORIENT
NSHELL = 32
NBIN = 16
AXES = ("zl", "co", "y", "zh", "x")
CLS = ("zl", "co")
PTCL = ("y", "zh", "x")
PLANE = ("y", "x")
SIDE = 128
WIDE = COLS + SIDE
CODE = 32767.0
PARTS = 4
CHUNK = 256
PART = COLS // PARTS
F32 = jnp.float32
BF16 = jnp.bfloat16


def ctf_table():
    bins = jnp.arange(NBIN, dtype=F32)
    defocus = (bins + 1.0) / NBIN
    radius = (jnp.arange(PIXC, dtype=F32) + 0.5) / PIXC
    phase = 0.3 + 2.5 * defocus[:, None] * radius[None, :]
    return jnp.sin(phase) + 0.1 * jnp.cos(phase)


def lookup_small(indices, values):
    count = values.shape[0]
    match = indices[:, None] == jnp.arange(count, dtype=jnp.int32)[None, :]
    return jnp.sum(jnp.where(match, values[None, :], 0.0), axis=1)


def exchange(blocks, axes):
    return lax.all_to_all(blocks, axes, split_axis=0, concat_axis=0, tiled=True)


def from_all(shard, axes, count):
    return exchange(jnp.broadcast_to(shard[None], (count,) + shard.shape), axes)


def row_maps():
    r = jnp.arange(ROWS, dtype=jnp.int32)
    j, swap, zh, x, y = r % 2, (r // 2) % 2, (r // 4) % 4, (r // 16) % 4, r // 64
    direction = 4 * (((y % 2) * 4 + zh) * 4 + x) + 2 * (y // 2) + j
    return direction, (swap + y // 2) % 2


def gathered_orients():
    r = jnp.arange(ORIENT, dtype=jnp.int32)
    j, zh, x, y = r % 2, (r // 2) % 4, (r // 8) % 4, r // 32
    return ((y * 4 + zh) * 4 + x) * 2 + j


def three_parts(table, axis):
    high = table.astype(BF16)
    rest = table - high.astype(F32)
    mid = rest.astype(BF16)
    low = (rest - mid.astype(F32)).astype(BF16)
    return jnp.concatenate([high, mid, low], axis=axis)


def table_parts(table):
    high = lax.reduce_precision(table, 8, 7)
    mid = lax.reduce_precision(table - high, 8, 7)
    low = table - high - mid
    return jnp.concatenate([high, mid, low], axis=0).astype(BF16)


def bin_match(bins, copies):
    row = lax.broadcasted_iota(jnp.int32, (copies * NBIN, bins.shape[1]), 0)
    return jnp.where(row % NBIN == bins, 1.0, 0.0).astype(BF16)


def contract(left, right, dims):
    return lax.dot_general(left, right, (dims, ((), ())), preferred_element_type=F32)


def encode(values):
    size = jnp.abs(values)
    top = jnp.max(size, axis=1, keepdims=True)
    expo = jnp.floor(jnp.log2(jnp.maximum(top, 1e-30))) + 1.0
    root = lax.rsqrt(lax.rsqrt(jnp.maximum(size * jnp.exp2(-expo), 1e-36)))
    code = root * CODE + 0.5
    codes = jnp.where(values < 0.0, -code, code).astype(jnp.int32).astype(jnp.int16)
    return codes, expo


def side_block(sums, expos, unit):
    fixed = jnp.floor(sums * unit + 0.5).astype(jnp.int32)
    high = lax.shift_right_arithmetic(fixed, 16)
    low = (fixed & 65535) - 32768
    shape = (sums.shape[0], SIDE - 2 * NBIN)
    lane = lax.broadcasted_iota(jnp.int32, shape, 1)
    tail = jnp.zeros(shape, F32)
    for part, expo in enumerate(expos):
        tail = jnp.where(lane == part, expo, tail)
    return jnp.concatenate([high, low, tail.astype(jnp.int32)], axis=1).astype(jnp.int16)


def decode_part(ref, count, part):
    cols = slice(part * PART, (part + 1) * PART)
    at = COLS + 2 * NBIN + part
    data = jnp.zeros((ref.shape[1], PART), F32)
    for source in range(count):
        expo = ref[source, :, COLS:].astype(jnp.int32)[:, at - COLS : at - COLS + 1]
        scale = jnp.exp2(expo.astype(F32)) * (1.0 / CODE**4)
        root = ref[source, :, cols].astype(jnp.int32).astype(F32)
        data = data + root * jnp.abs(root) * (root * root) * scale
    return data


def decode_bins(ref, count, unit):
    sums = jnp.zeros((ref.shape[1], NBIN), F32)
    for source in range(count):
        side = ref[source, :, COLS:].astype(jnp.int32)
        fixed = side[:, :NBIN] * 65536 + (side[:, NBIN : 2 * NBIN] + 32768)
        sums = sums + fixed.astype(F32) * (1.0 / unit)
    return sums


def image_kernel(
    x_ref, bins_ref, table_ref, noise_ref, centred_0, centred_1, centred_2, centred_3,
    weighted_near, weighted_far, x_buf, centred_buf, weighted_buf, sems
):
    noise = noise_ref[...]
    steps = PARTS
    step = x_buf.shape[0] // steps
    edge = weighted_near.shape[0] // step

    def read(i):
        rows = pl.ds(i * step, step)
        return pltpu.make_async_copy(x_ref.at[rows], x_buf.at[rows], sems.at[0, i])

    def write(i, k):
        if k < PARTS:
            rows, out = pl.ds(i * step, step), (centred_0, centred_1, centred_2, centred_3)[k]
            buf = centred_buf.at[:, k * PART : (k + 1) * PART]
        else:
            rows, buf, out = pl.ds((i - edge) * step, step), weighted_buf, weighted_far
        return pltpu.make_async_copy(buf.at[rows], out.at[rows], sems.at[k + 1, i])

    def chunk(i, keep):
        rows = pl.ds(pl.multiple_of(i * step, step), step)
        match = bin_match(bins_ref[:, rows], 3)
        contrast = contract(match, table_ref[...], ((0,), (0,)))
        read(i).wait()
        for part in range(2):
            cols = slice(part * PIXC, (part + 1) * PIXC)
            product = x_buf[rows, cols].astype(F32) * contrast
            centred_buf[rows, cols] = product.astype(BF16)
            scaled = (product * noise).astype(BF16)
            if keep:
                weighted_near[rows, cols] = scaled
            else:
                weighted_buf[pl.ds(pl.multiple_of((i - edge) * step, step), step), cols] = scaled
        for k in range(PARTS):
            write(i, k).start()
        if not keep:
            write(i, PARTS).start()

    for i in range(steps):
        read(i).start()
    lax.fori_loop(0, edge, lambda i, c: (chunk(i, True), c)[1], 0)
    lax.fori_loop(edge, steps, lambda i, c: (chunk(i, False), c)[1], 0)
    for i in range(steps):
        for k in range(PARTS):
            write(i, k).wait()
        if i >= edge:
            write(i, PARTS).wait()


def score_kernel(
    panel_ref, power_ref, bins_ref, mask_ref, near_ref, far_ref, exp_ref, pair_ref, far_buf, sems
):
    steps = far_ref.shape[0] // CHUNK

    def read(i):
        rows = pl.ds(i * CHUNK, CHUNK)
        return pltpu.make_async_copy(far_ref.at[rows], far_buf.at[rows], sems.at[i])

    for i in range(steps):
        read(i).start()
    real = panel_ref[:, :PIXC].astype(F32)
    imag = panel_ref[:, PIXC:].astype(F32)
    panel_power = (real * real + imag * imag).astype(BF16)
    norm = three_parts(contract(panel_power, power_ref[...], ((1,), (1,))), 1)

    def chunk(at, weighted):
        rows = pl.ds(at, CHUNK)
        norm_part = contract(norm, bin_match(bins_ref[:, rows], 3), ((1,), (0,)))
        direct = contract(panel_ref[...], weighted, ((1,), (1,)))
        scores = direct - 0.5 * norm_part
        allowed = mask_ref[:, rows] > 0
        masked = jnp.where(allowed, scores, -1e30)
        peak = jnp.max(masked, axis=0, keepdims=True)
        weights = jnp.where(allowed, jnp.exp(masked - peak), 0.0)
        exp_ref[:, rows] = weights
        total = jnp.sum(weights, axis=0, keepdims=True)
        pair = jnp.concatenate([peak, total], axis=0)
        for other in range(8):
            pair_ref[other, :, rows] = pair

    def near_chunk(i, carry):
        start = pl.multiple_of(i * CHUNK, CHUNK)
        chunk(start, near_ref[pl.ds(start, CHUNK), :])
        return carry

    def far_chunk(i, carry):
        read(i).wait()
        start = pl.multiple_of(i * CHUNK, CHUNK)
        chunk(pl.multiple_of(start + near_ref.shape[0], CHUNK), far_buf[pl.ds(start, CHUNK), :])
        return carry

    lax.fori_loop(0, near_ref.shape[0] // CHUNK, near_chunk, 0)
    lax.fori_loop(0, steps, far_chunk, 0)


def project_kernel(
    exp_ref, own_ref, both_ref, permuter_ref, row_half_ref, half_ref, bins_ref, *rest_refs
):
    packed_ref, evidence_ref, evidence_buf, sem = rest_refs[PARTS:]
    spans = [slice(part * PART, (part + 1) * PART) for part in range(PARTS)]
    own_peak = own_ref[0, 0:1, :]
    peaks = both_ref[:, 0, :]
    peak = jnp.max(peaks, axis=0, keepdims=True)
    total = jnp.sum(both_ref[:, 1, :] * jnp.exp(peaks - peak), axis=0, keepdims=True)
    evidence_buf[...] = peak + jnp.log(total)
    evidence = pltpu.make_async_copy(evidence_buf, evidence_ref, sem)
    evidence.start()
    posterior = (exp_ref[...] * (jnp.exp(own_peak - peak) / total)).astype(BF16)
    by_direction = contract(permuter_ref[...], posterior, ((1,), (0,)))
    kept = row_half_ref[...] == half_ref[...]
    post = jnp.where(kept, by_direction, 0.0).astype(BF16)
    sums = contract(post, bin_match(bins_ref[...], 1), ((1,), (1,)))
    expos = []
    for part, cols in enumerate(spans):
        codes, expo = encode(contract(post, rest_refs[part][...], ((1,), (0,))))
        expos.append(expo)
        packed_ref[:, cols] = codes
    packed_ref[:, COLS:] = side_block(sums, expos, 2.0**20)
    evidence.wait()


def plane_kernel(came_ref, packed_ref):
    expos = []
    for part in range(PARTS):
        codes, expo = encode(decode_part(came_ref, 16, part))
        expos.append(expo)
        for other in range(4):
            packed_ref[other, :, part * PART : (part + 1) * PART] = codes
    side = side_block(decode_bins(came_ref, 16, 2.0**20), expos, 2.0**16)
    for other in range(4):
        packed_ref[other, :, COLS:] = side


def shell_kernel(where_ref, came_ref, squares_ref, shells_ref, keep_ref, stats_ref):
    upper = where_ref[0:1, 0:1]
    zh = where_ref[1:2, 0:1]
    data = jnp.concatenate([decode_part(came_ref, 4, part) for part in range(PARTS)], axis=1)
    sums = decode_bins(came_ref, 4, 2.0**16)
    cross = jnp.zeros((1, COLS), F32)
    first = jnp.zeros((1, COLS), F32)
    second = jnp.zeros((1, COLS), F32)
    own_data = jnp.zeros((4, COLS), F32)
    own_sums = jnp.zeros((4, NBIN), F32)
    for z in range(4):
        rows = data[4 * z : 4 * z + 4]
        own_data = jnp.where(zh == z, rows, own_data)
        own_sums = jnp.where(zh == z, sums[4 * z : 4 * z + 4], own_sums)
        cross = cross + jnp.sum(rows[:2] * rows[2:], axis=0, keepdims=True)
        first = first + jnp.sum(rows[:2] * rows[:2], axis=0, keepdims=True)
        second = second + jnp.sum(rows[2:] * rows[2:], axis=0, keepdims=True)
    power0 = jnp.where(upper == 0, first, second)
    power1 = jnp.where(upper == 0, second, first)
    three = jnp.concatenate([cross, power0, power1, jnp.zeros((5, COLS), F32)], axis=0)
    folded = three[:, :PIXC] + three[:, PIXC:]
    by_shell = contract(three_parts(folded, 0), shells_ref[...], ((1,), (0,)))
    by_shell = by_shell[0:8] + by_shell[8:16] + by_shell[16:24]
    squares = squares_ref[...]
    weight = contract(
        three_parts(own_sums, 1), jnp.concatenate([squares] * 3, axis=0), ((1,), (0,))
    )
    whole = own_data / (jnp.concatenate([weight, weight], axis=1) + 1.0)
    keep_ref[...] = whole[:2]
    for other in range(16):
        stats_ref[other, :, PART:] = by_shell
    for part in range(PARTS):
        piece = whole[2:, part * PART : (part + 1) * PART]
        for other in range(16):
            stats_ref[other, 2 * part : 2 * part + 2, :PART] = piece


def finish_kernel(where_ref, came_ref, keep_ref, spread_ref, out_ref):
    totals = came_ref[0, :, PART:]
    for source in range(1, 16):
        totals = totals + came_ref[source, :, PART:]
    fsc = totals[0:1] / jnp.sqrt(totals[1:2] * totals[2:3] + 1e-06)
    half = jnp.broadcast_to((1.0 + fsc) / 2.0, (8, ORIENT))
    factor = contract(three_parts(half, 0), spread_ref[...], ((1,), (0,)))
    factor = factor[0:1] + factor[8:9] + factor[16:17]
    low = where_ref[0:1, 0:1] == 0
    source = where_ref[2:3, 0:1]
    partner = jnp.zeros((8, PART), F32)
    for other in range(16):
        partner = jnp.where(source == other, came_ref[other, :, :PART], partner)
    for part in range(PARTS):
        cols = slice(part * PART, (part + 1) * PART)
        start = (part * PART) % PIXC
        scale = factor[:, start : start + PART]
        keep = keep_ref[:, cols] * scale
        got = partner[2 * part : 2 * part + 2] * scale
        out_ref[0, 0:2, cols] = jnp.where(low, keep, got)
        out_ref[0, 2:4, cols] = jnp.where(low, got, keep)


def call(kernel, name, out_shape, mega, *args, scalars=0, far=(), far_out=(), scratch=()):
    def space(i, hbm):
        if i < 0:
            return pl.BlockSpec(memory_space=pltpu.MemorySpace.SMEM)
        return pl.BlockSpec(
            memory_space=pltpu.MemorySpace.HBM if i in hbm else pltpu.MemorySpace.VMEM
        )

    args = [
        pltpu.with_memory_space_constraint(arg, pltpu.MemorySpace.HBM) if i in far else arg
        for i, arg in enumerate(args)
    ]
    return pl.pallas_call(
        kernel,
        in_specs=[space(i if i >= scalars else -1, far) for i in range(len(args))],
        out_specs=[space(i, far_out) for i in range(len(out_shape))],
        out_shape=out_shape,
        scratch_shapes=scratch,
        compiler_params=pltpu.CompilerParams(vmem_limit_bytes=mega * 1024 * 1024),
        name=name,
    )(*args)


def on_device(particles, panels, sigma2, defocus_bins, half_sets, prior_mask, orient_ids):
    count = particles.shape[0]
    of = jax.ShapeDtypeStruct

    shells = jnp.arange(PIXC, dtype=jnp.int32) * NSHELL // PIXC
    inverse_noise = lookup_small(shells, 1.0 / sigma2)
    table = ctf_table()
    power = (table * table * inverse_noise[None, :]).astype(BF16)
    squares = (table * table).astype(BF16)
    lanes = jnp.arange(ORIENT, dtype=jnp.int32)
    shell_match = (shells[:, None] == lanes[None, :]).astype(BF16)
    shell_spread = (lanes[:, None] == shells[None, :]).astype(BF16)
    y, zh, x = lax.axis_index("y"), lax.axis_index("zh"), lax.axis_index("x")
    places = jnp.stack([y // 2, zh, (y ^ 2) * 4 + x]).astype(jnp.int32)
    where = jnp.broadcast_to(jnp.pad(places, (0, 5))[:, None], (8, ORIENT))

    direction, row_half = row_maps()
    match = gathered_orients()[:, None] == jnp.arange(ORIENT, dtype=jnp.int32)[None, :]
    select = jnp.sum(jnp.where(match, orient_ids[None, :], 0), axis=1)

    near, far = pltpu.MemorySpace.VMEM, pltpu.MemorySpace.HBM
    first, rest = 2 * CHUNK, count - 2 * CHUNK
    permuter = (direction[:, None] == select[None, :]).astype(BF16)
    (
        by_zh, bins_row, parts, noise_row, power, squares, permuter, row_half, where, shell_match,
        shell_spread, half_row, mask_row,
    ) = lax.optimization_barrier(
        (
            from_all(panels[0], "zh", 4), defocus_bins[None, :], table_parts(table),
            inverse_noise[None, :], power, squares, permuter, row_half[:, None], where,
            shell_match, shell_spread, half_sets[None, :], prior_mask.reshape(1, count),
        )
    )
    *centred, weighted_near, weighted_far = call(
        image_kernel, "images",
        [
            *[far((count, PART), BF16)] * PARTS,
            near((first, COLS), BF16), far((rest, COLS), BF16),
        ],
        24, particles, bins_row, parts, noise_row,
        far=(0,), far_out=(0, 1, 2, 3, 5),
        scratch=[
            near((count, COLS), BF16), near((count, COLS), BF16), near((rest, COLS), BF16),
            pltpu.SemaphoreType.DMA((PARTS + 2, PARTS)),
        ],
    )
    piece = from_all(by_zh.reshape(8, COLS), PLANE, 16).reshape(ORIENT, COLS)

    own_exp, pair = call(
        score_kernel, "scores", [of((ORIENT, count), F32), of((8, 2, count), F32)], 14,
        piece, power, bins_row, mask_row, weighted_near, weighted_far,
        far=(5,), scratch=[near((rest, COLS), BF16), pltpu.SemaphoreType.DMA((PARTS,))],
    )
    packed, evidence = call(
        project_kernel, "project", [of((ROWS, WIDE), jnp.int16), of((1, count), F32)], 20,
        own_exp, pair, exchange(pair, CLS), permuter, row_half, half_row, bins_row,
        *centred, far_out=(1,), scratch=[near((1, count), F32), pltpu.SemaphoreType.DMA],
    )
    (second,) = call(
        plane_kernel, "plane", [of((4, 16, WIDE), jnp.int16)], 8,
        exchange(packed.reshape(16, 16, WIDE), PLANE),
    )
    keep, stats = call(
        shell_kernel, "shells", [of((2, COLS), F32), of((16, 8, PART + ORIENT), F32)], 8,
        where, exchange(second, "zh"), squares, shell_match,
    )
    (half_maps,) = call(
        finish_kernel, "finish", [of((1, 4, COLS), F32)], 8,
        where, exchange(stats, PLANE), keep, shell_spread,
    )
    return (half_maps, evidence.reshape(count))


def solution(mesh):
    split = Mesh(mesh.devices.reshape(4, 2, 4, 4, 4), AXES)
    placed = (
        P(PTCL, None),
        P(CLS, PTCL, None),
        P(),
        P(PTCL),
        P(PTCL),
        P(PTCL, CLS),
        P(),
    )
    return jax.shard_map(
        on_device,
        mesh=split,
        in_specs=placed,
        out_specs=(P(CLS, PTCL, None), P(PTCL)),
        check_vma=False,
    )
```

```python
import jax
import jax.numpy as jnp
from jax import lax
from jax.experimental import pallas as pl
from jax.experimental.pallas import tpu as pltpu
from jax.sharding import Mesh
from jax.sharding import PartitionSpec as P

PIXC = 1024
COLS = 2 * PIXC
ORIENT = 128
ROWS = 2 * ORIENT
NSHELL = 32
NBIN = 16
AXES = ("zl", "co", "y", "zh", "x")
CLS = ("zl", "co")
PTCL = ("y", "zh", "x")
PLANE = ("y", "x")
SIDE = 128
WIDE = COLS + SIDE
CODE = 32767.0
PARTS = 4
CHUNK = 256
PART = COLS // PARTS
F32 = jnp.float32
BF16 = jnp.bfloat16


def ctf_table():
    bins = jnp.arange(NBIN, dtype=F32)
    defocus = (bins + 1.0) / NBIN
    radius = (jnp.arange(PIXC, dtype=F32) + 0.5) / PIXC
    phase = 0.3 + 2.5 * defocus[:, None] * radius[None, :]
    return jnp.sin(phase) + 0.1 * jnp.cos(phase)


def lookup_small(indices, values):
    count = values.shape[0]
    match = indices[:, None] == jnp.arange(count, dtype=jnp.int32)[None, :]
    return jnp.sum(jnp.where(match, values[None, :], 0.0), axis=1)


def exchange(blocks, axes):
    return lax.all_to_all(blocks, axes, split_axis=0, concat_axis=0, tiled=True)


def from_all(shard, axes, count):
    return exchange(jnp.broadcast_to(shard[None], (count,) + shard.shape), axes)


def row_direction(r):
    j, zh, x, y = r & 1, (r >> 2) & 3, (r >> 4) & 3, r >> 6
    return 4 * (((y & 1) * 4 + zh) * 4 + x) + 2 * (y >> 1) + j


def row_half(r):
    return ((r >> 1) & 1) ^ (r >> 7)


def gathered_orients():
    r = jnp.arange(ORIENT, dtype=jnp.int32)
    j, zh, x, y = r % 2, (r // 2) % 4, (r // 8) % 4, r // 32
    return ((y * 4 + zh) * 4 + x) * 2 + j


def three_parts(table, axis):
    high = table.astype(BF16)
    rest = table - high.astype(F32)
    mid = rest.astype(BF16)
    low = (rest - mid.astype(F32)).astype(BF16)
    return jnp.concatenate([high, mid, low], axis=axis)


def table_parts(table):
    high = lax.reduce_precision(table, 8, 7)
    mid = lax.reduce_precision(table - high, 8, 7)
    low = table - high - mid
    return jnp.concatenate([high, mid, low], axis=0).astype(BF16)


def bin_match(bins, copies):
    row = lax.broadcasted_iota(jnp.int32, (copies * NBIN, bins.shape[1]), 0)
    return jnp.where(row % NBIN == bins, 1.0, 0.0).astype(BF16)


def contract(left, right, dims):
    return lax.dot_general(left, right, (dims, ((), ())), preferred_element_type=F32)


def encode(values):
    size = jnp.abs(values)
    top = jnp.max(size, axis=1, keepdims=True)
    expo = jnp.floor(jnp.log2(jnp.maximum(top, 1e-37))) + 1.0
    root = lax.rsqrt(lax.rsqrt(jnp.maximum(size * jnp.exp2(-expo), 1e-36)))
    code = root * CODE + 0.5
    codes = jnp.where(values < 0.0, -code, code).astype(jnp.int32).astype(jnp.int16)
    return codes, expo


def side_block(sums, expos, unit):
    fixed = jnp.floor(sums * unit + 0.5).astype(jnp.int32)
    high = lax.shift_right_arithmetic(fixed, 16)
    low = (fixed & 65535) - 32768
    shape = (sums.shape[0], SIDE - 2 * NBIN)
    lane = lax.broadcasted_iota(jnp.int32, shape, 1)
    tail = jnp.zeros(shape, F32)
    for part, expo in enumerate(expos):
        tail = jnp.where(lane == part, expo, tail)
    return jnp.concatenate([high, low, tail.astype(jnp.int32)], axis=1).astype(jnp.int16)


def decode_part(ref, count, part):
    cols = slice(part * PART, (part + 1) * PART)
    at = COLS + 2 * NBIN + part
    data = jnp.zeros((ref.shape[1], PART), F32)
    for source in range(count):
        expo = ref[source, :, COLS:].astype(jnp.int32)[:, at - COLS : at - COLS + 1]
        scale = jnp.exp2(expo.astype(F32))
        root = ref[source, :, cols].astype(jnp.int32).astype(F32) * (1.0 / CODE)
        data = data + root * jnp.abs(root) * (root * root) * scale
    return data


def decode_bins(ref, count, unit):
    sums = jnp.zeros((ref.shape[1], NBIN), F32)
    for source in range(count):
        side = ref[source, :, COLS:].astype(jnp.int32)
        fixed = side[:, :NBIN] * 65536 + (side[:, NBIN : 2 * NBIN] + 32768)
        sums = sums + fixed.astype(F32) * (1.0 / unit)
    return sums


def image_kernel(
    x_ref, bins_ref, table_ref, noise_ref, centred_0, centred_1, centred_2, centred_3,
    weighted_near, weighted_far, x_buf, centred_buf, weighted_buf, sems
):
    noise = noise_ref[...]
    steps = PARTS
    step = x_buf.shape[0] // steps
    edge = weighted_near.shape[0] // step

    def read(i):
        rows = pl.ds(i * step, step)
        return pltpu.make_async_copy(x_ref.at[rows], x_buf.at[rows], sems.at[0, i])

    def write(i, k):
        if k < PARTS:
            rows, out = pl.ds(i * step, step), (centred_0, centred_1, centred_2, centred_3)[k]
            buf = centred_buf.at[:, k * PART : (k + 1) * PART]
        else:
            rows, buf, out = pl.ds((i - edge) * step, step), weighted_buf, weighted_far
        return pltpu.make_async_copy(buf.at[rows], out.at[rows], sems.at[k + 1, i])

    def chunk(i, keep):
        rows = pl.ds(pl.multiple_of(i * step, step), step)
        match = bin_match(bins_ref[:, rows], 3)
        contrast = contract(match, table_ref[...], ((0,), (0,)))
        read(i).wait()
        for part in range(2):
            cols = slice(part * PIXC, (part + 1) * PIXC)
            product = x_buf[rows, cols].astype(F32) * contrast
            centred_buf[rows, cols] = product.astype(BF16)
            scaled = (product * noise).astype(BF16)
            if keep:
                weighted_near[rows, cols] = scaled
            else:
                weighted_buf[pl.ds(pl.multiple_of((i - edge) * step, step), step), cols] = scaled
        for k in range(PARTS):
            write(i, k).start()
        if not keep:
            write(i, PARTS).start()

    for i in range(steps):
        read(i).start()
    lax.fori_loop(0, edge, lambda i, c: (chunk(i, True), c)[1], 0)
    lax.fori_loop(edge, steps, lambda i, c: (chunk(i, False), c)[1], 0)
    for i in range(steps):
        for k in range(PARTS):
            write(i, k).wait()
        if i >= edge:
            write(i, PARTS).wait()


def score_kernel(
    panel_ref, power_ref, bins_ref, mask_ref, near_ref, far_ref, exp_ref, pair_ref, far_buf, sems
):
    steps = far_ref.shape[0] // CHUNK

    def read(i):
        rows = pl.ds(i * CHUNK, CHUNK)
        return pltpu.make_async_copy(far_ref.at[rows], far_buf.at[rows], sems.at[i])

    for i in range(steps):
        read(i).start()
    real = panel_ref[:, :PIXC].astype(F32)
    imag = panel_ref[:, PIXC:].astype(F32)
    panel_power = (real * real + imag * imag).astype(BF16)
    norm = three_parts(contract(panel_power, power_ref[...], ((1,), (1,))), 1)

    def chunk(at, weighted):
        rows = pl.ds(at, CHUNK)
        norm_part = contract(norm, bin_match(bins_ref[:, rows], 3), ((1,), (0,)))
        direct = contract(panel_ref[...], weighted, ((1,), (1,)))
        scores = direct - 0.5 * norm_part
        allowed = mask_ref[:, rows] > 0
        masked = jnp.where(allowed, scores, -1e30)
        peak = jnp.max(masked, axis=0, keepdims=True)
        weights = jnp.where(allowed, jnp.exp(masked - peak), 0.0)
        exp_ref[:, rows] = weights
        total = jnp.sum(weights, axis=0, keepdims=True)
        pair = jnp.concatenate([peak, total], axis=0)
        for other in range(8):
            pair_ref[other, :, rows] = pair

    def near_chunk(i, carry):
        start = pl.multiple_of(i * CHUNK, CHUNK)
        chunk(start, near_ref[pl.ds(start, CHUNK), :])
        return carry

    def far_chunk(i, carry):
        read(i).wait()
        start = pl.multiple_of(i * CHUNK, CHUNK)
        chunk(pl.multiple_of(start + near_ref.shape[0], CHUNK), far_buf[pl.ds(start, CHUNK), :])
        return carry

    lax.fori_loop(0, near_ref.shape[0] // CHUNK, near_chunk, 0)
    lax.fori_loop(0, steps, far_chunk, 0)


def project_kernel(
    exp_ref, own_ref, both_ref, permuter_ref, half_ref, bins_ref, *rest_refs
):
    packed_ref, evidence_ref, evidence_buf, sem = rest_refs[PARTS:]
    spans = [slice(part * PART, (part + 1) * PART) for part in range(PARTS)]
    own_peak = own_ref[0, 0:1, :]
    peaks = both_ref[:, 0, :]
    peak = jnp.max(peaks, axis=0, keepdims=True)
    total = jnp.sum(both_ref[:, 1, :] * jnp.exp(peaks - peak), axis=0, keepdims=True)
    evidence_buf[...] = peak + jnp.log(total)
    evidence = pltpu.make_async_copy(evidence_buf, evidence_ref, sem)
    evidence.start()
    posterior = (exp_ref[...] * (jnp.exp(own_peak - peak) / total)).astype(BF16)
    by_direction = contract(permuter_ref[...], posterior, ((1,), (0,)))
    row = lax.broadcasted_iota(jnp.int32, (ROWS, 1), 0)
    kept = row_half(row) == half_ref[...]
    post = jnp.where(kept, by_direction, 0.0).astype(BF16)
    sums = contract(post, bin_match(bins_ref[...], 1), ((1,), (1,)))
    expos = []
    for part, cols in enumerate(spans):
        codes, expo = encode(contract(post, rest_refs[part][...], ((1,), (0,))))
        expos.append(expo)
        packed_ref[:, cols] = codes
    packed_ref[:, COLS:] = side_block(sums, expos, 2.0**20)
    evidence.wait()


def plane_kernel(came_ref, packed_ref):
    expos = []
    for part in range(PARTS):
        codes, expo = encode(decode_part(came_ref, 16, part))
        expos.append(expo)
        for other in range(4):
            packed_ref[other, :, part * PART : (part + 1) * PART] = codes
    side = side_block(decode_bins(came_ref, 16, 2.0**20), expos, 2.0**16)
    for other in range(4):
        packed_ref[other, :, COLS:] = side


def shell_kernel(where_ref, came_ref, squares_ref, shells_ref, keep_ref, stats_ref):
    upper = where_ref[0:1, 0:1]
    zh = where_ref[1:2, 0:1]
    data = jnp.concatenate([decode_part(came_ref, 4, part) for part in range(PARTS)], axis=1)
    sums = decode_bins(came_ref, 4, 2.0**16)
    cross = jnp.zeros((1, COLS), F32)
    first = jnp.zeros((1, COLS), F32)
    second = jnp.zeros((1, COLS), F32)
    own_data = jnp.zeros((4, COLS), F32)
    own_sums = jnp.zeros((4, NBIN), F32)
    for z in range(4):
        rows = data[4 * z : 4 * z + 4]
        own_data = jnp.where(zh == z, rows, own_data)
        own_sums = jnp.where(zh == z, sums[4 * z : 4 * z + 4], own_sums)
        cross = cross + jnp.sum(rows[:2] * rows[2:], axis=0, keepdims=True)
        first = first + jnp.sum(rows[:2] * rows[:2], axis=0, keepdims=True)
        second = second + jnp.sum(rows[2:] * rows[2:], axis=0, keepdims=True)
    power0 = jnp.where(upper == 0, first, second)
    power1 = jnp.where(upper == 0, second, first)
    three = jnp.concatenate([cross, power0, power1, jnp.zeros((5, COLS), F32)], axis=0)
    folded = three[:, :PIXC] + three[:, PIXC:]
    by_shell = contract(three_parts(folded, 0), shells_ref[...], ((1,), (1,)))
    by_shell = by_shell[0:8] + by_shell[8:16] + by_shell[16:24]
    squares = squares_ref[...]
    weight = contract(
        three_parts(own_sums, 1), jnp.concatenate([squares] * 3, axis=0), ((1,), (0,))
    )
    whole = own_data / (jnp.concatenate([weight, weight], axis=1) + 1.0)
    keep_ref[...] = whole[:2]
    for other in range(16):
        stats_ref[other, :, PART:] = by_shell
    for part in range(PARTS):
        piece = whole[2:, part * PART : (part + 1) * PART]
        for other in range(16):
            stats_ref[other, 2 * part : 2 * part + 2, :PART] = piece


def finish_kernel(where_ref, came_ref, keep_ref, spread_ref, out_ref):
    totals = came_ref[0, :, PART:]
    for source in range(1, 16):
        totals = totals + came_ref[source, :, PART:]
    fsc = totals[0:1] / jnp.sqrt(totals[1:2] * totals[2:3] + 1e-06)
    half = jnp.broadcast_to((1.0 + fsc) / 2.0, (8, ORIENT))
    factor = contract(three_parts(half, 0), spread_ref[...], ((1,), (0,)))
    factor = factor[0:1] + factor[8:9] + factor[16:17]
    low = where_ref[0:1, 0:1] == 0
    source = where_ref[2:3, 0:1]
    partner = jnp.zeros((8, PART), F32)
    for other in range(16):
        partner = jnp.where(source == other, came_ref[other, :, :PART], partner)
    for part in range(PARTS):
        cols = slice(part * PART, (part + 1) * PART)
        start = (part * PART) % PIXC
        scale = factor[:, start : start + PART]
        keep = keep_ref[:, cols] * scale
        got = partner[2 * part : 2 * part + 2] * scale
        out_ref[0, 0:2, cols] = jnp.where(low, keep, got)
        out_ref[0, 2:4, cols] = jnp.where(low, got, keep)


def call(kernel, name, out_shape, mega, *args, scalars=0, far=(), far_out=(), scratch=()):
    def space(i, hbm):
        if i < 0:
            return pl.BlockSpec(memory_space=pltpu.MemorySpace.SMEM)
        return pl.BlockSpec(
            memory_space=pltpu.MemorySpace.HBM if i in hbm else pltpu.MemorySpace.VMEM
        )

    args = [
        pltpu.with_memory_space_constraint(arg, pltpu.MemorySpace.HBM) if i in far else arg
        for i, arg in enumerate(args)
    ]
    return pl.pallas_call(
        kernel,
        in_specs=[space(i if i >= scalars else -1, far) for i in range(len(args))],
        out_specs=[space(i, far_out) for i in range(len(out_shape))],
        out_shape=out_shape,
        scratch_shapes=scratch,
        compiler_params=pltpu.CompilerParams(vmem_limit_bytes=mega * 1024 * 1024),
        name=name,
    )(*args)


def on_device(particles, panels, sigma2, defocus_bins, half_sets, prior_mask, orient_ids):
    count = particles.shape[0]
    of = jax.ShapeDtypeStruct

    shells = jnp.arange(PIXC, dtype=jnp.int32) * NSHELL // PIXC
    inverse_noise = lookup_small(shells, 1.0 / sigma2)
    table = ctf_table()
    power = (table * table * inverse_noise[None, :]).astype(BF16)
    squares = (table * table).astype(BF16)
    lanes = jnp.arange(ORIENT, dtype=jnp.int32)
    shell_spread = (lanes[:, None] == shells[None, :]).astype(BF16)
    y, zh, x = lax.axis_index("y"), lax.axis_index("zh"), lax.axis_index("x")
    places = jnp.stack([y // 2, zh, (y ^ 2) * 4 + x]).astype(jnp.int32)
    where = jnp.broadcast_to(jnp.pad(places, (0, 5))[:, None], (8, ORIENT))

    direction = row_direction(jnp.arange(ROWS, dtype=jnp.int32))
    match = gathered_orients()[:, None] == jnp.arange(ORIENT, dtype=jnp.int32)[None, :]
    select = jnp.sum(jnp.where(match, orient_ids[None, :], 0), axis=1)

    near, far = pltpu.MemorySpace.VMEM, pltpu.MemorySpace.HBM
    first, rest = 2 * CHUNK, count - 2 * CHUNK
    permuter = (direction[:, None] == select[None, :]).astype(BF16)
    (
        by_zh, bins_row, parts, noise_row, power, squares, permuter, where, shell_spread, half_row,
        mask_row,
    ) = lax.optimization_barrier(
        (
            from_all(panels[0], "zh", 4), defocus_bins[None, :], table_parts(table),
            inverse_noise[None, :], power, squares, permuter, where, shell_spread, half_sets[None, :], prior_mask.reshape(1, count),
        )
    )
    *centred, weighted_near, weighted_far = call(
        image_kernel, "images",
        [
            *[far((count, PART), BF16)] * PARTS,
            near((first, COLS), BF16), far((rest, COLS), BF16),
        ],
        24, particles, bins_row, parts, noise_row,
        far=(0,), far_out=(0, 1, 2, 3, 5),
        scratch=[
            near((count, COLS), BF16), near((count, COLS), BF16), near((rest, COLS), BF16),
            pltpu.SemaphoreType.DMA((PARTS + 2, PARTS)),
        ],
    )
    piece = from_all(by_zh.reshape(8, COLS), PLANE, 16).reshape(ORIENT, COLS)

    own_exp, pair = call(
        score_kernel, "scores", [of((ORIENT, count), F32), of((8, 2, count), F32)], 14,
        piece, power, bins_row, mask_row, weighted_near, weighted_far,
        far=(5,), scratch=[near((rest, COLS), BF16), pltpu.SemaphoreType.DMA((PARTS,))],
    )
    packed, evidence = call(
        project_kernel, "project", [of((ROWS, WIDE), jnp.int16), of((1, count), F32)], 20,
        own_exp, pair, exchange(pair, CLS), permuter, half_row, bins_row,
        *centred, far_out=(1,), scratch=[near((1, count), F32), pltpu.SemaphoreType.DMA],
    )
    (second,) = call(
        plane_kernel, "plane", [of((4, 16, WIDE), jnp.int16)], 8,
        exchange(packed.reshape(16, 16, WIDE), PLANE),
    )
    keep, stats = call(
        shell_kernel, "shells", [of((2, COLS), F32), of((16, 8, PART + ORIENT), F32)], 8,
        where, exchange(second, "zh"), squares, shell_spread,
    )
    (half_maps,) = call(
        finish_kernel, "finish", [of((1, 4, COLS), F32)], 8,
        where, exchange(stats, PLANE), keep, shell_spread,
    )
    return (half_maps, evidence.reshape(count))


def solution(mesh):
    split = Mesh(mesh.devices.reshape(4, 2, 4, 4, 4), AXES)
    placed = (
        P(PTCL, None),
        P(CLS, PTCL, None),
        P(),
        P(PTCL),
        P(PTCL),
        P(PTCL, CLS),
        P(),
    )
    return jax.shard_map(
        on_device,
        mesh=split,
        in_specs=placed,
        out_specs=(P(CLS, PTCL, None), P(PTCL)),
        check_vma=False,
    )
```

```python
import jax
import jax.numpy as jnp
from jax import lax
from jax.experimental import pallas as pl
from jax.experimental.pallas import tpu as pltpu
from jax.sharding import Mesh
from jax.sharding import PartitionSpec as P

PIXC = 1024
COLS = 2 * PIXC
ORIENT = 128
ROWS = 2 * ORIENT
NSHELL = 32
NBIN = 16
AXES = ("zl", "co", "y", "zh", "x")
CLS = ("zl", "co")
PTCL = ("y", "zh", "x")
PLANE = ("y", "x")
SIDE = 128
WIDE = COLS + SIDE
CODE = 32767.0
PARTS = 4
CHUNK = 256
PART = COLS // PARTS
F32 = jnp.float32
BF16 = jnp.bfloat16


def ctf_table():
    bins = jnp.arange(NBIN, dtype=F32)
    defocus = (bins + 1.0) / NBIN
    radius = (jnp.arange(PIXC, dtype=F32) + 0.5) / PIXC
    phase = 0.3 + 2.5 * defocus[:, None] * radius[None, :]
    return jnp.sin(phase) + 0.1 * jnp.cos(phase)


def lookup_small(indices, values):
    count = values.shape[0]
    match = indices[:, None] == jnp.arange(count, dtype=jnp.int32)[None, :]
    return jnp.sum(jnp.where(match, values[None, :], 0.0), axis=1)


def exchange(blocks, axes):
    return lax.all_to_all(blocks, axes, split_axis=0, concat_axis=0, tiled=True)


def from_all(shard, axes, count):
    return exchange(jnp.broadcast_to(shard[None], (count,) + shard.shape), axes)


def row_direction(r):
    j, zh, x, y = r & 1, (r >> 2) & 3, (r >> 4) & 3, r >> 6
    return 4 * (((y & 1) * 4 + zh) * 4 + x) + 2 * (y >> 1) + j


def row_half(r):
    return ((r >> 1) & 1) ^ (r >> 7)


def gathered_orients():
    r = jnp.arange(ORIENT, dtype=jnp.int32)
    j, zh, x, y = r % 2, (r // 2) % 4, (r // 8) % 4, r // 32
    return ((y * 4 + zh) * 4 + x) * 2 + j


def three_parts(table, axis):
    high = table.astype(BF16)
    rest = table - high.astype(F32)
    mid = rest.astype(BF16)
    low = (rest - mid.astype(F32)).astype(BF16)
    return jnp.concatenate([high, mid, low], axis=axis)


def table_parts(table):
    high = lax.reduce_precision(table, 8, 7)
    mid = lax.reduce_precision(table - high, 8, 7)
    low = table - high - mid
    return jnp.concatenate([high, mid, low], axis=0).astype(BF16)


def bin_match(bins, copies):
    row = lax.broadcasted_iota(jnp.int32, (copies * NBIN, bins.shape[1]), 0)
    return jnp.where(row % NBIN == bins, 1.0, 0.0).astype(BF16)


def contract(left, right, dims):
    return lax.dot_general(left, right, (dims, ((), ())), preferred_element_type=F32)


def encode(values):
    size = jnp.abs(values)
    top = jnp.max(size, axis=1, keepdims=True)
    expo = jnp.floor(jnp.log2(jnp.maximum(top, 1e-37))) + 1.0
    root = lax.rsqrt(lax.rsqrt(jnp.maximum(size * jnp.exp2(-expo), 1e-36)))
    code = root * CODE + 0.5
    codes = jnp.where(values < 0.0, -code, code).astype(jnp.int32).astype(jnp.int16)
    return codes, expo


def side_block(sums, expos, unit):
    fixed = jnp.floor(sums * unit + 0.5).astype(jnp.int32)
    high = lax.shift_right_arithmetic(fixed, 16)
    low = (fixed & 65535) - 32768
    shape = (sums.shape[0], SIDE - 2 * NBIN)
    lane = lax.broadcasted_iota(jnp.int32, shape, 1)
    tail = jnp.zeros(shape, F32)
    for part, expo in enumerate(expos):
        tail = jnp.where(lane == part, expo, tail)
    return jnp.concatenate([high, low, tail.astype(jnp.int32)], axis=1).astype(jnp.int16)


def decode_part(ref, count, part):
    cols = slice(part * PART, (part + 1) * PART)
    at = COLS + 2 * NBIN + part
    data = jnp.zeros((ref.shape[1], PART), F32)
    for source in range(count):
        expo = ref[source, :, COLS:].astype(jnp.int32)[:, at - COLS : at - COLS + 1]
        scale = jnp.exp2(expo.astype(F32))
        root = ref[source, :, cols].astype(jnp.int32).astype(F32) * (1.0 / CODE)
        data = data + root * jnp.abs(root) * (root * root) * scale
    return data


def decode_bins(ref, count, unit):
    sums = jnp.zeros((ref.shape[1], NBIN), F32)
    for source in range(count):
        side = ref[source, :, COLS:].astype(jnp.int32)
        fixed = side[:, :NBIN] * 65536 + (side[:, NBIN : 2 * NBIN] + 32768)
        sums = sums + fixed.astype(F32) * (1.0 / unit)
    return sums


def image_kernel(
    x_ref, bins_ref, table_ref, noise_ref, centred_0, centred_1, centred_2, centred_3,
    weighted_near, weighted_far, x_buf, centred_buf, weighted_buf, sems
):
    noise = noise_ref[...]
    steps = PARTS
    step = x_buf.shape[0] // steps
    edge = weighted_near.shape[0] // step

    def read(i):
        rows = pl.ds(i * step, step)
        return pltpu.make_async_copy(x_ref.at[rows], x_buf.at[rows], sems.at[0, i])

    def write(i, k):
        if k < PARTS:
            rows, out = pl.ds(i * step, step), (centred_0, centred_1, centred_2, centred_3)[k]
            buf = centred_buf.at[:, k * PART : (k + 1) * PART]
        else:
            rows, buf, out = pl.ds((i - edge) * step, step), weighted_buf, weighted_far
        return pltpu.make_async_copy(buf.at[rows], out.at[rows], sems.at[k + 1, i])

    def chunk(i, keep):
        rows = pl.ds(pl.multiple_of(i * step, step), step)
        match = bin_match(bins_ref[:, rows], 3)
        contrast = contract(match, table_ref[...], ((0,), (0,)))
        read(i).wait()
        for part in range(2):
            cols = slice(part * PIXC, (part + 1) * PIXC)
            product = x_buf[rows, cols].astype(F32) * contrast
            centred_buf[rows, cols] = product.astype(BF16)
            scaled = (product * noise).astype(BF16)
            if keep:
                weighted_near[rows, cols] = scaled
            else:
                weighted_buf[pl.ds(pl.multiple_of((i - edge) * step, step), step), cols] = scaled
        for k in range(PARTS):
            write(i, k).start()
        if not keep:
            write(i, PARTS).start()

    for i in range(steps):
        read(i).start()
    lax.fori_loop(0, edge, lambda i, c: (chunk(i, True), c)[1], 0)
    lax.fori_loop(edge, steps, lambda i, c: (chunk(i, False), c)[1], 0)
    for i in range(steps):
        for k in range(PARTS):
            write(i, k).wait()
        if i >= edge:
            write(i, PARTS).wait()


def score_kernel(
    panel_ref, power_ref, bins_ref, mask_ref, near_ref, far_ref, exp_ref, pair_ref, far_buf, sems
):
    steps = far_ref.shape[0] // CHUNK

    def read(i):
        rows = pl.ds(i * CHUNK, CHUNK)
        return pltpu.make_async_copy(far_ref.at[rows], far_buf.at[rows], sems.at[i])

    for i in range(steps):
        read(i).start()
    real = panel_ref[:, :PIXC].astype(F32)
    imag = panel_ref[:, PIXC:].astype(F32)
    panel_power = (real * real + imag * imag).astype(BF16)
    norm = three_parts(contract(panel_power, power_ref[...], ((1,), (1,))), 1)

    def chunk(at, weighted):
        rows = pl.ds(at, CHUNK)
        norm_part = contract(norm, bin_match(bins_ref[:, rows], 3), ((1,), (0,)))
        direct = contract(panel_ref[...], weighted, ((1,), (1,)))
        scores = direct - 0.5 * norm_part
        allowed = mask_ref[:, rows] > 0
        masked = jnp.where(allowed, scores, -1e30)
        peak = jnp.max(masked, axis=0, keepdims=True)
        weights = jnp.where(allowed, jnp.exp(masked - peak), 0.0)
        exp_ref[:, rows] = weights
        total = jnp.sum(weights, axis=0, keepdims=True)
        pair = jnp.concatenate([peak, total], axis=0)
        for other in range(8):
            pair_ref[other, :, rows] = pair

    def near_chunk(i, carry):
        start = pl.multiple_of(i * CHUNK, CHUNK)
        chunk(start, near_ref[pl.ds(start, CHUNK), :])
        return carry

    def far_chunk(i, carry):
        read(i).wait()
        start = pl.multiple_of(i * CHUNK, CHUNK)
        chunk(pl.multiple_of(start + near_ref.shape[0], CHUNK), far_buf[pl.ds(start, CHUNK), :])
        return carry

    lax.fori_loop(0, near_ref.shape[0] // CHUNK, near_chunk, 0)
    lax.fori_loop(0, steps, far_chunk, 0)


def project_kernel(
    exp_ref, own_ref, both_ref, permuter_ref, half_ref, bins_ref, *rest_refs
):
    packed_ref, evidence_ref, evidence_buf, sem = rest_refs[PARTS:]
    spans = [slice(part * PART, (part + 1) * PART) for part in range(PARTS)]
    own_peak = own_ref[0, 0:1, :]
    peaks = both_ref[:, 0, :]
    peak = jnp.max(peaks, axis=0, keepdims=True)
    total = jnp.sum(both_ref[:, 1, :] * jnp.exp(peaks - peak), axis=0, keepdims=True)
    evidence_buf[...] = peak + jnp.log(total)
    evidence = pltpu.make_async_copy(evidence_buf, evidence_ref, sem)
    evidence.start()
    posterior = (exp_ref[...] * (jnp.exp(own_peak - peak) / total)).astype(BF16)
    by_direction = contract(permuter_ref[...], posterior, ((1,), (0,)))
    row = lax.broadcasted_iota(jnp.int32, (ROWS, 1), 0)
    kept = row_half(row) == half_ref[...]
    post = jnp.where(kept, by_direction, 0.0).astype(BF16)
    sums = contract(post, bin_match(bins_ref[...], 1), ((1,), (1,)))
    expos = []
    for part, cols in enumerate(spans):
        codes, expo = encode(contract(post, rest_refs[part][...], ((1,), (0,))))
        expos.append(expo)
        packed_ref[:, cols] = codes
    packed_ref[:, COLS:] = side_block(sums, expos, 2.0**20)
    evidence.wait()


def plane_kernel(came_ref, packed_ref):
    expos = []
    for part in range(PARTS):
        codes, expo = encode(decode_part(came_ref, 16, part))
        expos.append(expo)
        packed_ref[:, part * PART : (part + 1) * PART] = codes
    packed_ref[:, COLS:] = side_block(decode_bins(came_ref, 16, 2.0**20), expos, 2.0**16)


def shell_kernel(where_ref, came_ref, squares_ref, shells_ref, keep_ref, stats_ref):
    upper = where_ref[0:1, 0:1]
    zh = where_ref[1:2, 0:1]
    data = jnp.concatenate([decode_part(came_ref, 4, part) for part in range(PARTS)], axis=1)
    sums = decode_bins(came_ref, 4, 2.0**16)
    cross = jnp.zeros((1, COLS), F32)
    first = jnp.zeros((1, COLS), F32)
    second = jnp.zeros((1, COLS), F32)
    own_data = jnp.zeros((4, COLS), F32)
    own_sums = jnp.zeros((4, NBIN), F32)
    for z in range(4):
        rows = data[4 * z : 4 * z + 4]
        own_data = jnp.where(zh == z, rows, own_data)
        own_sums = jnp.where(zh == z, sums[4 * z : 4 * z + 4], own_sums)
        cross = cross + jnp.sum(rows[:2] * rows[2:], axis=0, keepdims=True)
        first = first + jnp.sum(rows[:2] * rows[:2], axis=0, keepdims=True)
        second = second + jnp.sum(rows[2:] * rows[2:], axis=0, keepdims=True)
    power0 = jnp.where(upper == 0, first, second)
    power1 = jnp.where(upper == 0, second, first)
    three = jnp.concatenate([cross, power0, power1, jnp.zeros((5, COLS), F32)], axis=0)
    folded = three[:, :PIXC] + three[:, PIXC:]
    by_shell = contract(three_parts(folded, 0), shells_ref[...], ((1,), (1,)))
    by_shell = by_shell[0:8] + by_shell[8:16] + by_shell[16:24]
    squares = squares_ref[...]
    weight = contract(
        three_parts(own_sums, 1), jnp.concatenate([squares] * 3, axis=0), ((1,), (0,))
    )
    whole = own_data / (jnp.concatenate([weight, weight], axis=1) + 1.0)
    keep_ref[...] = whole[:2]
    for other in range(16):
        stats_ref[other, :, PART:] = by_shell
    for part in range(PARTS):
        piece = whole[2:, part * PART : (part + 1) * PART]
        for other in range(16):
            stats_ref[other, 2 * part : 2 * part + 2, :PART] = piece


def finish_kernel(where_ref, came_ref, keep_ref, spread_ref, out_ref):
    totals = came_ref[0, :, PART:]
    for source in range(1, 16):
        totals = totals + came_ref[source, :, PART:]
    fsc = totals[0:1] / jnp.sqrt(totals[1:2] * totals[2:3] + 1e-06)
    half = jnp.broadcast_to((1.0 + fsc) / 2.0, (8, ORIENT))
    factor = contract(three_parts(half, 0), spread_ref[...], ((1,), (0,)))
    factor = factor[0:1] + factor[8:9] + factor[16:17]
    low = where_ref[0:1, 0:1] == 0
    source = where_ref[2:3, 0:1]
    partner = jnp.zeros((8, PART), F32)
    for other in range(16):
        partner = jnp.where(source == other, came_ref[other, :, :PART], partner)
    for part in range(PARTS):
        cols = slice(part * PART, (part + 1) * PART)
        start = (part * PART) % PIXC
        scale = factor[:, start : start + PART]
        keep = keep_ref[:, cols] * scale
        got = partner[2 * part : 2 * part + 2] * scale
        out_ref[0, 0:2, cols] = jnp.where(low, keep, got)
        out_ref[0, 2:4, cols] = jnp.where(low, got, keep)


def call(kernel, name, out_shape, mega, *args, scalars=0, far=(), far_out=(), scratch=()):
    def space(i, hbm):
        if i < 0:
            return pl.BlockSpec(memory_space=pltpu.MemorySpace.SMEM)
        return pl.BlockSpec(
            memory_space=pltpu.MemorySpace.HBM if i in hbm else pltpu.MemorySpace.VMEM
        )

    args = [
        pltpu.with_memory_space_constraint(arg, pltpu.MemorySpace.HBM) if i in far else arg
        for i, arg in enumerate(args)
    ]
    return pl.pallas_call(
        kernel,
        in_specs=[space(i if i >= scalars else -1, far) for i in range(len(args))],
        out_specs=[space(i, far_out) for i in range(len(out_shape))],
        out_shape=out_shape,
        scratch_shapes=scratch,
        compiler_params=pltpu.CompilerParams(vmem_limit_bytes=mega * 1024 * 1024),
        name=name,
    )(*args)


def on_device(particles, panels, sigma2, defocus_bins, half_sets, prior_mask, orient_ids):
    count = particles.shape[0]
    of = jax.ShapeDtypeStruct

    shells = jnp.arange(PIXC, dtype=jnp.int32) * NSHELL // PIXC
    inverse_noise = lookup_small(shells, 1.0 / sigma2)
    table = ctf_table()
    power = (table * table * inverse_noise[None, :]).astype(BF16)
    squares = (table * table).astype(BF16)
    lanes = jnp.arange(ORIENT, dtype=jnp.int32)
    shell_spread = (lanes[:, None] == shells[None, :]).astype(BF16)
    y, zh, x = lax.axis_index("y"), lax.axis_index("zh"), lax.axis_index("x")
    places = jnp.stack([y // 2, zh, (y ^ 2) * 4 + x]).astype(jnp.int32)
    where = jnp.broadcast_to(jnp.pad(places, (0, 5))[:, None], (8, ORIENT))

    direction = row_direction(jnp.arange(ROWS, dtype=jnp.int32))
    match = gathered_orients()[:, None] == jnp.arange(ORIENT, dtype=jnp.int32)[None, :]
    select = jnp.sum(jnp.where(match, orient_ids[None, :], 0), axis=1)

    near, far = pltpu.MemorySpace.VMEM, pltpu.MemorySpace.HBM
    first, rest = 2 * CHUNK, count - 2 * CHUNK
    permuter = (direction[:, None] == select[None, :]).astype(BF16)
    (
        by_zh, bins_row, parts, noise_row, power, squares, permuter, where, shell_spread, half_row,
        mask_row,
    ) = lax.optimization_barrier(
        (
            from_all(panels[0], "zh", 4), defocus_bins[None, :], table_parts(table),
            inverse_noise[None, :], power, squares, permuter, where, shell_spread, half_sets[None, :], prior_mask.reshape(1, count),
        )
    )
    *centred, weighted_near, weighted_far = call(
        image_kernel, "images",
        [
            *[far((count, PART), BF16)] * PARTS,
            near((first, COLS), BF16), far((rest, COLS), BF16),
        ],
        24, particles, bins_row, parts, noise_row,
        far=(0,), far_out=(0, 1, 2, 3, 5),
        scratch=[
            near((count, COLS), BF16), near((count, COLS), BF16), near((rest, COLS), BF16),
            pltpu.SemaphoreType.DMA((PARTS + 2, PARTS)),
        ],
    )
    piece = from_all(by_zh.reshape(8, COLS), PLANE, 16).reshape(ORIENT, COLS)

    own_exp, pair = call(
        score_kernel, "scores", [of((ORIENT, count), F32), of((8, 2, count), F32)], 14,
        piece, power, bins_row, mask_row, weighted_near, weighted_far,
        far=(5,), scratch=[near((rest, COLS), BF16), pltpu.SemaphoreType.DMA((PARTS,))],
    )
    packed, evidence = call(
        project_kernel, "project", [of((ROWS, WIDE), jnp.int16), of((1, count), F32)], 20,
        own_exp, pair, exchange(pair, CLS), permuter, half_row, bins_row,
        *centred, far_out=(1,), scratch=[near((1, count), F32), pltpu.SemaphoreType.DMA],
    )
    (second,) = call(
        plane_kernel, "plane", [of((16, WIDE), jnp.int16)], 8,
        exchange(packed.reshape(16, 16, WIDE), PLANE),
    )
    keep, stats = call(
        shell_kernel, "shells", [of((2, COLS), F32), of((16, 8, PART + ORIENT), F32)], 8,
        where, lax.all_gather(second, "zh"), squares, shell_spread,
    )
    (half_maps,) = call(
        finish_kernel, "finish", [of((1, 4, COLS), F32)], 8,
        where, exchange(stats, PLANE), keep, shell_spread,
    )
    return (half_maps, evidence.reshape(count))


def solution(mesh):
    split = Mesh(mesh.devices.reshape(4, 2, 4, 4, 4), AXES)
    placed = (
        P(PTCL, None),
        P(CLS, PTCL, None),
        P(),
        P(PTCL),
        P(PTCL),
        P(PTCL, CLS),
        P(),
    )
    return jax.shard_map(
        on_device,
        mesh=split,
        in_specs=placed,
        out_specs=(P(CLS, PTCL, None), P(PTCL)),
        check_vma=False,
    )
```

```python
import jax
import jax.numpy as jnp
from jax import lax
from jax.experimental import pallas as pl
from jax.experimental.pallas import tpu as pltpu
from jax.sharding import Mesh
from jax.sharding import PartitionSpec as P

PIXC = 1024
COLS = 2 * PIXC
ORIENT = 128
ROWS = 2 * ORIENT
NSHELL = 32
NBIN = 16
AXES = ("zl", "co", "y", "zh", "x")
CLS = ("zl", "co")
PTCL = ("y", "zh", "x")
PLANE = ("y", "x")
SIDE = 128
WIDE = COLS + SIDE
CODE = 32767.0
PARTS = 4
CHUNK = 256
PART = COLS // PARTS
F32 = jnp.float32
BF16 = jnp.bfloat16


def ctf_table():
    bins = jnp.arange(NBIN, dtype=F32)
    defocus = (bins + 1.0) / NBIN
    radius = (jnp.arange(PIXC, dtype=F32) + 0.5) / PIXC
    phase = 0.3 + 2.5 * defocus[:, None] * radius[None, :]
    return jnp.sin(phase) + 0.1 * jnp.cos(phase)


def lookup_small(indices, values):
    count = values.shape[0]
    match = indices[:, None] == jnp.arange(count, dtype=jnp.int32)[None, :]
    return jnp.sum(jnp.where(match, values[None, :], 0.0), axis=1)


def exchange(blocks, axes):
    return lax.all_to_all(blocks, axes, split_axis=0, concat_axis=0, tiled=True)


def from_all(shard, axes, count):
    return exchange(jnp.broadcast_to(shard[None], (count,) + shard.shape), axes)


def row_direction(r):
    j, zh, x, y = r & 1, (r >> 2) & 3, (r >> 4) & 3, r >> 6
    return 4 * (((y & 1) * 4 + zh) * 4 + x) + 2 * (y >> 1) + j


def row_half(r):
    return ((r >> 1) & 1) ^ (r >> 7)


def gathered_orients():
    r = jnp.arange(ORIENT, dtype=jnp.int32)
    j, zh, x, y = r % 2, (r // 2) % 4, (r // 8) % 4, r // 32
    return ((y * 4 + zh) * 4 + x) * 2 + j


def three_parts(table, axis):
    high = table.astype(BF16)
    rest = table - high.astype(F32)
    mid = rest.astype(BF16)
    low = (rest - mid.astype(F32)).astype(BF16)
    return jnp.concatenate([high, mid, low], axis=axis)


def table_parts(table):
    high = lax.reduce_precision(table, 8, 7)
    mid = lax.reduce_precision(table - high, 8, 7)
    low = table - high - mid
    return jnp.concatenate([high, mid, low], axis=0).astype(BF16)


def bin_match(bins, copies):
    row = lax.broadcasted_iota(jnp.int32, (copies * NBIN, bins.shape[1]), 0)
    return jnp.where(row % NBIN == bins, 1.0, 0.0).astype(BF16)


def contract(left, right, dims):
    return lax.dot_general(left, right, (dims, ((), ())), preferred_element_type=F32)


def encode(values):
    size = jnp.abs(values)
    top = jnp.max(size, axis=1, keepdims=True)
    expo = jnp.floor(jnp.log2(jnp.maximum(top, 1e-37))) + 1.0
    root = lax.rsqrt(lax.rsqrt(jnp.maximum(size * jnp.exp2(-expo), 1e-36)))
    code = root * CODE + 0.5
    codes = jnp.where(values < 0.0, -code, code).astype(jnp.int32).astype(jnp.int16)
    return codes, expo


def side_block(sums, expos, unit):
    fixed = jnp.floor(sums * unit + 0.5).astype(jnp.int32)
    high = lax.shift_right_arithmetic(fixed, 16)
    low = (fixed & 65535) - 32768
    shape = (sums.shape[0], SIDE - 2 * NBIN)
    lane = lax.broadcasted_iota(jnp.int32, shape, 1)
    tail = jnp.zeros(shape, F32)
    for part, expo in enumerate(expos):
        tail = jnp.where(lane == part, expo, tail)
    return jnp.concatenate([high, low, tail.astype(jnp.int32)], axis=1).astype(jnp.int16)


def decode_part(ref, count, part):
    cols = slice(part * PART, (part + 1) * PART)
    at = COLS + 2 * NBIN + part
    data = jnp.zeros((ref.shape[1], PART), F32)
    for source in range(count):
        expo = ref[source, :, COLS:].astype(jnp.int32)[:, at - COLS : at - COLS + 1]
        scale = jnp.exp2(expo.astype(F32))
        root = ref[source, :, cols].astype(jnp.int32).astype(F32) * (1.0 / CODE)
        data = data + root * jnp.abs(root) * (root * root) * scale
    return data


def decode_bins(ref, count, unit):
    sums = jnp.zeros((ref.shape[1], NBIN), F32)
    for source in range(count):
        side = ref[source, :, COLS:].astype(jnp.int32)
        fixed = side[:, :NBIN] * 65536 + (side[:, NBIN : 2 * NBIN] + 32768)
        sums = sums + fixed.astype(F32) * (1.0 / unit)
    return sums


def image_kernel(
    x_ref, bins_ref, table_ref, noise_ref, centred_0, centred_1, centred_2, centred_3,
    weighted_near, weighted_far, x_buf, centred_buf, weighted_buf, sems
):
    noise = noise_ref[...]
    steps = PARTS
    step = x_buf.shape[0] // steps
    edge = weighted_near.shape[0] // step

    def read(i):
        rows = pl.ds(i * step, step)
        return pltpu.make_async_copy(x_ref.at[rows], x_buf.at[rows], sems.at[0, i])

    def write(i, k):
        if k < PARTS:
            rows, out = pl.ds(i * step, step), (centred_0, centred_1, centred_2, centred_3)[k]
            buf = centred_buf.at[:, k * PART : (k + 1) * PART]
        else:
            rows, buf, out = pl.ds((i - edge) * step, step), weighted_buf, weighted_far
        return pltpu.make_async_copy(buf.at[rows], out.at[rows], sems.at[k + 1, i])

    def chunk(i, keep):
        rows = pl.ds(pl.multiple_of(i * step, step), step)
        match = bin_match(bins_ref[:, rows], 3)
        contrast = contract(match, table_ref[...], ((0,), (0,)))
        read(i).wait()
        for part in range(2):
            cols = slice(part * PIXC, (part + 1) * PIXC)
            product = x_buf[rows, cols].astype(F32) * contrast
            centred_buf[rows, cols] = product.astype(BF16)
            scaled = (product * noise).astype(BF16)
            if keep:
                weighted_near[rows, cols] = scaled
            else:
                weighted_buf[pl.ds(pl.multiple_of((i - edge) * step, step), step), cols] = scaled
        for k in range(PARTS):
            write(i, k).start()
        if not keep:
            write(i, PARTS).start()

    for i in range(steps):
        read(i).start()
    lax.fori_loop(0, edge, lambda i, c: (chunk(i, True), c)[1], 0)
    lax.fori_loop(edge, steps, lambda i, c: (chunk(i, False), c)[1], 0)
    for i in range(steps):
        for k in range(PARTS):
            write(i, k).wait()
        if i >= edge:
            write(i, PARTS).wait()


def score_kernel(
    panel_ref, power_ref, bins_ref, mask_ref, near_ref, far_ref, *more_refs
):
    exp_ref, pair_ref = more_refs[PARTS : PARTS + 2]
    far_buf, sems = more_refs[-2:]
    steps = far_ref.shape[0] // CHUNK

    def read(i):
        rows = pl.ds(i * CHUNK, CHUNK)
        return pltpu.make_async_copy(far_ref.at[rows], far_buf.at[rows], sems.at[i])

    for i in range(steps):
        read(i).start()
    real = panel_ref[:, :PIXC].astype(F32)
    imag = panel_ref[:, PIXC:].astype(F32)
    panel_power = (real * real + imag * imag).astype(BF16)
    norm = three_parts(contract(panel_power, power_ref[...], ((1,), (1,))), 1)

    def chunk(at, weighted):
        rows = pl.ds(at, CHUNK)
        norm_part = contract(norm, bin_match(bins_ref[:, rows], 3), ((1,), (0,)))
        direct = contract(panel_ref[...], weighted, ((1,), (1,)))
        scores = direct - 0.5 * norm_part
        allowed = mask_ref[:, rows] > 0
        masked = jnp.where(allowed, scores, -1e30)
        peak = jnp.max(masked, axis=0, keepdims=True)
        weights = jnp.where(allowed, jnp.exp(masked - peak), 0.0)
        exp_ref[:, rows] = weights
        total = jnp.sum(weights, axis=0, keepdims=True)
        pair = jnp.concatenate([peak, total], axis=0)
        for other in range(8):
            pair_ref[other, :, rows] = pair

    def near_chunk(i, carry):
        start = pl.multiple_of(i * CHUNK, CHUNK)
        chunk(start, near_ref[pl.ds(start, CHUNK), :])
        return carry

    def far_chunk(i, carry):
        read(i).wait()
        start = pl.multiple_of(i * CHUNK, CHUNK)
        chunk(pl.multiple_of(start + near_ref.shape[0], CHUNK), far_buf[pl.ds(start, CHUNK), :])
        return carry

    lax.fori_loop(0, near_ref.shape[0] // CHUNK, near_chunk, 0)
    lax.fori_loop(0, steps, far_chunk, 0)


def project_kernel(
    exp_ref, own_ref, both_ref, permuter_ref, half_ref, bins_ref, *rest_refs
):
    packed_ref, evidence_ref, evidence_buf, sem = rest_refs[PARTS:]
    spans = [slice(part * PART, (part + 1) * PART) for part in range(PARTS)]
    own_peak = own_ref[0, 0:1, :]
    peaks = both_ref[:, 0, :]
    peak = jnp.max(peaks, axis=0, keepdims=True)
    total = jnp.sum(both_ref[:, 1, :] * jnp.exp(peaks - peak), axis=0, keepdims=True)
    evidence_buf[...] = peak + jnp.log(total)
    evidence = pltpu.make_async_copy(evidence_buf, evidence_ref, sem)
    evidence.start()
    posterior = (exp_ref[...] * (jnp.exp(own_peak - peak) / total)).astype(BF16)
    by_direction = contract(permuter_ref[...], posterior, ((1,), (0,)))
    row = lax.broadcasted_iota(jnp.int32, (ROWS, 1), 0)
    kept = row_half(row) == half_ref[...]
    post = jnp.where(kept, by_direction, 0.0).astype(BF16)
    sums = contract(post, bin_match(bins_ref[...], 1), ((1,), (1,)))
    expos = []
    for part, cols in enumerate(spans):
        codes, expo = encode(contract(post, rest_refs[part][...], ((1,), (0,))))
        expos.append(expo)
        packed_ref[:, cols] = codes
    packed_ref[:, COLS:] = side_block(sums, expos, 2.0**20)
    evidence.wait()


def plane_kernel(came_ref, packed_ref):
    expos = []
    for part in range(PARTS):
        codes, expo = encode(decode_part(came_ref, 16, part))
        expos.append(expo)
        packed_ref[:, part * PART : (part + 1) * PART] = codes
    packed_ref[:, COLS:] = side_block(decode_bins(came_ref, 16, 2.0**20), expos, 2.0**16)


def shell_kernel(where_ref, came_ref, squares_ref, shells_ref, keep_ref, stats_ref):
    upper = where_ref[0:1, 0:1]
    zh = where_ref[1:2, 0:1]
    data = jnp.concatenate([decode_part(came_ref, 4, part) for part in range(PARTS)], axis=1)
    sums = decode_bins(came_ref, 4, 2.0**16)
    cross = jnp.zeros((1, COLS), F32)
    first = jnp.zeros((1, COLS), F32)
    second = jnp.zeros((1, COLS), F32)
    own_data = jnp.zeros((4, COLS), F32)
    own_sums = jnp.zeros((4, NBIN), F32)
    for z in range(4):
        rows = data[4 * z : 4 * z + 4]
        own_data = jnp.where(zh == z, rows, own_data)
        own_sums = jnp.where(zh == z, sums[4 * z : 4 * z + 4], own_sums)
        cross = cross + jnp.sum(rows[:2] * rows[2:], axis=0, keepdims=True)
        first = first + jnp.sum(rows[:2] * rows[:2], axis=0, keepdims=True)
        second = second + jnp.sum(rows[2:] * rows[2:], axis=0, keepdims=True)
    power0 = jnp.where(upper == 0, first, second)
    power1 = jnp.where(upper == 0, second, first)
    three = jnp.concatenate([cross, power0, power1, jnp.zeros((5, COLS), F32)], axis=0)
    folded = three[:, :PIXC] + three[:, PIXC:]
    by_shell = contract(three_parts(folded, 0), shells_ref[...], ((1,), (1,)))
    by_shell = by_shell[0:8] + by_shell[8:16] + by_shell[16:24]
    squares = squares_ref[...]
    weight = contract(
        three_parts(own_sums, 1), jnp.concatenate([squares] * 3, axis=0), ((1,), (0,))
    )
    whole = own_data / (jnp.concatenate([weight, weight], axis=1) + 1.0)
    keep_ref[...] = whole[:2]
    for other in range(16):
        stats_ref[other, :, PART:] = by_shell
    for part in range(PARTS):
        piece = whole[2:, part * PART : (part + 1) * PART]
        for other in range(16):
            stats_ref[other, 2 * part : 2 * part + 2, :PART] = piece


def finish_kernel(where_ref, came_ref, keep_ref, spread_ref, out_ref):
    totals = came_ref[0, :, PART:]
    for source in range(1, 16):
        totals = totals + came_ref[source, :, PART:]
    fsc = totals[0:1] / jnp.sqrt(totals[1:2] * totals[2:3] + 1e-06)
    half = jnp.broadcast_to((1.0 + fsc) / 2.0, (8, ORIENT))
    factor = contract(three_parts(half, 0), spread_ref[...], ((1,), (0,)))
    factor = factor[0:1] + factor[8:9] + factor[16:17]
    low = where_ref[0:1, 0:1] == 0
    source = where_ref[2:3, 0:1]
    partner = jnp.zeros((8, PART), F32)
    for other in range(16):
        partner = jnp.where(source == other, came_ref[other, :, :PART], partner)
    for part in range(PARTS):
        cols = slice(part * PART, (part + 1) * PART)
        start = (part * PART) % PIXC
        scale = factor[:, start : start + PART]
        keep = keep_ref[:, cols] * scale
        got = partner[2 * part : 2 * part + 2] * scale
        out_ref[0, 0:2, cols] = jnp.where(low, keep, got)
        out_ref[0, 2:4, cols] = jnp.where(low, got, keep)


def call(kernel, name, out_shape, mega, *args, scalars=0, far=(), far_out=(), scratch=(), alias={}):
    def space(i, hbm):
        if i < 0:
            return pl.BlockSpec(memory_space=pltpu.MemorySpace.SMEM)
        return pl.BlockSpec(
            memory_space=pltpu.MemorySpace.HBM if i in hbm else pltpu.MemorySpace.VMEM
        )

    args = [
        pltpu.with_memory_space_constraint(arg, pltpu.MemorySpace.HBM) if i in far else arg
        for i, arg in enumerate(args)
    ]
    return pl.pallas_call(
        kernel,
        in_specs=[space(i if i >= scalars else -1, far) for i in range(len(args))],
        out_specs=[space(i, far_out) for i in range(len(out_shape))],
        out_shape=out_shape,
        scratch_shapes=scratch,
        input_output_aliases=alias,
        compiler_params=pltpu.CompilerParams(vmem_limit_bytes=mega * 1024 * 1024),
        name=name,
    )(*args)


def on_device(particles, panels, sigma2, defocus_bins, half_sets, prior_mask, orient_ids):
    count = particles.shape[0]
    of = jax.ShapeDtypeStruct

    shells = jnp.arange(PIXC, dtype=jnp.int32) * NSHELL // PIXC
    inverse_noise = lookup_small(shells, 1.0 / sigma2)
    table = ctf_table()
    power = (table * table * inverse_noise[None, :]).astype(BF16)
    squares = (table * table).astype(BF16)
    lanes = jnp.arange(ORIENT, dtype=jnp.int32)
    shell_spread = (lanes[:, None] == shells[None, :]).astype(BF16)
    y, zh, x = lax.axis_index("y"), lax.axis_index("zh"), lax.axis_index("x")
    places = jnp.stack([y // 2, zh, (y ^ 2) * 4 + x]).astype(jnp.int32)
    where = jnp.broadcast_to(jnp.pad(places, (0, 5))[:, None], (8, ORIENT))

    direction = row_direction(jnp.arange(ROWS, dtype=jnp.int32))
    match = gathered_orients()[:, None] == jnp.arange(ORIENT, dtype=jnp.int32)[None, :]
    select = jnp.sum(jnp.where(match, orient_ids[None, :], 0), axis=1)

    near, far = pltpu.MemorySpace.VMEM, pltpu.MemorySpace.HBM
    first, rest = 2 * CHUNK, count - 2 * CHUNK
    permuter = (direction[:, None] == select[None, :]).astype(BF16)
    (
        by_zh, bins_row, parts, noise_row, power, squares, permuter, where, shell_spread, half_row,
        mask_row,
    ) = lax.optimization_barrier(
        (
            from_all(panels[0], "zh", 4), defocus_bins[None, :], table_parts(table),
            inverse_noise[None, :], power, squares, permuter, where, shell_spread, half_sets[None, :], prior_mask.reshape(1, count),
        )
    )
    *centred, weighted_near, weighted_far = call(
        image_kernel, "images",
        [
            *[far((count, PART), BF16)] * PARTS,
            near((first, COLS), BF16), far((rest, COLS), BF16),
        ],
        24, particles, bins_row, parts, noise_row,
        far=(0,), far_out=(0, 1, 2, 3, 5),
        scratch=[
            near((count, COLS), BF16), near((count, COLS), BF16), near((rest, COLS), BF16),
            pltpu.SemaphoreType.DMA((PARTS + 2, PARTS)),
        ],
    )
    piece = from_all(by_zh.reshape(8, COLS), PLANE, 16).reshape(ORIENT, COLS)

    own_exp, pair, *centred = call(
        score_kernel, "scores",
        [of((ORIENT, count), F32), of((8, 2, count), F32), *[far((count, PART), BF16)] * PARTS],
        14, piece, power, bins_row, mask_row, weighted_near, weighted_far, *centred,
        far=(5, 6, 7, 8, 9), far_out=(2, 3, 4, 5), alias={6: 2, 7: 3, 8: 4, 9: 5}, scratch=[near((rest, COLS), BF16), pltpu.SemaphoreType.DMA((PARTS,))],
    )
    packed, evidence = call(
        project_kernel, "project", [of((ROWS, WIDE), jnp.int16), of((1, count), F32)], 20,
        own_exp, pair, exchange(pair, CLS), permuter, half_row, bins_row,
        *centred, far_out=(1,), scratch=[near((1, count), F32), pltpu.SemaphoreType.DMA],
    )
    (second,) = call(
        plane_kernel, "plane", [of((16, WIDE), jnp.int16)], 8,
        exchange(packed.reshape(16, 16, WIDE), PLANE),
    )
    keep, stats = call(
        shell_kernel, "shells", [of((2, COLS), F32), of((16, 8, PART + ORIENT), F32)], 8,
        where, lax.all_gather(second, "zh"), squares, shell_spread,
    )
    (half_maps,) = call(
        finish_kernel, "finish", [of((1, 4, COLS), F32)], 8,
        where, exchange(stats, PLANE), keep, shell_spread,
    )
    return (half_maps, evidence.reshape(count))


def solution(mesh):
    split = Mesh(mesh.devices.reshape(4, 2, 4, 4, 4), AXES)
    placed = (
        P(PTCL, None),
        P(CLS, PTCL, None),
        P(),
        P(PTCL),
        P(PTCL),
        P(PTCL, CLS),
        P(),
    )
    return jax.shard_map(
        on_device,
        mesh=split,
        in_specs=placed,
        out_specs=(P(CLS, PTCL, None), P(PTCL)),
        check_vma=False,
    )
```

```python
import jax
import jax.numpy as jnp
from jax import lax
from jax.experimental import pallas as pl
from jax.experimental.pallas import tpu as pltpu
from jax.sharding import Mesh
from jax.sharding import PartitionSpec as P

PIXC = 1024
COLS = 2 * PIXC
ORIENT = 128
ROWS = 2 * ORIENT
NSHELL = 32
NBIN = 16
AXES = ("zl", "co", "y", "zh", "x")
CLS = ("zl", "co")
PTCL = ("y", "zh", "x")
PLANE = ("y", "x")
SIDE = 128
WIDE = COLS + SIDE
CODE = 32767.0
PARTS = 4
CHUNK = 256
PART = COLS // PARTS
F32 = jnp.float32
BF16 = jnp.bfloat16


def ctf_table():
    bins = jnp.arange(NBIN, dtype=F32)
    defocus = (bins + 1.0) / NBIN
    radius = (jnp.arange(PIXC, dtype=F32) + 0.5) / PIXC
    phase = 0.3 + 2.5 * defocus[:, None] * radius[None, :]
    return jnp.sin(phase) + 0.1 * jnp.cos(phase)


def lookup_small(indices, values):
    count = values.shape[0]
    match = indices[:, None] == jnp.arange(count, dtype=jnp.int32)[None, :]
    return jnp.sum(jnp.where(match, values[None, :], 0.0), axis=1)


def exchange(blocks, axes):
    return lax.all_to_all(blocks, axes, split_axis=0, concat_axis=0, tiled=True)


def from_all(shard, axes, count):
    return exchange(jnp.broadcast_to(shard[None], (count,) + shard.shape), axes)


def row_direction(r):
    j, zh, x, y = r & 1, (r >> 2) & 3, (r >> 4) & 3, r >> 6
    return 4 * (((y & 1) * 4 + zh) * 4 + x) + 2 * (y >> 1) + j


def row_half(r):
    return ((r >> 1) & 1) ^ (r >> 7)


def gathered_orients():
    r = jnp.arange(ORIENT, dtype=jnp.int32)
    j, zh, x, y = r % 2, (r // 2) % 4, (r // 8) % 4, r // 32
    return ((y * 4 + zh) * 4 + x) * 2 + j


def three_parts(table, axis):
    high = table.astype(BF16)
    rest = table - high.astype(F32)
    mid = rest.astype(BF16)
    low = (rest - mid.astype(F32)).astype(BF16)
    return jnp.concatenate([high, mid, low], axis=axis)


def table_parts(table):
    high = lax.reduce_precision(table, 8, 7)
    mid = lax.reduce_precision(table - high, 8, 7)
    low = table - high - mid
    return jnp.concatenate([high, mid, low], axis=0).astype(BF16)


def bin_match(bins, copies):
    row = lax.broadcasted_iota(jnp.int32, (copies * NBIN, bins.shape[1]), 0)
    return jnp.where(row % NBIN == bins, 1.0, 0.0).astype(BF16)


def contract(left, right, dims):
    return lax.dot_general(left, right, (dims, ((), ())), preferred_element_type=F32)


def encode(values):
    size = jnp.abs(values)
    top = jnp.max(size, axis=1, keepdims=True)
    expo = jnp.floor(jnp.log2(jnp.maximum(top, 1e-37))) + 1.0
    root = lax.rsqrt(lax.rsqrt(jnp.maximum(size * jnp.exp2(-expo), 1e-36)))
    code = root * CODE + 0.5
    codes = jnp.where(values < 0.0, -code, code).astype(jnp.int32).astype(jnp.int16)
    return codes, expo


def side_block(sums, expos, unit):
    fixed = jnp.floor(sums * unit + 0.5).astype(jnp.int32)
    high = lax.shift_right_arithmetic(fixed, 16)
    low = (fixed & 65535) - 32768
    shape = (sums.shape[0], SIDE - 2 * NBIN)
    lane = lax.broadcasted_iota(jnp.int32, shape, 1)
    tail = jnp.zeros(shape, F32)
    for part, expo in enumerate(expos):
        tail = jnp.where(lane == part, expo, tail)
    return jnp.concatenate([high, low, tail.astype(jnp.int32)], axis=1).astype(jnp.int16)


def decode_part(ref, count, part):
    cols = slice(part * PART, (part + 1) * PART)
    at = COLS + 2 * NBIN + part
    data = jnp.zeros((ref.shape[1], PART), F32)
    for source in range(count):
        expo = ref[source, :, COLS:].astype(jnp.int32)[:, at - COLS : at - COLS + 1]
        scale = jnp.exp2(expo.astype(F32))
        root = ref[source, :, cols].astype(jnp.int32).astype(F32) * (1.0 / CODE)
        data = data + root * jnp.abs(root) * (root * root) * scale
    return data


def decode_bins(ref, count, unit):
    sums = jnp.zeros((ref.shape[1], NBIN), F32)
    for source in range(count):
        side = ref[source, :, COLS:].astype(jnp.int32)
        fixed = side[:, :NBIN] * 65536 + (side[:, NBIN : 2 * NBIN] + 32768)
        sums = sums + fixed.astype(F32) * (1.0 / unit)
    return sums


def image_kernel(
    x_ref, bins_ref, table_ref, noise_ref, centred_0, centred_1, centred_2, centred_3,
    weighted_near, weighted_far, x_buf, centred_buf, weighted_buf, sems
):
    noise = noise_ref[...]
    steps = PARTS
    step = x_buf.shape[0] // steps
    edge = weighted_near.shape[0] // step

    def read(i):
        rows = pl.ds(i * step, step)
        return pltpu.make_async_copy(x_ref.at[rows], x_buf.at[rows], sems.at[0, i])

    def write(i, k):
        if k < PARTS:
            rows, out = pl.ds(i * step, step), (centred_0, centred_1, centred_2, centred_3)[k]
            buf = centred_buf.at[:, k * PART : (k + 1) * PART]
        else:
            rows, buf, out = pl.ds((i - edge) * step, step), weighted_buf, weighted_far
        return pltpu.make_async_copy(buf.at[rows], out.at[rows], sems.at[k + 1, i])

    def chunk(i, keep):
        rows = pl.ds(pl.multiple_of(i * step, step), step)
        match = bin_match(bins_ref[:, rows], 3)
        contrast = contract(match, table_ref[...], ((0,), (0,)))
        read(i).wait()
        for part in range(2):
            cols = slice(part * PIXC, (part + 1) * PIXC)
            product = x_buf[rows, cols].astype(F32) * contrast
            centred_buf[rows, cols] = product.astype(BF16)
            scaled = (product * noise).astype(BF16)
            if keep:
                weighted_near[rows, cols] = scaled
            else:
                weighted_buf[pl.ds(pl.multiple_of((i - edge) * step, step), step), cols] = scaled
        for k in range(PARTS):
            write(i, k).start()
        if not keep:
            write(i, PARTS).start()

    for i in range(steps):
        read(i).start()
    lax.fori_loop(0, edge, lambda i, c: (chunk(i, True), c)[1], 0)
    lax.fori_loop(edge, steps, lambda i, c: (chunk(i, False), c)[1], 0)
    for i in range(steps):
        for k in range(PARTS):
            write(i, k).wait()
        if i >= edge:
            write(i, PARTS).wait()


def score_kernel(
    panel_ref, power_ref, bins_ref, mask_ref, near_ref, far_ref, exp_ref, pair_ref, far_buf, sems
):
    steps = far_ref.shape[0] // CHUNK

    def read(i):
        rows = pl.ds(i * CHUNK, CHUNK)
        return pltpu.make_async_copy(far_ref.at[rows], far_buf.at[rows], sems.at[i])

    for i in range(steps):
        read(i).start()
    real = panel_ref[:, :PIXC].astype(F32)
    imag = panel_ref[:, PIXC:].astype(F32)
    panel_power = (real * real + imag * imag).astype(BF16)
    norm = three_parts(contract(panel_power, power_ref[...], ((1,), (1,))), 1)

    def chunk(at, weighted):
        rows = pl.ds(at, CHUNK)
        norm_part = contract(norm, bin_match(bins_ref[:, rows], 3), ((1,), (0,)))
        direct = contract(panel_ref[...], weighted, ((1,), (1,)))
        scores = direct - 0.5 * norm_part
        allowed = mask_ref[:, rows] > 0
        masked = jnp.where(allowed, scores, -1e30)
        peak = jnp.max(masked, axis=0, keepdims=True)
        weights = jnp.where(allowed, jnp.exp(masked - peak), 0.0)
        exp_ref[:, rows] = weights
        total = jnp.sum(weights, axis=0, keepdims=True)
        pair = jnp.concatenate([peak, total], axis=0)
        for other in range(8):
            pair_ref[other, :, rows] = pair

    def near_chunk(i, carry):
        start = pl.multiple_of(i * CHUNK, CHUNK)
        chunk(start, near_ref[pl.ds(start, CHUNK), :])
        return carry

    def far_chunk(i, carry):
        read(i).wait()
        start = pl.multiple_of(i * CHUNK, CHUNK)
        chunk(pl.multiple_of(start + near_ref.shape[0], CHUNK), far_buf[pl.ds(start, CHUNK), :])
        return carry

    lax.fori_loop(0, near_ref.shape[0] // CHUNK, near_chunk, 0)
    lax.fori_loop(0, steps, far_chunk, 0)


def project_kernel(
    exp_ref, own_ref, both_ref, permuter_ref, half_ref, bins_ref, *rest_refs
):
    packed_ref, evidence_ref, evidence_buf, sem = rest_refs[PARTS:]
    spans = [slice(part * PART, (part + 1) * PART) for part in range(PARTS)]
    own_peak = own_ref[0, 0:1, :]
    peaks = both_ref[:, 0, :]
    peak = jnp.max(peaks, axis=0, keepdims=True)
    total = jnp.sum(both_ref[:, 1, :] * jnp.exp(peaks - peak), axis=0, keepdims=True)
    evidence_buf[...] = peak + jnp.log(total)
    evidence = pltpu.make_async_copy(evidence_buf, evidence_ref, sem)
    evidence.start()
    posterior = (exp_ref[...] * (jnp.exp(own_peak - peak) / total)).astype(BF16)
    by_direction = contract(permuter_ref[...], posterior, ((1,), (0,)))
    row = lax.broadcasted_iota(jnp.int32, (ROWS, 1), 0)
    kept = row_half(row) == half_ref[...]
    post = jnp.where(kept, by_direction, 0.0).astype(BF16)
    sums = contract(post, bin_match(bins_ref[...], 1), ((1,), (1,)))
    expos = []
    for part, cols in enumerate(spans):
        codes, expo = encode(contract(post, rest_refs[part][...], ((1,), (0,))))
        expos.append(expo)
        packed_ref[:, cols] = codes
    packed_ref[:, COLS:] = side_block(sums, expos, 2.0**20)
    evidence.wait()


def plane_kernel(came_ref, packed_ref):
    expos = []
    for part in range(PARTS):
        codes, expo = encode(decode_part(came_ref, 16, part))
        expos.append(expo)
        packed_ref[:, part * PART : (part + 1) * PART] = codes
    packed_ref[:, COLS:] = side_block(decode_bins(came_ref, 16, 2.0**20), expos, 2.0**16)


def shell_kernel(where_ref, came_ref, squares_ref, shells_ref, keep_ref, stats_ref):
    upper = where_ref[0:1, 0:1]
    zh = where_ref[1:2, 0:1]
    data = jnp.concatenate([decode_part(came_ref, 4, part) for part in range(PARTS)], axis=1)
    sums = decode_bins(came_ref, 4, 2.0**16)
    cross = jnp.zeros((1, COLS), F32)
    first = jnp.zeros((1, COLS), F32)
    second = jnp.zeros((1, COLS), F32)
    own_data = jnp.zeros((4, COLS), F32)
    own_sums = jnp.zeros((4, NBIN), F32)
    for z in range(4):
        rows = data[4 * z : 4 * z + 4]
        own_data = jnp.where(zh == z, rows, own_data)
        own_sums = jnp.where(zh == z, sums[4 * z : 4 * z + 4], own_sums)
        cross = cross + jnp.sum(rows[:2] * rows[2:], axis=0, keepdims=True)
        first = first + jnp.sum(rows[:2] * rows[:2], axis=0, keepdims=True)
        second = second + jnp.sum(rows[2:] * rows[2:], axis=0, keepdims=True)
    power0 = jnp.where(upper == 0, first, second)
    power1 = jnp.where(upper == 0, second, first)
    three = jnp.concatenate([cross, power0, power1, jnp.zeros((5, COLS), F32)], axis=0)
    folded = three[:, :PIXC] + three[:, PIXC:]
    by_shell = contract(three_parts(folded, 0), shells_ref[...], ((1,), (1,)))
    by_shell = by_shell[0:8] + by_shell[8:16] + by_shell[16:24]
    squares = squares_ref[...]
    weight = contract(
        three_parts(own_sums, 1), jnp.concatenate([squares] * 3, axis=0), ((1,), (0,))
    )
    whole = own_data / (jnp.concatenate([weight, weight], axis=1) + 1.0)
    keep_ref[...] = whole[:2]
    for other in range(16):
        stats_ref[other, :, PART:] = by_shell
    for part in range(PARTS):
        piece = whole[2:, part * PART : (part + 1) * PART]
        for other in range(16):
            stats_ref[other, 2 * part : 2 * part + 2, :PART] = piece


def finish_kernel(where_ref, came_ref, keep_ref, spread_ref, out_ref):
    totals = came_ref[0, :, PART:]
    for source in range(1, 16):
        totals = totals + came_ref[source, :, PART:]
    fsc = totals[0:1] / jnp.sqrt(totals[1:2] * totals[2:3] + 1e-06)
    half = jnp.broadcast_to((1.0 + fsc) / 2.0, (8, ORIENT))
    factor = contract(three_parts(half, 0), spread_ref[...], ((1,), (0,)))
    factor = factor[0:1] + factor[8:9] + factor[16:17]
    low = where_ref[0:1, 0:1] == 0
    source = where_ref[2:3, 0:1]
    partner = jnp.zeros((8, PART), F32)
    for other in range(16):
        partner = jnp.where(source == other, came_ref[other, :, :PART], partner)
    for part in range(PARTS):
        cols = slice(part * PART, (part + 1) * PART)
        start = (part * PART) % PIXC
        scale = factor[:, start : start + PART]
        keep = keep_ref[:, cols] * scale
        got = partner[2 * part : 2 * part + 2] * scale
        out_ref[0, 0:2, cols] = jnp.where(low, keep, got)
        out_ref[0, 2:4, cols] = jnp.where(low, got, keep)


def call(kernel, name, out_shape, mega, *args, scalars=0, far=(), far_out=(), scratch=()):
    def space(i, hbm):
        if i < 0:
            return pl.BlockSpec(memory_space=pltpu.MemorySpace.SMEM)
        return pl.BlockSpec(
            memory_space=pltpu.MemorySpace.HBM if i in hbm else pltpu.MemorySpace.VMEM
        )

    args = [
        pltpu.with_memory_space_constraint(arg, pltpu.MemorySpace.HBM) if i in far else arg
        for i, arg in enumerate(args)
    ]
    return pl.pallas_call(
        kernel,
        in_specs=[space(i if i >= scalars else -1, far) for i in range(len(args))],
        out_specs=[space(i, far_out) for i in range(len(out_shape))],
        out_shape=out_shape,
        scratch_shapes=scratch,
        compiler_params=pltpu.CompilerParams(vmem_limit_bytes=mega * 1024 * 1024),
        name=name,
    )(*args)


def on_device(particles, panels, sigma2, defocus_bins, half_sets, prior_mask, orient_ids):
    count = particles.shape[0]
    of = jax.ShapeDtypeStruct

    by_zh, sigma2, orient_ids = lax.optimization_barrier(
        (lax.all_gather(panels[0], "zh"), sigma2, orient_ids)
    )
    shells = jnp.arange(PIXC, dtype=jnp.int32) * NSHELL // PIXC
    inverse_noise = lookup_small(shells, 1.0 / sigma2)
    table = ctf_table()
    power = (table * table * inverse_noise[None, :]).astype(BF16)
    squares = (table * table).astype(BF16)
    lanes = jnp.arange(ORIENT, dtype=jnp.int32)
    shell_spread = (lanes[:, None] == shells[None, :]).astype(BF16)
    y, zh, x = lax.axis_index("y"), lax.axis_index("zh"), lax.axis_index("x")
    places = jnp.stack([y // 2, zh, (y ^ 2) * 4 + x]).astype(jnp.int32)
    where = jnp.broadcast_to(jnp.pad(places, (0, 5))[:, None], (8, ORIENT))

    direction = row_direction(jnp.arange(ROWS, dtype=jnp.int32))
    match = gathered_orients()[:, None] == jnp.arange(ORIENT, dtype=jnp.int32)[None, :]
    select = jnp.sum(jnp.where(match, orient_ids[None, :], 0), axis=1)

    near, far = pltpu.MemorySpace.VMEM, pltpu.MemorySpace.HBM
    first, rest = 2 * CHUNK, count - 2 * CHUNK
    permuter = (direction[:, None] == select[None, :]).astype(BF16)
    bins_row = defocus_bins[None, :]
    *centred, weighted_near, weighted_far = call(
        image_kernel, "images",
        [
            *[far((count, PART), BF16)] * PARTS,
            near((first, COLS), BF16), far((rest, COLS), BF16),
        ],
        24, particles, bins_row, table_parts(table), inverse_noise[None, :],
        far=(0,), far_out=(0, 1, 2, 3, 5),
        scratch=[
            near((count, COLS), BF16), near((count, COLS), BF16), near((rest, COLS), BF16),
            pltpu.SemaphoreType.DMA((PARTS + 2, PARTS)),
        ],
    )
    piece, power, squares, permuter, where, shell_spread, half_row, mask_row = (
        lax.optimization_barrier(
            (
                from_all(by_zh.reshape(8, COLS), PLANE, 16).reshape(ORIENT, COLS),
                power, squares, permuter, where, shell_spread, half_sets[None, :],
                prior_mask.reshape(1, count),
            )
        )
    )

    own_exp, pair = call(
        score_kernel, "scores", [of((ORIENT, count), F32), of((8, 2, count), F32)], 14,
        piece, power, bins_row, mask_row, weighted_near, weighted_far,
        far=(5,), scratch=[near((rest, COLS), BF16), pltpu.SemaphoreType.DMA((PARTS,))],
    )
    packed, evidence = call(
        project_kernel, "project", [of((ROWS, WIDE), jnp.int16), of((1, count), F32)], 20,
        own_exp, pair, exchange(pair, CLS), permuter, half_row, bins_row,
        *centred, far_out=(1,), scratch=[near((1, count), F32), pltpu.SemaphoreType.DMA],
    )
    (second,) = call(
        plane_kernel, "plane", [of((16, WIDE), jnp.int16)], 8,
        exchange(packed.reshape(16, 16, WIDE), PLANE),
    )
    keep, stats = call(
        shell_kernel, "shells", [of((2, COLS), F32), of((16, 8, PART + ORIENT), F32)], 8,
        where, lax.all_gather(second, "zh"), squares, shell_spread,
    )
    (half_maps,) = call(
        finish_kernel, "finish", [of((1, 4, COLS), F32)], 8,
        where, exchange(stats, PLANE), keep, shell_spread,
    )
    return (half_maps, evidence.reshape(count))


def solution(mesh):
    split = Mesh(mesh.devices.reshape(4, 2, 4, 4, 4), AXES)
    placed = (
        P(PTCL, None),
        P(CLS, PTCL, None),
        P(),
        P(PTCL),
        P(PTCL),
        P(PTCL, CLS),
        P(),
    )
    return jax.shard_map(
        on_device,
        mesh=split,
        in_specs=placed,
        out_specs=(P(CLS, PTCL, None), P(PTCL)),
        check_vma=False,
    )
```

```python
import jax
import jax.numpy as jnp
from jax import lax
from jax.experimental import pallas as pl
from jax.experimental.pallas import tpu as pltpu
from jax.sharding import Mesh
from jax.sharding import PartitionSpec as P

PIXC = 1024
COLS = 2 * PIXC
ORIENT = 128
ROWS = 2 * ORIENT
NSHELL = 32
NBIN = 16
AXES = ("zl", "co", "y", "zh", "x")
CLS = ("zl", "co")
PTCL = ("y", "zh", "x")
PLANE = ("y", "x")
SIDE = 128
WIDE = COLS + SIDE
CODE = 32767.0
PARTS = 4
CHUNK = 256
PART = COLS // PARTS
F32 = jnp.float32
BF16 = jnp.bfloat16


def ctf_table():
    bins = jnp.arange(NBIN, dtype=F32)
    defocus = (bins + 1.0) / NBIN
    radius = (jnp.arange(PIXC, dtype=F32) + 0.5) / PIXC
    phase = 0.3 + 2.5 * defocus[:, None] * radius[None, :]
    return jnp.sin(phase) + 0.1 * jnp.cos(phase)


def lookup_small(indices, values):
    count = values.shape[0]
    match = indices[:, None] == jnp.arange(count, dtype=jnp.int32)[None, :]
    return jnp.sum(jnp.where(match, values[None, :], 0.0), axis=1)


def exchange(blocks, axes):
    return lax.all_to_all(blocks, axes, split_axis=0, concat_axis=0, tiled=True)


def from_all(shard, axes, count):
    return exchange(jnp.broadcast_to(shard[None], (count,) + shard.shape), axes)


def row_direction(r):
    j, zh, x, y = r & 1, (r >> 2) & 3, (r >> 4) & 3, r >> 6
    return 4 * (((y & 1) * 4 + zh) * 4 + x) + 2 * (y >> 1) + j


def row_half(r):
    return ((r >> 1) & 1) ^ (r >> 7)


def gathered_orient(r):
    j, zh, x, y = r & 1, (r >> 1) & 3, (r >> 3) & 3, r >> 5
    return ((y * 4 + zh) * 4 + x) * 2 + j


def row_permuter(orient_ids):
    row = lax.broadcasted_iota(jnp.int32, (ROWS, ORIENT), 0)
    wanted = jnp.where(row_direction(row) == orient_ids, 1.0, 0.0).astype(BF16)
    orient = lax.broadcasted_iota(jnp.int32, (ORIENT, ORIENT), 0)
    column = lax.broadcasted_iota(jnp.int32, (ORIENT, ORIENT), 1)
    order = jnp.where(orient == gathered_orient(column), 1.0, 0.0).astype(BF16)
    return contract(wanted, order, ((1,), (0,))).astype(BF16)


def three_parts(table, axis):
    high = table.astype(BF16)
    rest = table - high.astype(F32)
    mid = rest.astype(BF16)
    low = (rest - mid.astype(F32)).astype(BF16)
    return jnp.concatenate([high, mid, low], axis=axis)


def table_parts(table):
    high = lax.reduce_precision(table, 8, 7)
    mid = lax.reduce_precision(table - high, 8, 7)
    low = table - high - mid
    return jnp.concatenate([high, mid, low], axis=0).astype(BF16)


def bin_match(bins, copies):
    row = lax.broadcasted_iota(jnp.int32, (copies * NBIN, bins.shape[1]), 0)
    return jnp.where(row % NBIN == bins, 1.0, 0.0).astype(BF16)


def contract(left, right, dims):
    return lax.dot_general(left, right, (dims, ((), ())), preferred_element_type=F32)


def encode(values):
    size = jnp.abs(values)
    top = jnp.max(size, axis=1, keepdims=True)
    expo = jnp.floor(jnp.log2(jnp.maximum(top, 1e-37))) + 1.0
    root = lax.rsqrt(lax.rsqrt(jnp.maximum(size * jnp.exp2(-expo), 1e-36)))
    code = root * CODE + 0.5
    codes = jnp.where(values < 0.0, -code, code).astype(jnp.int32).astype(jnp.int16)
    return codes, expo


def side_block(sums, expos, unit):
    fixed = jnp.floor(sums * unit + 0.5).astype(jnp.int32)
    high = lax.shift_right_arithmetic(fixed, 16)
    low = (fixed & 65535) - 32768
    shape = (sums.shape[0], SIDE - 2 * NBIN)
    lane = lax.broadcasted_iota(jnp.int32, shape, 1)
    tail = jnp.zeros(shape, F32)
    for part, expo in enumerate(expos):
        tail = jnp.where(lane == part, expo, tail)
    return jnp.concatenate([high, low, tail.astype(jnp.int32)], axis=1).astype(jnp.int16)


def decode_part(ref, count, part):
    cols = slice(part * PART, (part + 1) * PART)
    at = COLS + 2 * NBIN + part
    data = jnp.zeros((ref.shape[1], PART), F32)
    for source in range(count):
        expo = ref[source, :, COLS:].astype(jnp.int32)[:, at - COLS : at - COLS + 1]
        scale = jnp.exp2(expo.astype(F32))
        root = ref[source, :, cols].astype(jnp.int32).astype(F32) * (1.0 / CODE)
        data = data + root * jnp.abs(root) * (root * root) * scale
    return data


def decode_bins(ref, count, unit):
    sums = jnp.zeros((ref.shape[1], NBIN), F32)
    for source in range(count):
        side = ref[source, :, COLS:].astype(jnp.int32)
        fixed = side[:, :NBIN] * 65536 + (side[:, NBIN : 2 * NBIN] + 32768)
        sums = sums + fixed.astype(F32) * (1.0 / unit)
    return sums


def image_kernel(
    x_ref, bins_ref, table_ref, noise_ref, centred_0, centred_1, centred_2, centred_3,
    weighted_near, weighted_far, x_buf, centred_buf, weighted_buf, sems
):
    noise = noise_ref[...]
    steps = PARTS
    step = x_buf.shape[0] // steps
    edge = weighted_near.shape[0] // step

    def read(i):
        rows = pl.ds(i * step, step)
        return pltpu.make_async_copy(x_ref.at[rows], x_buf.at[rows], sems.at[0, i])

    def write(i, k):
        if k < PARTS:
            rows, out = pl.ds(i * step, step), (centred_0, centred_1, centred_2, centred_3)[k]
            buf = centred_buf.at[:, k * PART : (k + 1) * PART]
        else:
            rows, buf, out = pl.ds((i - edge) * step, step), weighted_buf, weighted_far
        return pltpu.make_async_copy(buf.at[rows], out.at[rows], sems.at[k + 1, i])

    def chunk(i, keep):
        rows = pl.ds(pl.multiple_of(i * step, step), step)
        match = bin_match(bins_ref[:, rows], 3)
        contrast = contract(match, table_ref[...], ((0,), (0,)))
        read(i).wait()
        for part in range(2):
            cols = slice(part * PIXC, (part + 1) * PIXC)
            product = x_buf[rows, cols].astype(F32) * contrast
            centred_buf[rows, cols] = product.astype(BF16)
            scaled = (product * noise).astype(BF16)
            if keep:
                weighted_near[rows, cols] = scaled
            else:
                weighted_buf[pl.ds(pl.multiple_of((i - edge) * step, step), step), cols] = scaled
        for k in range(PARTS):
            write(i, k).start()
        if not keep:
            write(i, PARTS).start()

    for i in range(steps):
        read(i).start()
    lax.fori_loop(0, edge, lambda i, c: (chunk(i, True), c)[1], 0)
    lax.fori_loop(edge, steps, lambda i, c: (chunk(i, False), c)[1], 0)
    for i in range(steps):
        for k in range(PARTS):
            write(i, k).wait()
        if i >= edge:
            write(i, PARTS).wait()


def score_kernel(
    panel_ref, power_ref, bins_ref, mask_ref, near_ref, far_ref, exp_ref, pair_ref, far_buf, sems
):
    steps = far_ref.shape[0] // CHUNK

    def read(i):
        rows = pl.ds(i * CHUNK, CHUNK)
        return pltpu.make_async_copy(far_ref.at[rows], far_buf.at[rows], sems.at[i])

    for i in range(steps):
        read(i).start()
    real = panel_ref[:, :PIXC].astype(F32)
    imag = panel_ref[:, PIXC:].astype(F32)
    panel_power = (real * real + imag * imag).astype(BF16)
    norm = three_parts(contract(panel_power, power_ref[...], ((1,), (1,))), 1)

    def chunk(at, weighted):
        rows = pl.ds(at, CHUNK)
        norm_part = contract(norm, bin_match(bins_ref[:, rows], 3), ((1,), (0,)))
        direct = contract(panel_ref[...], weighted, ((1,), (1,)))
        scores = direct - 0.5 * norm_part
        allowed = mask_ref[:, rows] > 0
        masked = jnp.where(allowed, scores, -1e30)
        peak = jnp.max(masked, axis=0, keepdims=True)
        weights = jnp.where(allowed, jnp.exp(masked - peak), 0.0)
        exp_ref[:, rows] = weights
        total = jnp.sum(weights, axis=0, keepdims=True)
        pair = jnp.concatenate([peak, total], axis=0)
        for other in range(8):
            pair_ref[other, :, rows] = pair

    def near_chunk(i, carry):
        start = pl.multiple_of(i * CHUNK, CHUNK)
        chunk(start, near_ref[pl.ds(start, CHUNK), :])
        return carry

    def far_chunk(i, carry):
        read(i).wait()
        start = pl.multiple_of(i * CHUNK, CHUNK)
        chunk(pl.multiple_of(start + near_ref.shape[0], CHUNK), far_buf[pl.ds(start, CHUNK), :])
        return carry

    lax.fori_loop(0, near_ref.shape[0] // CHUNK, near_chunk, 0)
    lax.fori_loop(0, steps, far_chunk, 0)


def project_kernel(
    exp_ref, own_ref, both_ref, orient_ref, half_ref, bins_ref, *rest_refs
):
    packed_ref, evidence_ref, evidence_buf, sem = rest_refs[PARTS:]
    spans = [slice(part * PART, (part + 1) * PART) for part in range(PARTS)]
    own_peak = own_ref[0, 0:1, :]
    peaks = both_ref[:, 0, :]
    peak = jnp.max(peaks, axis=0, keepdims=True)
    total = jnp.sum(both_ref[:, 1, :] * jnp.exp(peaks - peak), axis=0, keepdims=True)
    evidence_buf[...] = peak + jnp.log(total)
    evidence = pltpu.make_async_copy(evidence_buf, evidence_ref, sem)
    evidence.start()
    posterior = (exp_ref[...] * (jnp.exp(own_peak - peak) / total)).astype(BF16)
    by_direction = contract(row_permuter(orient_ref[...]), posterior, ((1,), (0,)))
    row = lax.broadcasted_iota(jnp.int32, (ROWS, 1), 0)
    kept = row_half(row) == half_ref[...]
    post = jnp.where(kept, by_direction, 0.0).astype(BF16)
    sums = contract(post, bin_match(bins_ref[...], 1), ((1,), (1,)))
    expos = []
    for part, cols in enumerate(spans):
        codes, expo = encode(contract(post, rest_refs[part][...], ((1,), (0,))))
        expos.append(expo)
        packed_ref[:, cols] = codes
    packed_ref[:, COLS:] = side_block(sums, expos, 2.0**20)
    evidence.wait()


def plane_kernel(came_ref, packed_ref):
    expos = []
    for part in range(PARTS):
        codes, expo = encode(decode_part(came_ref, 16, part))
        expos.append(expo)
        packed_ref[:, part * PART : (part + 1) * PART] = codes
    packed_ref[:, COLS:] = side_block(decode_bins(came_ref, 16, 2.0**20), expos, 2.0**16)


def shell_kernel(where_ref, came_ref, squares_ref, shells_ref, keep_ref, stats_ref):
    upper = where_ref[0:1, 0:1]
    zh = where_ref[1:2, 0:1]
    data = jnp.concatenate([decode_part(came_ref, 4, part) for part in range(PARTS)], axis=1)
    sums = decode_bins(came_ref, 4, 2.0**16)
    cross = jnp.zeros((1, COLS), F32)
    first = jnp.zeros((1, COLS), F32)
    second = jnp.zeros((1, COLS), F32)
    own_data = jnp.zeros((4, COLS), F32)
    own_sums = jnp.zeros((4, NBIN), F32)
    for z in range(4):
        rows = data[4 * z : 4 * z + 4]
        own_data = jnp.where(zh == z, rows, own_data)
        own_sums = jnp.where(zh == z, sums[4 * z : 4 * z + 4], own_sums)
        cross = cross + jnp.sum(rows[:2] * rows[2:], axis=0, keepdims=True)
        first = first + jnp.sum(rows[:2] * rows[:2], axis=0, keepdims=True)
        second = second + jnp.sum(rows[2:] * rows[2:], axis=0, keepdims=True)
    power0 = jnp.where(upper == 0, first, second)
    power1 = jnp.where(upper == 0, second, first)
    three = jnp.concatenate([cross, power0, power1, jnp.zeros((5, COLS), F32)], axis=0)
    folded = three[:, :PIXC] + three[:, PIXC:]
    by_shell = contract(three_parts(folded, 0), shells_ref[...], ((1,), (1,)))
    by_shell = by_shell[0:8] + by_shell[8:16] + by_shell[16:24]
    squares = squares_ref[...]
    weight = contract(
        three_parts(own_sums, 1), jnp.concatenate([squares] * 3, axis=0), ((1,), (0,))
    )
    whole = own_data / (jnp.concatenate([weight, weight], axis=1) + 1.0)
    keep_ref[...] = whole[:2]
    for other in range(16):
        stats_ref[other, :, PART:] = by_shell
    for part in range(PARTS):
        piece = whole[2:, part * PART : (part + 1) * PART]
        for other in range(16):
            stats_ref[other, 2 * part : 2 * part + 2, :PART] = piece


def finish_kernel(where_ref, came_ref, keep_ref, spread_ref, out_ref):
    totals = came_ref[0, :, PART:]
    for source in range(1, 16):
        totals = totals + came_ref[source, :, PART:]
    fsc = totals[0:1] / jnp.sqrt(totals[1:2] * totals[2:3] + 1e-06)
    half = jnp.broadcast_to((1.0 + fsc) / 2.0, (8, ORIENT))
    factor = contract(three_parts(half, 0), spread_ref[...], ((1,), (0,)))
    factor = factor[0:1] + factor[8:9] + factor[16:17]
    low = where_ref[0:1, 0:1] == 0
    source = where_ref[2:3, 0:1]
    partner = jnp.zeros((8, PART), F32)
    for other in range(16):
        partner = jnp.where(source == other, came_ref[other, :, :PART], partner)
    for part in range(PARTS):
        cols = slice(part * PART, (part + 1) * PART)
        start = (part * PART) % PIXC
        scale = factor[:, start : start + PART]
        keep = keep_ref[:, cols] * scale
        got = partner[2 * part : 2 * part + 2] * scale
        out_ref[0, 0:2, cols] = jnp.where(low, keep, got)
        out_ref[0, 2:4, cols] = jnp.where(low, got, keep)


def call(kernel, name, out_shape, mega, *args, scalars=0, far=(), far_out=(), scratch=()):
    def space(i, hbm):
        if i < 0:
            return pl.BlockSpec(memory_space=pltpu.MemorySpace.SMEM)
        return pl.BlockSpec(
            memory_space=pltpu.MemorySpace.HBM if i in hbm else pltpu.MemorySpace.VMEM
        )

    args = [
        pltpu.with_memory_space_constraint(arg, pltpu.MemorySpace.HBM) if i in far else arg
        for i, arg in enumerate(args)
    ]
    return pl.pallas_call(
        kernel,
        in_specs=[space(i if i >= scalars else -1, far) for i in range(len(args))],
        out_specs=[space(i, far_out) for i in range(len(out_shape))],
        out_shape=out_shape,
        scratch_shapes=scratch,
        compiler_params=pltpu.CompilerParams(vmem_limit_bytes=mega * 1024 * 1024),
        name=name,
    )(*args)


def on_device(particles, panels, sigma2, defocus_bins, half_sets, prior_mask, orient_ids):
    count = particles.shape[0]
    of = jax.ShapeDtypeStruct

    by_zh, sigma2 = lax.optimization_barrier((lax.all_gather(panels[0], "zh"), sigma2))
    shells = jnp.arange(PIXC, dtype=jnp.int32) * NSHELL // PIXC
    inverse_noise = lookup_small(shells, 1.0 / sigma2)
    table = ctf_table()
    power = (table * table * inverse_noise[None, :]).astype(BF16)
    squares = (table * table).astype(BF16)
    lanes = jnp.arange(ORIENT, dtype=jnp.int32)
    shell_spread = (lanes[:, None] == shells[None, :]).astype(BF16)
    y, zh, x = lax.axis_index("y"), lax.axis_index("zh"), lax.axis_index("x")
    places = jnp.stack([y // 2, zh, (y ^ 2) * 4 + x]).astype(jnp.int32)
    where = jnp.broadcast_to(jnp.pad(places, (0, 5))[:, None], (8, ORIENT))

    near, far = pltpu.MemorySpace.VMEM, pltpu.MemorySpace.HBM
    first, rest = 2 * CHUNK, count - 2 * CHUNK
    bins_row = defocus_bins[None, :]
    *centred, weighted_near, weighted_far = call(
        image_kernel, "images",
        [
            *[far((count, PART), BF16)] * PARTS,
            near((first, COLS), BF16), far((rest, COLS), BF16),
        ],
        24, particles, bins_row, table_parts(table), inverse_noise[None, :],
        far=(0,), far_out=(0, 1, 2, 3, 5),
        scratch=[
            near((count, COLS), BF16), near((count, COLS), BF16), near((rest, COLS), BF16),
            pltpu.SemaphoreType.DMA((PARTS + 2, PARTS)),
        ],
    )
    piece, power, squares, where, shell_spread, half_row, mask_row = (
        lax.optimization_barrier(
            (
                from_all(by_zh.reshape(8, COLS), PLANE, 16).reshape(ORIENT, COLS),
                power, squares, where, shell_spread, half_sets[None, :],
                prior_mask.reshape(1, count),
            )
        )
    )

    own_exp, pair = call(
        score_kernel, "scores", [of((ORIENT, count), F32), of((8, 2, count), F32)], 14,
        piece, power, bins_row, mask_row, weighted_near, weighted_far,
        far=(5,), scratch=[near((rest, COLS), BF16), pltpu.SemaphoreType.DMA((PARTS,))],
    )
    packed, evidence = call(
        project_kernel, "project", [of((ROWS, WIDE), jnp.int16), of((1, count), F32)], 20,
        own_exp, pair, exchange(pair, CLS), orient_ids[None, :], half_row, bins_row,
        *centred, far_out=(1,), scratch=[near((1, count), F32), pltpu.SemaphoreType.DMA],
    )
    (second,) = call(
        plane_kernel, "plane", [of((16, WIDE), jnp.int16)], 8,
        exchange(packed.reshape(16, 16, WIDE), PLANE),
    )
    keep, stats = call(
        shell_kernel, "shells", [of((2, COLS), F32), of((16, 8, PART + ORIENT), F32)], 8,
        where, lax.all_gather(second, "zh"), squares, shell_spread,
    )
    (half_maps,) = call(
        finish_kernel, "finish", [of((1, 4, COLS), F32)], 8,
        where, exchange(stats, PLANE), keep, shell_spread,
    )
    return (half_maps, evidence.reshape(count))


def solution(mesh):
    split = Mesh(mesh.devices.reshape(4, 2, 4, 4, 4), AXES)
    placed = (
        P(PTCL, None),
        P(CLS, PTCL, None),
        P(),
        P(PTCL),
        P(PTCL),
        P(PTCL, CLS),
        P(),
    )
    return jax.shard_map(
        on_device,
        mesh=split,
        in_specs=placed,
        out_specs=(P(CLS, PTCL, None), P(PTCL)),
        check_vma=False,
    )
```

```python
import jax
import jax.numpy as jnp
from jax import lax
from jax.experimental import pallas as pl
from jax.experimental.pallas import tpu as pltpu
from jax.sharding import Mesh
from jax.sharding import PartitionSpec as P

PIXC = 1024
COLS = 2 * PIXC
ORIENT = 128
ROWS = 2 * ORIENT
NSHELL = 32
NBIN = 16
AXES = ("zl", "co", "y", "zh", "x")
CLS = ("zl", "co")
PTCL = ("y", "zh", "x")
PLANE = ("y", "x")
SIDE = 128
WIDE = COLS + SIDE
CODE = 32767.0
PARTS = 4
CHUNK = 256
PART = COLS // PARTS
F32 = jnp.float32
BF16 = jnp.bfloat16


def ctf_table():
    bins = jnp.arange(NBIN, dtype=F32)
    defocus = (bins + 1.0) / NBIN
    radius = (jnp.arange(PIXC, dtype=F32) + 0.5) / PIXC
    phase = 0.3 + 2.5 * defocus[:, None] * radius[None, :]
    return jnp.sin(phase) + 0.1 * jnp.cos(phase)


def lookup_small(indices, values):
    count = values.shape[0]
    match = indices[:, None] == jnp.arange(count, dtype=jnp.int32)[None, :]
    return jnp.sum(jnp.where(match, values[None, :], 0.0), axis=1)


def exchange(blocks, axes):
    return lax.all_to_all(blocks, axes, split_axis=0, concat_axis=0, tiled=True)


def from_all(shard, axes, count):
    return exchange(jnp.broadcast_to(shard[None], (count,) + shard.shape), axes)


def row_direction(r):
    j, zh, x, y = r & 1, (r >> 2) & 3, (r >> 4) & 3, r >> 6
    return 4 * (((y & 1) * 4 + zh) * 4 + x) + 2 * (y >> 1) + j


def row_half(r):
    return ((r >> 1) & 1) ^ (r >> 7)


def gathered_orient(r):
    j, zh, x, y = r & 1, (r >> 1) & 3, (r >> 3) & 3, r >> 5
    return ((y * 4 + zh) * 4 + x) * 2 + j


def row_permuter(orient_ids):
    row = lax.broadcasted_iota(jnp.int32, (ROWS, ORIENT), 0)
    wanted = jnp.where(row_direction(row) == orient_ids, 1.0, 0.0).astype(BF16)
    orient = lax.broadcasted_iota(jnp.int32, (ORIENT, ORIENT), 0)
    column = lax.broadcasted_iota(jnp.int32, (ORIENT, ORIENT), 1)
    order = jnp.where(orient == gathered_orient(column), 1.0, 0.0).astype(BF16)
    return contract(wanted, order, ((1,), (0,))).astype(BF16)


def three_parts(table, axis):
    high = table.astype(BF16)
    rest = table - high.astype(F32)
    mid = rest.astype(BF16)
    low = (rest - mid.astype(F32)).astype(BF16)
    return jnp.concatenate([high, mid, low], axis=axis)


def table_parts(table):
    high = lax.reduce_precision(table, 8, 7)
    mid = lax.reduce_precision(table - high, 8, 7)
    low = table - high - mid
    return jnp.concatenate([high, mid, low], axis=0).astype(BF16)


def bin_match(bins, copies):
    row = lax.broadcasted_iota(jnp.int32, (copies * NBIN, bins.shape[1]), 0)
    return jnp.where(row % NBIN == bins, 1.0, 0.0).astype(BF16)


def contract(left, right, dims):
    return lax.dot_general(left, right, (dims, ((), ())), preferred_element_type=F32)


def encode(values):
    size = jnp.abs(values)
    top = jnp.max(size, axis=1, keepdims=True)
    expo = jnp.floor(jnp.log2(jnp.maximum(top, 1e-37))) + 1.0
    root = lax.rsqrt(lax.rsqrt(jnp.maximum(size * jnp.exp2(-expo), 1e-36)))
    code = root * CODE + 0.5
    codes = jnp.where(values < 0.0, -code, code).astype(jnp.int32).astype(jnp.int16)
    return codes, expo


def side_block(sums, expos, unit):
    fixed = jnp.floor(sums * unit + 0.5).astype(jnp.int32)
    high = lax.shift_right_arithmetic(fixed, 16)
    low = (fixed & 65535) - 32768
    shape = (sums.shape[0], SIDE - 2 * NBIN)
    lane = lax.broadcasted_iota(jnp.int32, shape, 1)
    tail = jnp.zeros(shape, F32)
    for part, expo in enumerate(expos):
        tail = jnp.where(lane == part, expo, tail)
    return jnp.concatenate([high, low, tail.astype(jnp.int32)], axis=1).astype(jnp.int16)


def decode_part(ref, count, part):
    cols = slice(part * PART, (part + 1) * PART)
    at = COLS + 2 * NBIN + part
    data = jnp.zeros((ref.shape[1], PART), F32)
    for source in range(count):
        expo = ref[source, :, COLS:].astype(jnp.int32)[:, at - COLS : at - COLS + 1]
        scale = jnp.exp2(expo.astype(F32))
        root = ref[source, :, cols].astype(jnp.int32).astype(F32) * (1.0 / CODE)
        data = data + root * jnp.abs(root) * (root * root) * scale
    return data


def decode_bins(ref, count, unit):
    sums = jnp.zeros((ref.shape[1], NBIN), F32)
    for source in range(count):
        side = ref[source, :, COLS:].astype(jnp.int32)
        fixed = side[:, :NBIN] * 65536 + (side[:, NBIN : 2 * NBIN] + 32768)
        sums = sums + fixed.astype(F32) * (1.0 / unit)
    return sums


def image_kernel(
    x_ref, bins_ref, table_ref, noise_ref, centred_0, centred_1, centred_2, centred_3,
    weighted_near, weighted_far, x_buf, centred_buf, weighted_buf, sems
):
    noise = noise_ref[...]
    steps = PARTS
    step = x_buf.shape[0] // steps
    edge = weighted_near.shape[0] // step

    def read(i):
        rows = pl.ds(i * step, step)
        return pltpu.make_async_copy(x_ref.at[rows], x_buf.at[rows], sems.at[0, i])

    def write(i, k):
        if k < PARTS:
            rows, out = pl.ds(i * step, step), (centred_0, centred_1, centred_2, centred_3)[k]
            buf = centred_buf.at[:, k * PART : (k + 1) * PART]
        else:
            rows, buf, out = pl.ds((i - edge) * step, step), weighted_buf, weighted_far
        return pltpu.make_async_copy(buf.at[rows], out.at[rows], sems.at[k + 1, i])

    def chunk(i, keep):
        rows = pl.ds(pl.multiple_of(i * step, step), step)
        match = bin_match(bins_ref[:, rows], 3)
        contrast = contract(match, table_ref[...], ((0,), (0,)))
        read(i).wait()
        for part in range(2):
            cols = slice(part * PIXC, (part + 1) * PIXC)
            product = x_buf[rows, cols].astype(F32) * contrast
            centred_buf[rows, cols] = product.astype(BF16)
            scaled = (product * noise).astype(BF16)
            if keep:
                weighted_near[rows, cols] = scaled
            else:
                weighted_buf[pl.ds(pl.multiple_of((i - edge) * step, step), step), cols] = scaled
        for k in range(PARTS):
            write(i, k).start()
        if not keep:
            write(i, PARTS).start()

    for i in range(steps):
        read(i).start()
    lax.fori_loop(0, edge, lambda i, c: (chunk(i, True), c)[1], 0)
    lax.fori_loop(edge, steps, lambda i, c: (chunk(i, False), c)[1], 0)
    for i in range(steps):
        for k in range(PARTS):
            write(i, k).wait()
        if i >= edge:
            write(i, PARTS).wait()


def score_kernel(
    panel_ref, power_ref, bins_ref, mask_ref, near_ref, far_ref, exp_ref, pair_ref, far_buf, sems
):
    steps = far_ref.shape[0] // CHUNK

    def read(i):
        rows = pl.ds(i * CHUNK, CHUNK)
        return pltpu.make_async_copy(far_ref.at[rows], far_buf.at[rows], sems.at[i])

    for i in range(steps):
        read(i).start()
    real = panel_ref[:, :PIXC].astype(F32)
    imag = panel_ref[:, PIXC:].astype(F32)
    panel_power = (real * real + imag * imag).astype(BF16)
    norm = three_parts(contract(panel_power, power_ref[...], ((1,), (1,))), 1)

    def chunk(at, weighted):
        rows = pl.ds(at, CHUNK)
        norm_part = contract(norm, bin_match(bins_ref[:, rows], 3), ((1,), (0,)))
        direct = contract(panel_ref[...], weighted, ((1,), (1,)))
        scores = direct - 0.5 * norm_part
        allowed = mask_ref[:, rows] > 0
        masked = jnp.where(allowed, scores, -1e30)
        peak = jnp.max(masked, axis=0, keepdims=True)
        weights = jnp.where(allowed, jnp.exp(masked - peak), 0.0)
        exp_ref[:, rows] = weights
        total = jnp.sum(weights, axis=0, keepdims=True)
        pair = jnp.concatenate([peak, total], axis=0)
        for other in range(8):
            pair_ref[other, :, rows] = pair

    def near_chunk(i, carry):
        start = pl.multiple_of(i * CHUNK, CHUNK)
        chunk(start, near_ref[pl.ds(start, CHUNK), :])
        return carry

    def far_chunk(i, carry):
        read(i).wait()
        start = pl.multiple_of(i * CHUNK, CHUNK)
        chunk(pl.multiple_of(start + near_ref.shape[0], CHUNK), far_buf[pl.ds(start, CHUNK), :])
        return carry

    lax.fori_loop(0, near_ref.shape[0] // CHUNK, near_chunk, 0)
    lax.fori_loop(0, steps, far_chunk, 0)


def project_kernel(
    exp_ref, own_ref, both_ref, orient_ref, half_ref, bins_ref, *rest_refs
):
    packed_ref, evidence_ref, evidence_buf, sem = rest_refs[PARTS:]
    spans = [slice(part * PART, (part + 1) * PART) for part in range(PARTS)]
    own_peak = own_ref[0, 0:1, :]
    peaks = both_ref[:, 0, :]
    peak = jnp.max(peaks, axis=0, keepdims=True)
    total = jnp.sum(both_ref[:, 1, :] * jnp.exp(peaks - peak), axis=0, keepdims=True)
    evidence_buf[...] = peak + jnp.log(total)
    evidence = pltpu.make_async_copy(evidence_buf, evidence_ref, sem)
    evidence.start()
    posterior = (exp_ref[...] * (jnp.exp(own_peak - peak) / total)).astype(BF16)
    by_direction = contract(row_permuter(orient_ref[...]), posterior, ((1,), (0,)))
    row = lax.broadcasted_iota(jnp.int32, (ROWS, 1), 0)
    kept = row_half(row) == half_ref[...]
    post = jnp.where(kept, by_direction, 0.0).astype(BF16)
    sums = contract(post, bin_match(bins_ref[...], 1), ((1,), (1,)))
    expos = []
    for part, cols in enumerate(spans):
        codes, expo = encode(contract(post, rest_refs[part][...], ((1,), (0,))))
        expos.append(expo)
        packed_ref[:, cols] = codes
    packed_ref[:, COLS:] = side_block(sums, expos, 2.0**20)
    evidence.wait()


def plane_kernel(came_ref, packed_ref):
    expos = []
    for part in range(PARTS):
        codes, expo = encode(decode_part(came_ref, 16, part))
        expos.append(expo)
        packed_ref[:, part * PART : (part + 1) * PART] = codes
    packed_ref[:, COLS:] = side_block(decode_bins(came_ref, 16, 2.0**20), expos, 2.0**16)


def shell_kernel(where_ref, came_ref, squares_ref, shells_ref, keep_ref, stats_ref):
    upper = where_ref[0:1, 0:1]
    zh = where_ref[1:2, 0:1]
    data = jnp.concatenate([decode_part(came_ref, 4, part) for part in range(PARTS)], axis=1)
    sums = decode_bins(came_ref, 4, 2.0**16)
    cross = jnp.zeros((1, COLS), F32)
    first = jnp.zeros((1, COLS), F32)
    second = jnp.zeros((1, COLS), F32)
    own_data = jnp.zeros((4, COLS), F32)
    own_sums = jnp.zeros((4, NBIN), F32)
    for z in range(4):
        rows = data[4 * z : 4 * z + 4]
        own_data = jnp.where(zh == z, rows, own_data)
        own_sums = jnp.where(zh == z, sums[4 * z : 4 * z + 4], own_sums)
        cross = cross + jnp.sum(rows[:2] * rows[2:], axis=0, keepdims=True)
        first = first + jnp.sum(rows[:2] * rows[:2], axis=0, keepdims=True)
        second = second + jnp.sum(rows[2:] * rows[2:], axis=0, keepdims=True)
    power0 = jnp.where(upper == 0, first, second)
    power1 = jnp.where(upper == 0, second, first)
    three = jnp.concatenate([cross, power0, power1, jnp.zeros((5, COLS), F32)], axis=0)
    folded = three[:, :PIXC] + three[:, PIXC:]
    by_shell = contract(three_parts(folded, 0), shells_ref[...], ((1,), (1,)))
    by_shell = by_shell[0:8] + by_shell[8:16] + by_shell[16:24]
    squares = squares_ref[...]
    weight = contract(
        three_parts(own_sums, 1), jnp.concatenate([squares] * 3, axis=0), ((1,), (0,))
    )
    whole = own_data / (jnp.concatenate([weight, weight], axis=1) + 1.0)
    keep_ref[...] = whole[:2]
    for other in range(16):
        stats_ref[other, :, PART:] = by_shell
    for part in range(PARTS):
        piece = whole[2:, part * PART : (part + 1) * PART]
        for other in range(16):
            stats_ref[other, 2 * part : 2 * part + 2, :PART] = piece


def finish_kernel(where_ref, came_ref, keep_ref, spread_ref, out_ref):
    totals = came_ref[0, :, PART:]
    for source in range(1, 16):
        totals = totals + came_ref[source, :, PART:]
    fsc = totals[0:1] / jnp.sqrt(totals[1:2] * totals[2:3] + 1e-06)
    half = jnp.broadcast_to((1.0 + fsc) / 2.0, (8, ORIENT))
    factor = contract(three_parts(half, 0), spread_ref[...], ((1,), (0,)))
    factor = factor[0:1] + factor[8:9] + factor[16:17]
    low = where_ref[0:1, 0:1] == 0
    source = where_ref[2:3, 0:1]
    partner = jnp.zeros((8, PART), F32)
    for other in range(16):
        partner = jnp.where(source == other, came_ref[other, :, :PART], partner)
    for part in range(PARTS):
        cols = slice(part * PART, (part + 1) * PART)
        start = (part * PART) % PIXC
        scale = factor[:, start : start + PART]
        keep = keep_ref[:, cols] * scale
        got = partner[2 * part : 2 * part + 2] * scale
        out_ref[0, 0:2, cols] = jnp.where(low, keep, got)
        out_ref[0, 2:4, cols] = jnp.where(low, got, keep)


def call(kernel, name, out_shape, mega, *args, scalars=0, far=(), far_out=(), scratch=()):
    def space(i, hbm):
        if i < 0:
            return pl.BlockSpec(memory_space=pltpu.MemorySpace.SMEM)
        return pl.BlockSpec(
            memory_space=pltpu.MemorySpace.HBM if i in hbm else pltpu.MemorySpace.VMEM
        )

    args = [
        pltpu.with_memory_space_constraint(arg, pltpu.MemorySpace.HBM) if i in far else arg
        for i, arg in enumerate(args)
    ]
    return pl.pallas_call(
        kernel,
        in_specs=[space(i if i >= scalars else -1, far) for i in range(len(args))],
        out_specs=[space(i, far_out) for i in range(len(out_shape))],
        out_shape=out_shape,
        scratch_shapes=scratch,
        compiler_params=pltpu.CompilerParams(vmem_limit_bytes=mega * 1024 * 1024),
        name=name,
    )(*args)


def on_device(particles, panels, sigma2, defocus_bins, half_sets, prior_mask, orient_ids):
    count = particles.shape[0]
    of = jax.ShapeDtypeStruct

    by_zh, sigma2 = lax.optimization_barrier((lax.all_gather(panels[0], "zh"), sigma2))
    shells = jnp.arange(PIXC, dtype=jnp.int32) * NSHELL // PIXC
    inverse_noise = 1.0 / lookup_small(shells, sigma2)
    table = ctf_table()
    power = (table * table * inverse_noise[None, :]).astype(BF16)
    squares = (table * table).astype(BF16)
    lanes = jnp.arange(ORIENT, dtype=jnp.int32)
    shell_spread = (lanes[:, None] == shells[None, :]).astype(BF16)
    y, zh, x = lax.axis_index("y"), lax.axis_index("zh"), lax.axis_index("x")
    places = jnp.stack([y // 2, zh, (y ^ 2) * 4 + x]).astype(jnp.int32)
    where = jnp.broadcast_to(jnp.pad(places, (0, 5))[:, None], (8, ORIENT))

    near, far = pltpu.MemorySpace.VMEM, pltpu.MemorySpace.HBM
    first, rest = 2 * CHUNK, count - 2 * CHUNK
    bins_row = defocus_bins[None, :]
    *centred, weighted_near, weighted_far = call(
        image_kernel, "images",
        [
            *[far((count, PART), BF16)] * PARTS,
            near((first, COLS), BF16), far((rest, COLS), BF16),
        ],
        24, particles, bins_row, table_parts(table), inverse_noise[None, :],
        far=(0,), far_out=(0, 1, 2, 3, 5),
        scratch=[
            near((count, COLS), BF16), near((count, COLS), BF16), near((rest, COLS), BF16),
            pltpu.SemaphoreType.DMA((PARTS + 2, PARTS)),
        ],
    )
    piece, power, squares, where, shell_spread, half_row, mask_row = (
        lax.optimization_barrier(
            (
                from_all(by_zh.reshape(8, COLS), PLANE, 16).reshape(ORIENT, COLS),
                power, squares, where, shell_spread, half_sets[None, :],
                prior_mask.reshape(1, count),
            )
        )
    )

    own_exp, pair = call(
        score_kernel, "scores", [of((ORIENT, count), F32), of((8, 2, count), F32)], 14,
        piece, power, bins_row, mask_row, weighted_near, weighted_far,
        far=(5,), scratch=[near((rest, COLS), BF16), pltpu.SemaphoreType.DMA((PARTS,))],
    )
    packed, evidence = call(
        project_kernel, "project", [of((ROWS, WIDE), jnp.int16), of((1, count), F32)], 20,
        own_exp, pair, exchange(pair, CLS), orient_ids[None, :], half_row, bins_row,
        *centred, far_out=(1,), scratch=[near((1, count), F32), pltpu.SemaphoreType.DMA],
    )
    (second,) = call(
        plane_kernel, "plane", [of((16, WIDE), jnp.int16)], 8,
        exchange(packed.reshape(16, 16, WIDE), PLANE),
    )
    keep, stats = call(
        shell_kernel, "shells", [of((2, COLS), F32), of((16, 8, PART + ORIENT), F32)], 8,
        where, lax.all_gather(second, "zh"), squares, shell_spread,
    )
    (half_maps,) = call(
        finish_kernel, "finish", [of((1, 4, COLS), F32)], 8,
        where, exchange(stats, PLANE), keep, shell_spread,
    )
    return (half_maps, evidence.reshape(count))


def solution(mesh):
    split = Mesh(mesh.devices.reshape(4, 2, 4, 4, 4), AXES)
    placed = (
        P(PTCL, None),
        P(CLS, PTCL, None),
        P(),
        P(PTCL),
        P(PTCL),
        P(PTCL, CLS),
        P(),
    )
    return jax.shard_map(
        on_device,
        mesh=split,
        in_specs=placed,
        out_specs=(P(CLS, PTCL, None), P(PTCL)),
        check_vma=False,
    )
```
